512 devices in a mesh: req: 128 (over z, y, core), tp: 4 (over x).
Axes of the slice: x: 4, y: 4, z: 16, core: 2. Of those that a mesh axis runs over, the one named last changes fastest.
Arguments:
- queries: bfloat16 [512, 2048], P('req', 'tp'), may hold values from -8 to 8
- fresh_key_value: bfloat16 [512, 512], P('req', 'tp'), may hold values from -6 to 6
- key_value_page_pool: bfloat16 [8192, 128, 512], P('req', None, 'tp'), may hold values from -6 to 6
- block_owner: int32 [65536, 1], P('req'), may hold values from 0 to 127; in each aligned block of 512 rows (0 to 511, 512 to 1023, ...) at most 8 rows name the same one
- block_page: int32 [65536], P('req'), may hold values from 0 to 63
- lengths: int32 [512], P('req'), may hold values from 1 to 16384, 4194304 in all
- o_weight: bfloat16 [2048, 2048], P('tp'), may hold values from -0.125 to 0.125
- resid_in: bfloat16 [512, 2048], P('req'), may hold values from -0.59765625 to 0.59765625
- norm_gain: bfloat16 [2048], replicated, may hold values from 0.25 to 1.75
Outputs:
- resid_out: bfloat16 [512, 2048], P('req')
- normed: bfloat16 [512, 2048], P('req')
The draws below stay inside these ranges and needn't reach their ends.
Inputs may be any that keep to these rules, and one draw needn't show every extreme that they name: `block_owner`: among the 512 block entries of the slots of one index of req, no owner is named more than 8 times.
All inputs are finite; a program needn't handle non-finite values. No bound on the sum of `lengths` on one device may be relied on, other than what follows from the above.
Results may differ from the reference program's by a relative error of at most 0.0047.
Values may be sent and summed in bfloat16 or wider, within the bound.
A program may use at most 64 MiB of HBM per device.

```python
import math
import jax
import jax.numpy as jnp
import numpy as np
from jax import lax

D = 2048
QUERY_HEADS = 32
KEY_VALUE_HEADS = 4
HEAD_WIDTH = 64
PAGE_TOKENS = 128
BLOCK_LIST_SIZE = 128
SLOT_DEV = 4
P_DEV = 64
SLOT_TOTAL = 512
CAP = 8
N_REQ = 128


def aligned_signs(key):
    coin_flags = jax.random.bernoulli(jax.random.fold_in(key, 7301), 0.5, (KEY_VALUE_HEADS, HEAD_WIDTH))
    return jnp.where(coin_flags, 1.0, -1.0).astype(jnp.float32)


def high_level():
    return min(6.0, 30.0 / math.sqrt(HEAD_WIDTH))


def draw_queries(key, part):
    query_group_width = QUERY_HEADS // KEY_VALUE_HEADS
    complete_shape = (SLOT_TOTAL, QUERY_HEADS, HEAD_WIDTH)
    base = jnp.clip(jax.random.normal(jax.random.fold_in(key, 7401), complete_shape, jnp.float32) * 2.0, -8.0, 8.0)
    signs = jnp.repeat(aligned_signs(key), query_group_width, axis=0)
    selected_pages = jax.random.bernoulli(jax.random.fold_in(key, 7403), 0.25, (SLOT_TOTAL, KEY_VALUE_HEADS))
    selected_pages = jnp.repeat(selected_pages, query_group_width, axis=1)[:, :, None]
    target = jax.random.uniform(jax.random.fold_in(key, 7404), (SLOT_TOTAL, QUERY_HEADS, 1), jnp.float32, 165.0, 232.0)
    strength = jnp.minimum(target / (high_level() * math.sqrt(HEAD_WIDTH)), 7.8)
    aligned = strength * signs[None, :, :]
    return jnp.where(selected_pages, aligned, base).reshape(SLOT_TOTAL, QUERY_HEADS * HEAD_WIDTH).astype(jnp.bfloat16)


def draw_key_value_page_pool(key, part):
    cache_page_list = N_REQ * P_DEV
    complete_shape = (cache_page_list, PAGE_TOKENS, KEY_VALUE_HEADS, 2, HEAD_WIDTH)
    base = jnp.clip(jax.random.normal(jax.random.fold_in(key, 7501), complete_shape, jnp.float32), -6.0, 6.0)
    signs = aligned_signs(key)
    half_page = max(PAGE_TOKENS // 2, 2)
    first_spot = jax.random.randint(jax.random.fold_in(key, 7503), (cache_page_list,), 0, half_page)
    second_spot = (first_spot + 1 + jax.random.randint(jax.random.fold_in(key, 7504), (cache_page_list,), 0, half_page - 1)) % half_page
    spots = jnp.arange(PAGE_TOKENS, dtype=jnp.int32)
    at_first = (spots[None, :] == first_spot[:, None])[:, :, None, None]
    at_second = (spots[None, :] == second_spot[:, None])[:, :, None, None]
    level = high_level()
    lower = level - 0.25 / math.sqrt(HEAD_WIDTH)
    keys = base[:, :, :, 0, :]
    keys = jnp.where(at_first, level * signs[None, None, :, :], jnp.where(at_second, lower * signs[None, None, :, :], keys))
    concatenated = jnp.stack([keys, base[:, :, :, 1, :]], axis=3)
    return concatenated.reshape(cache_page_list, PAGE_TOKENS, KEY_VALUE_HEADS * 2 * HEAD_WIDTH).astype(jnp.bfloat16)


def plant(result, rng, smallest, high):
    longest = result.shape.index(max(result.shape))
    spots = []
    for shift in (0, 1):
        where = [jax.random.randint(jax.random.fold_in(rng, axis), (), 0, length) for axis, length in enumerate(result.shape)]
        where[longest] = (where[longest] + shift) % result.shape[longest]
        spots.append(tuple(where))
    return result.at[spots[0]].set(smallest).at[spots[1]].set(high)


def levels(own_key, shape, shards, least, largest):
    loudness = 1.0
    for dim, parts in shards:
        heights = jax.random.uniform(jax.random.fold_in(jax.random.fold_in(own_key, 6), dim), (parts,), jnp.float32, least / len(shards), largest / len(shards))
        loudness = loudness * jnp.repeat(jnp.exp(heights), shape[dim] // parts).reshape((-1,) + (1,) * (len(shape) - 1 - dim))
    return loudness


def length_profile(amount, total, most, slope):
    portions = [(1 << 20) // math.isqrt(standing ** slope) + 1 for standing in range(2, amount + 1)]
    spare, given = total - most - (amount - 1), [1] * (amount - 1)
    while spare > 0:
        movable = [i for i in range(amount - 1) if given[i] < most]
        whole, budget = sum([portions[i] for i in movable]), spare
        for i in movable:
            extra = min(most - given[i], max(1, budget * portions[i] // whole), spare)
            given[i] = given[i] + extra
            spare = spare - extra
    return np.array([most] + given)


def ragged(rng, count, total, limit, skew):
    if count == 2:
        one = jax.random.randint(rng, (), max(1, total - limit), min(limit, total - 1) + 1)
        return jnp.stack([one, total - one])
    sizes = jnp.asarray(length_profile(count, total, limit, skew), jnp.int32)
    couples = (count - 1) // 2
    source_of, taker = sizes[1:1 + 2 * couples:2], sizes[2:2 + 2 * couples:2]
    room = jnp.minimum(source_of - 1, limit - taker)
    shifted = jax.random.randint(jax.random.fold_in(rng, 1), (couples,), 0, 1 << 20) % (room + 1)
    sizes = sizes.at[1:1 + 2 * couples:2].set(source_of - shifted).at[2:2 + 2 * couples:2].set(taker + shifted)
    return sizes[jax.random.permutation(jax.random.fold_in(rng, 2), count)]


def shared_out(key, own, number, rows, count, top, reach, slope):
    ranking = jax.random.permutation(key, count)
    packed, usual = portions_of(count, rows * top, reach, slope, True), portions_of(count, rows * top, reach, slope, False)
    places = jnp.arange(count)

    def named(sizes, rotation):
        used = int((sizes > 0).sum())
        fixed = max(1, used // 4)
        passed = fixed + (places - fixed + rotation * (used - fixed)) % max(1, count - fixed)
        return jnp.zeros((count,), jnp.int32).at[ranking[jnp.where(places < fixed, places, passed)]].set(jnp.asarray(sizes, jnp.int32))

    sizes = jnp.where(number % 4 == 0, named(packed, number // 4), named(usual, number - number // 4 - 1))
    mixed = jax.random.permutation(jax.random.fold_in(own, 3), count)
    giver, receiver = mixed[0:count // 2 * 2:2], mixed[1:count // 2 * 2:2]
    room = jnp.minimum(sizes[giver] - 1, reach - sizes[receiver]) // 2
    room = jnp.where((giver == ranking[0]) | (receiver == ranking[0]) | (sizes[receiver] == 0), 0, jnp.maximum(room, 0))
    passed = jax.random.randint(jax.random.fold_in(own, 4), (count // 2,), 0, 1 << 20) % (room + 1)
    sizes = sizes.at[giver].add(-passed).at[receiver].add(passed)
    labels = jnp.searchsorted(jnp.cumsum(sizes), jnp.arange(rows * top), side="right").astype(jnp.int32)
    grid = labels.reshape(top, rows).T
    grid = grid[jax.random.permutation(jax.random.fold_in(own, 1), rows)]
    rotation = jax.random.randint(jax.random.fold_in(own, 2), (rows, 1), 0, top)
    return jnp.take_along_axis(grid, (jnp.arange(top)[None, :] + rotation) % top, axis=1)


def portions_of(number_of, total, most, slope, full):
    loads = [(1 << 20) // math.isqrt(grade ** slope) + 1 for grade in range(1, number_of + 1)]
    largest = most if full else min(most, max(-(-total // number_of), total * loads[0] // sum(loads)))
    least = 1 if total - largest >= number_of - 1 else 0
    given, rest = [largest] + [least] * (number_of - 1), total - largest - least * (number_of - 1)
    while rest > 0:
        candidates = [i for i in range(1, number_of) if given[i] < largest] or [i for i in range(1, number_of) if given[i] < most]
        whole, budget = sum([loads[i] for i in candidates]), rest
        for i in candidates:
            extra = min(most - given[i], max(1, budget * loads[i] // whole), rest)
            given[i] = given[i] + extra
            rest = rest - extra
    return np.array(given)


def gaussian(stream_key, dims, spread, bound, cuts=(), kind=jnp.bfloat16):
    entries = spread * jax.random.normal(stream_key, dims, jnp.float32)
    if cuts:
        entries = entries * levels(stream_key, dims, cuts, -0.22, 0.18)
    return jnp.clip(entries, -bound, bound).astype(kind)


def setup_inputs(seed: int = 0) -> dict:
    seeds = jax.random.split(jax.random.key(seed), 10)
    queries = draw_queries(jax.random.fold_in(seeds[9], 71), 0)
    fresh_key_value = gaussian(seeds[1], (SLOT_TOTAL, KEY_VALUE_HEADS * 2 * HEAD_WIDTH), 1.0, 6.0, ((0, 128), (1, 4)))
    key_value_page_pool = draw_key_value_page_pool(jax.random.fold_in(seeds[9], 71), 0)
    block_owner_keys = jax.random.split(jax.random.fold_in(seeds[3], 1), (SLOT_TOTAL * BLOCK_LIST_SIZE) // (SLOT_DEV * BLOCK_LIST_SIZE))
    block_owner_turns = jax.random.permutation(jax.random.fold_in(seeds[3], 3), (SLOT_TOTAL * BLOCK_LIST_SIZE) // (SLOT_DEV * BLOCK_LIST_SIZE))
    block_owner = jax.vmap(lambda own, number: shared_out(jax.random.fold_in(seeds[3], 2), own, number, SLOT_DEV * BLOCK_LIST_SIZE, N_REQ, 1, CAP, 2))(block_owner_keys, block_owner_turns).reshape((SLOT_TOTAL * BLOCK_LIST_SIZE, 1))
    block_page = plant(jax.random.randint(seeds[4], (SLOT_TOTAL * BLOCK_LIST_SIZE,), 0, P_DEV), jax.random.fold_in(seeds[4], 1), 0, P_DEV - 1).astype(jnp.int32)
    lengths = ragged(seeds[5], SLOT_TOTAL, SLOT_TOTAL * BLOCK_LIST_SIZE * PAGE_TOKENS // 2, BLOCK_LIST_SIZE * PAGE_TOKENS, 2).astype(jnp.int32)
    o_weight = gaussian(seeds[6], (QUERY_HEADS * HEAD_WIDTH, D), (QUERY_HEADS * HEAD_WIDTH) ** -0.5, 0.125, ((0, 4),))
    resid_in = gaussian(seeds[7], (SLOT_TOTAL, D), 0.1, 0.59765625, ((0, 128),))
    norm_gain = jnp.clip(1.0 + 0.15 * jax.random.normal(seeds[8], (D,), jnp.float32), 0.25, 1.75).astype(jnp.bfloat16)
    return dict(queries=queries, fresh_key_value=fresh_key_value, key_value_page_pool=key_value_page_pool, block_owner=block_owner, block_page=block_page, lengths=lengths, o_weight=o_weight, resid_in=resid_in, norm_gain=norm_gain)


SCORE_FLOOR = -1e+30
HIGH = lax.Precision.HIGHEST

def reference(queries, fresh_key_value, key_value_page_pool, block_owner, block_page, lengths, o_weight, resid_in, norm_gain):
    score_scale = HEAD_WIDTH ** (-0.5)
    query_group_width = QUERY_HEADS // KEY_VALUE_HEADS
    page_rows = (block_owner[:, 0] * P_DEV + block_page).reshape(SLOT_TOTAL, BLOCK_LIST_SIZE).astype(jnp.int32)

    def one_slot(slot_args):
        current_query_row, key_value_row, pages_for_slot, length = slot_args
        page_contents = key_value_page_pool[pages_for_slot].astype(jnp.float32).reshape(BLOCK_LIST_SIZE, PAGE_TOKENS, KEY_VALUE_HEADS, 2, HEAD_WIDTH)
        keys = page_contents[:, :, :, 0, :]
        values = page_contents[:, :, :, 1, :]
        query_head_rows = current_query_row.astype(jnp.float32).reshape(KEY_VALUE_HEADS, query_group_width, HEAD_WIDTH)
        scores = jnp.einsum('kgd,bpkd->bkgp', query_head_rows, keys, precision=HIGH) * score_scale
        live_count = jnp.clip(length - jnp.arange(BLOCK_LIST_SIZE, dtype=jnp.int32) * PAGE_TOKENS, 0, PAGE_TOKENS)
        keep_mask = jnp.arange(PAGE_TOKENS, dtype=jnp.int32)[None, None, None, :] < live_count[:, None, None, None]
        block_max = lax.optimization_barrier(jnp.max(jnp.where(keep_mask, scores, SCORE_FLOOR), axis=-1))
        probs = jnp.where(keep_mask, jnp.exp(scores - block_max[..., None]), jnp.float32(0.0))
        block_sum = lax.optimization_barrier(jnp.sum(probs, axis=-1))
        rounded = lax.optimization_barrier(probs.astype(jnp.bfloat16)).astype(jnp.float32)
        block_out = jnp.einsum('bkgp,bpkd->bkgd', rounded, values, precision=HIGH)
        own_token_key_value = key_value_row.astype(jnp.float32).reshape(KEY_VALUE_HEADS, 2, HEAD_WIDTH)
        self_score = jnp.einsum('kgd,kd->kg', query_head_rows, own_token_key_value[:, 0], precision=HIGH) * score_scale
        top_score = jnp.maximum(lax.optimization_barrier(jnp.max(block_max, axis=0)), self_score)
        weights = jnp.exp(block_max - top_score[None])
        self_weight = jnp.exp(self_score - top_score)
        numer = jnp.einsum('bkg,bkgd->kgd', weights, block_out, precision=HIGH) + self_weight[..., None] * own_token_key_value[:, 1][:, None, :]
        denom = lax.optimization_barrier(jnp.sum(weights * block_sum, axis=0)) + self_weight
        return (numer / denom[..., None]).reshape(QUERY_HEADS * HEAD_WIDTH).astype(jnp.bfloat16)
    attention = lax.map(one_slot, (queries, fresh_key_value, page_rows, lengths))
    stream = resid_in.astype(jnp.float32) + jnp.dot(attention, o_weight, preferred_element_type=jnp.float32)
    mean_square = lax.optimization_barrier(jnp.mean(stream * stream, axis=-1, keepdims=True))
    normed = stream * lax.rsqrt(mean_square + 1e-05) * norm_gain.astype(jnp.float32)
    return (stream.astype(jnp.bfloat16), normed.astype(jnp.bfloat16))
```

```python
import functools

import jax
import jax.numpy as jnp
from jax import lax
from jax.experimental import pallas as pl
from jax.experimental.pallas import tpu as pltpu
from jax.sharding import PartitionSpec as P

F32, BF16, I32 = jnp.float32, jnp.bfloat16, jnp.int32
MESH = pl.DeviceIdType.MESH
NEG = -1e30
CAP = 8
CHUNK = 16
SLOTS = 4
PLANE = 8
VM = pltpu.VMEM


def iota(shape, dim):
    return lax.broadcasted_iota(I32, shape, dim)


def dot_nt(a, b):
    return lax.dot_general(a, b, (((1,), (1,)), ((), ())), preferred_element_type=F32)


def dot_nn(a, b):
    return jnp.dot(a, b, preferred_element_type=F32)


def head_pair_rows(q):
    return jnp.concatenate([q[s : s + 1, 128 * h : 128 * h + 128] for s in range(SLOTS) for h in range(4)], axis=0)


def remote(src, dst, send, recv, peer):
    return pltpu.make_async_remote_copy(
        src_ref=src, dst_ref=dst, send_sem=send, recv_sem=recv, device_id=peer, device_id_type=MESH
    )


def dispatch_kernel(
    nz, q_ref, owner_ref, page_ref, len_ref, qall_ref, mall_ref,
    zq, zsend, zm, ysend, qs_z, qr_z, ms_z, mr_z, qs_y, qr_y, ms_y, mr_y,
):
    me = lax.axis_index("req")
    z, yc = me // PLANE, me % PLANE
    zpeers = [(z + k) % nz for k in range(1, nz)]
    ypeers = [(yc + k) % PLANE for k in range(1, PLANE)]
    barrier = pltpu.get_barrier_semaphore()
    for p in zpeers:
        pl.semaphore_signal(barrier, inc=1, device_id={"req": p * PLANE + yc}, device_id_type=MESH)
    for p in ypeers:
        pl.semaphore_signal(barrier, inc=1, device_id={"req": z * PLANE + p}, device_id_type=MESH)

    zq[z] = head_pair_rows(q_ref[...].astype(F32)).astype(BF16)
    rows, lanes = iota((128, 128), 0), iota((128, 128), 1)
    tri = jnp.where(rows <= lanes, 1.0, 0.0).astype(BF16)
    ones = jnp.ones((128, 128), BF16)
    base = jnp.zeros((128, 128), F32)
    table = jnp.zeros((128, 128), F32)
    for s in range(SLOTS):
        live = jnp.clip(len_ref[s] - iota((1, 128), 1) * 128, 0, 128)
        hit = jnp.logical_and(rows == owner_ref[s : s + 1, :], live > 0)
        hot = jnp.where(hit, 1.0, 0.0).astype(BF16)
        rank = jnp.sum(jnp.where(hit, base + dot_nn(hot, tri) - 1.0, 0.0), axis=0, keepdims=True)
        base = base + dot_nn(hot, ones)
        kind = rows // CAP
        val = jnp.where(
            kind == 0, page_ref[s : s + 1, :].astype(F32),
            jnp.where(kind == 1, live.astype(F32), jnp.where(kind == 2, float(s), 0.0)),
        )
        place = jnp.where((rows % CAP).astype(F32) == rank, val, 0.0).astype(BF16)
        table = table + dot_nt(hot, place)
    zsend[...] = table.reshape(nz, PLANE, 128).astype(BF16)
    zm[z] = zsend[z]

    pl.semaphore_wait(barrier, nz - 1 + PLANE - 1)
    copies = []
    for i, p in enumerate(zpeers):
        to = {"req": p * PLANE + yc}
        copies.append(remote(zq.at[z], zq.at[z], qs_z.at[i], qr_z.at[i], to))
        copies.append(remote(zsend.at[p], zm.at[z], ms_z.at[i], mr_z.at[i], to))
    for c in copies:
        c.start()
    for c in copies:
        c.wait()
    got = zm[...].astype(F32)
    for d in range(PLANE):
        ysend[d] = jnp.concatenate([got[i, d : d + 1, :] for i in range(nz)], axis=0).astype(BF16)
    qall_ref[yc] = zq[...]
    mall_ref[yc] = ysend[yc]
    copies = []
    for i, p in enumerate(ypeers):
        to = {"req": z * PLANE + p}
        copies.append(remote(zq, qall_ref.at[yc], qs_y.at[i], qr_y.at[i], to))
        copies.append(remote(ysend.at[p], mall_ref.at[yc], ms_y.at[i], mr_y.at[i], to))
    for c in copies:
        c.start()
    for c in copies:
        c.wait()


def owner_kernel(
    nz, npages, qall_ref, mall_ref, pool_hbm, po_ref, ps_ref,
    pool, qx, o_s, m_s, l_s, lst_v, sig_v, lst, sig, sems,
):
    nsrc = nz * PLANE
    pool_copy = pltpu.make_async_copy(pool_hbm, pool, sems.at[0])
    pool_copy.start()

    meta = mall_ref[...].astype(F32).reshape(nsrc, 128).T
    page, live, slot = meta[0:8], meta[8:16], meta[16:24]
    valid = live > 0.0
    sig_v[...] = jnp.where(valid, slot, -1.0).astype(I32)
    sig_copy = pltpu.make_async_copy(sig_v, sig, sems.at[1])
    sig_copy.start()

    n8 = npages * 8
    eq = jnp.concatenate([jnp.where(jnp.logical_and(valid, page == float(p)), 1.0, 0.0) for p in range(npages)], axis=0)
    eqb = eq.astype(BF16)
    tri = jnp.where(iota((128, 128), 0) <= iota((128, 128), 1), 1.0, 0.0).astype(BF16)
    cum = dot_nn(eqb, tri)
    tot = dot_nn(eqb, jnp.ones((128, 128), BF16)).astype(BF16)
    ra, rb = iota((n8, n8), 0), iota((n8, n8), 1)
    same = ra // 8 == rb // 8
    before = dot_nn(jnp.where(jnp.logical_and(same, rb < ra), 1.0, 0.0).astype(BF16), tot)
    count = dot_nn(jnp.where(same, 1.0, 0.0).astype(BF16), tot)
    chunks = jnp.floor((count + (CHUNK - 1)) * (1.0 / CHUNK))
    first = dot_nn(
        jnp.where(jnp.logical_and(rb % 8 == 0, rb // 8 < ra // 8), 1.0, 0.0).astype(BF16), chunks.astype(BF16)
    )
    total = (first + chunks)[n8 - 1 : n8, :]
    pos = jnp.sum((eq * (first * CHUNK + before + cum - 1.0)).reshape(npages, 8, 128), axis=0)
    chunk = jnp.floor(pos * (1.0 / CHUNK))
    place = pos - chunk * CHUNK

    krow = iota((CHUNK, 128), 0).astype(F32)
    crow = iota((128, 128), 0).astype(F32)
    src = iota((1, 128), 1).astype(F32)
    lists = jnp.zeros((5 * CHUNK, 128), F32)
    for r in range(CAP):
        row = slice(r, r + 1)
        here = jnp.logical_and(krow == place[row], live[row] > 0.0)
        pick = [jnp.where(here, v, 0.0) for v in (src, float(r + 1), live[row], slot[row], page[row])]
        col = jnp.where(crow == chunk[row], 1.0, 0.0)
        lists = lists + dot_nt(jnp.concatenate(pick, axis=0).astype(BF16), col.astype(BF16))
    srcs, ranks = lists[0:CHUNK], lists[CHUNK : 2 * CHUNK]
    lst_v[0:16] = (srcs * SLOTS + lists[3 * CHUNK : 4 * CHUNK]).astype(I32)
    lst_v[16:32] = jnp.where(ranks > 0.0, (ranks - 1.0) * 128.0 + srcs + 1.0, 0.0).astype(I32)
    lst_v[32:48] = lists[2 * CHUNK : 3 * CHUNK].astype(I32)
    lst_v[48:56] = jnp.concatenate(
        [lists[4 * CHUNK : 4 * CHUNK + 1], total, jnp.zeros((6, 128), F32)], axis=0
    ).astype(I32)
    lst_copy = pltpu.make_async_copy(lst_v, lst, sems.at[2])
    lst_copy.start()

    row8, lane8 = iota((8, 128), 0), iota((8, 128), 1)
    low, left = row8 < 4, lane8 < 64
    keep = jnp.where(left, 0.125, 0.0)

    @pl.loop(0, nsrc)
    def _(i):
        q = qall_ref[i // nz, i % nz].astype(F32)
        for t in range(2):
            v = q[8 * t : 8 * t + 8]
            vs = pltpu.roll(v, 4, 0)
            qx[i * SLOTS + 2 * t] = jnp.where(low, v, pltpu.roll(vs, 64, 1)) * keep
            qx[i * SLOTS + 2 * t + 1] = jnp.where(low, vs, pltpu.roll(v, 64, 1)) * keep

    lst_copy.wait()
    sig_copy.wait()
    pool_copy.wait()
    unroll = 2

    @pl.loop(0, (lst[49, 0] + unroll - 1) // unroll)
    def _(step):
        for u in range(unroll):
            c = step * unroll + u
            kv = pool[lst[48, c]]
            q = jnp.concatenate([qx[lst[k, c]] for k in range(CHUNK)], axis=0).astype(BF16)
            scores = dot_nt(q, kv)
            scores = jnp.concatenate(
                [jnp.where(lane8 < lst[32 + k, c], scores[8 * k : 8 * k + 8], NEG) for k in range(CHUNK)], axis=0
            )
            top = jnp.max(scores, axis=1, keepdims=True)
            probs = jnp.exp(scores - top)
            denom = jnp.sum(probs, axis=1, keepdims=True)
            out = dot_nn(probs.astype(BF16), kv)
            for k in range(CHUNK):
                to = lst[16 + k, c]
                o_s[to] = out[8 * k : 8 * k + 8]
                m_s[to] = jnp.broadcast_to(top[8 * k : 8 * k + 8], (8, 128))
                l_s[to] = jnp.broadcast_to(denom[8 * k : 8 * k + 8], (8, 128))

    for d in range(PLANE):

        def one_source(zi, stat):
            i = d * nz + zi
            slots = [jnp.full((8, 128), sig[r, i], I32) for r in range(CAP)]
            ms = [m_s[1 + r * 128 + i] for r in range(CAP)]
            tops = []
            for s in range(SLOTS):
                top = jnp.full((8, 128), NEG, F32)
                for r in range(CAP):
                    top = jnp.maximum(top, jnp.where(slots[r] == s, ms[r], NEG))
                tops.append(top)
            num = [jnp.zeros((8, 128), F32) for _ in range(SLOTS)]
            den = [jnp.zeros((8, 128), F32) for _ in range(SLOTS)]
            for r in range(CAP):
                top = tops[0]
                for s in range(1, SLOTS):
                    top = jnp.where(slots[r] == s, tops[s], top)
                w = jnp.exp(ms[r] - top)
                o = w * o_s[1 + r * 128 + i]
                l = w * l_s[1 + r * 128 + i]
                for s in range(SLOTS):
                    num[s] = num[s] + jnp.where(slots[r] == s, o, 0.0)
                    den[s] = den[s] + jnp.where(slots[r] == s, l, 0.0)
            outs = []
            for s in range(SLOTS):
                some = den[s] > 0.0
                safe = jnp.where(some, den[s], 1.0)
                outs.append(num[s] / safe)
                lse = jnp.where(some, tops[s] + jnp.log(safe), NEG)
                stat = jnp.where(lane8 == s * nz + zi, lse, stat)
            packed = []
            for t in range(2):
                a, b = outs[2 * t], outs[2 * t + 1]
                first_slot = jnp.where(left, pltpu.roll(a, 64, 1), pltpu.roll(a, 4, 0))
                second = jnp.where(left, pltpu.roll(pltpu.roll(b, 4, 0), 64, 1), b)
                packed.append(jnp.where(low, first_slot, second))
            po_ref[d, zi] = jnp.concatenate(packed, axis=0).astype(BF16)
            return stat

        ps_ref[d] = lax.fori_loop(0, nz, one_source, jnp.full((8, 128), NEG, F32))


def return_kernel(
    nz, ntp, po_ref, ps_ref, q_ref, fresh_ref, w_hbm, resid_ref, gain_ref, res_out, norm_out,
    ro, rs, wn, acc, o1, s1, ro2, rs2, wv, parts,
    os_y, or_y, ss_y, sr_y, os_z, or_z, ss_z, sr_z, ts, tr, wsem,
):
    me, tp = lax.axis_index("req"), lax.axis_index("tp")
    z, yc = me // PLANE, me % PLANE
    zpeers = [(z + k) % nz for k in range(1, nz)]
    ypeers = [(yc + k) % PLANE for k in range(1, PLANE)]
    tpeers = [(tp + k) % ntp for k in range(1, ntp)]
    barrier = pltpu.get_barrier_semaphore()
    for p in zpeers:
        pl.semaphore_signal(barrier, inc=1, device_id={"req": p * PLANE + yc}, device_id_type=MESH)
    for p in ypeers:
        pl.semaphore_signal(barrier, inc=1, device_id={"req": z * PLANE + p}, device_id_type=MESH)
    for p in tpeers:
        pl.semaphore_signal(barrier, inc=1, device_id={"tp": p}, device_id_type=MESH)
    w_copy = pltpu.make_async_copy(w_hbm, wv, wsem.at[0])
    w_copy.start()
    ro[yc] = po_ref[yc]
    rs[yc] = ps_ref[yc]
    pl.semaphore_wait(barrier, nz - 1 + PLANE - 1 + ntp - 1)

    copies = []
    for i, p in enumerate(ypeers):
        to = {"req": z * PLANE + p}
        copies.append(remote(po_ref.at[p], ro.at[yc], os_y.at[i], or_y.at[i], to))
        copies.append(remote(ps_ref.at[p], rs.at[yc], ss_y.at[i], sr_y.at[i], to))
    for c in copies:
        c.start()

    row8, lane8 = iota((8, 128), 0), iota((8, 128), 1)
    low, left = row8 < 4, lane8 < 64
    q16 = head_pair_rows(q_ref[...].astype(F32))
    fresh = fresh_ref[...].astype(F32)
    self_score, self_value = [], []
    for t in range(2):
        kv = jnp.concatenate([fresh[2 * t : 2 * t + 1]] * 4 + [fresh[2 * t + 1 : 2 * t + 2]] * 4, axis=0)
        other = pltpu.roll(kv, 64, 1)
        prod = q16[8 * t : 8 * t + 8] * jnp.where(left, kv, other)
        ls = jnp.sum(jnp.where(left, prod, 0.0), axis=1, keepdims=True)
        rsum = jnp.sum(jnp.where(left, 0.0, prod), axis=1, keepdims=True)
        self_score.append(jnp.where(left, ls, rsum) * 0.125)
        self_value.append(jnp.where(left, other, kv))

    for c in copies:
        c.wait()

    stats = [rs[p] for p in range(PLANE)]
    top = stats[0]
    for p in range(1, PLANE):
        top = jnp.maximum(top, stats[p])
    ws = [jnp.exp(s - top) for s in stats]
    wsum = ws[0]
    for p in range(1, PLANE):
        wsum = wsum + ws[p]
    for p in range(PLANE):
        wn[p] = ws[p] / wsum
    lse = top + jnp.log(wsum)
    acc[...] = jnp.zeros_like(acc)

    def add_part(p, carry):
        x = wn[p]
        xs = pltpu.roll(x, 4, 0)
        yl = jnp.where(low, x, pltpu.roll(xs, 128 - nz, 1))
        yr = jnp.where(low, xs, pltpu.roll(x, 128 - nz, 1))
        for zi in range(nz):
            part = ro[p, zi].astype(F32)
            for t in range(2):
                li = 2 * t * nz + zi
                w = jnp.where(left, yl[:, li : li + 1], yr[:, li : li + 1])
                acc[zi, 8 * t : 8 * t + 8] = acc[zi, 8 * t : 8 * t + 8] + w * part[8 * t : 8 * t + 8]
        return carry

    lax.fori_loop(0, PLANE, add_part, 0)
    o1[...] = acc[...].astype(BF16)
    by_slot = [pltpu.roll(lse, (128 - nz * s) % 128, 1) if s else lse for s in range(SLOTS)]
    rows = jnp.concatenate(by_slot + [jnp.zeros((96, 128), F32)], axis=0).T
    for zi in range(nz):
        s1[zi] = rows[zi : zi + 1]
    ro2[z] = o1[z]
    rs2[z] = s1[z]
    copies = []
    for i, p in enumerate(zpeers):
        to = {"req": p * PLANE + yc}
        copies.append(remote(o1.at[p], ro2.at[z], os_z.at[i], or_z.at[i], to))
        copies.append(remote(s1.at[p], rs2.at[z], ss_z.at[i], sr_z.at[i], to))
    for c in copies:
        c.start()
    for c in copies:
        c.wait()

    st = jnp.concatenate([rs2[zi] for zi in range(nz)], axis=0)
    top = jnp.max(st, axis=0, keepdims=True)
    cols = jnp.concatenate(
        [jnp.exp(st - top), jnp.broadcast_to(top, (8, 128)), jnp.zeros((120 - nz, 128), F32)], axis=0
    ).T
    att = []
    for t in range(2):
        x0, x1 = cols[16 * t : 16 * t + 8], cols[16 * t + 8 : 16 * t + 16]
        yl = jnp.where(low, x0, pltpu.roll(x1, 4, 0))
        yr = jnp.where(low, pltpu.roll(x0, 4, 0), x1)
        num = jnp.zeros((8, 128), F32)
        den = jnp.zeros((8, 128), F32)
        for zi in range(nz):
            w = jnp.where(left, yl[:, zi : zi + 1], yr[:, zi : zi + 1])
            num = num + w * ro2[zi, 8 * t : 8 * t + 8].astype(F32)
            den = den + w
        topm = jnp.where(left, yl[:, nz : nz + 1], yr[:, nz : nz + 1])
        best = jnp.maximum(topm, self_score[t])
        a, b = jnp.exp(topm - best), jnp.exp(self_score[t] - best)
        att.append((a * num + b * self_value[t]) / (a * den + b))
    att = jnp.concatenate(att, axis=0)
    r16 = iota((16, 128), 0)
    wide = jnp.concatenate([jnp.where(r16 % 4 == h, att, 0.0) for h in range(4)], axis=1).astype(BF16)
    sel = jnp.where(iota((16, 16), 1) // 4 == iota((16, 16), 0), 1.0, 0.0).astype(BF16)
    lhs = dot_nn(sel, wide).astype(BF16)
    w_copy.wait()
    parts[tp] = dot_nn(lhs, wv[...])[0:SLOTS]
    copies = []
    for i, p in enumerate(tpeers):
        copies.append(remote(parts.at[tp], parts.at[tp], ts.at[i], tr.at[i], {"tp": p}))
    for c in copies:
        c.start()
    for c in copies:
        c.wait()
    stream = parts[0]
    for p in range(1, ntp):
        stream = stream + parts[p]
    stream = resid_ref[...].astype(F32) + stream
    mean = jnp.mean(stream * stream, axis=1, keepdims=True)
    res_out[...] = stream.astype(BF16)
    norm_out[...] = (stream * lax.rsqrt(mean + 1e-5) * gain_ref[...].astype(F32)).astype(BF16)


def vmem(n):
    return [pl.BlockSpec(memory_space=pltpu.VMEM)] * n


ANY = pl.BlockSpec(memory_space=pl.ANY)


def body(nz, ntp, queries, fresh_key_value, pool, block_owner, block_page, lengths, o_weight, resid_in, norm_gain):
    npages = pool.shape[0]
    width = o_weight.shape[1]
    DMA = pltpu.SemaphoreType.DMA
    qall, mall = pl.pallas_call(
        functools.partial(dispatch_kernel, nz),
        out_shape=(
            jax.ShapeDtypeStruct((PLANE, nz, 16, 128), BF16),
            jax.ShapeDtypeStruct((PLANE, nz, 128), BF16),
        ),
        in_specs=vmem(3) + [pl.BlockSpec(memory_space=pltpu.SMEM)],
        out_specs=tuple(vmem(2)),
        scratch_shapes=[
            VM((nz, 16, 128), BF16), VM((nz, PLANE, 128), BF16), VM((nz, PLANE, 128), BF16),
            VM((PLANE, nz, 128), BF16),
        ]
        + [DMA((nz - 1,))] * 4 + [DMA((PLANE - 1,))] * 4,
        compiler_params=pltpu.CompilerParams(collective_id=0, has_side_effects=True),
        name="dispatch",
    )(queries, block_owner.reshape(SLOTS, 128), block_page.reshape(SLOTS, 128), lengths)

    po, ps = pl.pallas_call(
        functools.partial(owner_kernel, nz, npages),
        out_shape=(
            jax.ShapeDtypeStruct((PLANE, nz, 16, 128), BF16),
            jax.ShapeDtypeStruct((PLANE, 8, 128), F32),
        ),
        in_specs=vmem(2) + [ANY],
        out_specs=tuple(vmem(2)),
        scratch_shapes=[
            VM(pool.shape, BF16),
            VM((PLANE * nz * SLOTS, 8, 128), F32),
            VM((1032, 8, 128), F32), VM((1032, 8, 128), F32), VM((1032, 8, 128), F32),
            VM((56, 128), I32), VM((8, 128), I32),
            pltpu.SMEM((56, 128), I32), pltpu.SMEM((8, 128), I32),
            DMA((3,)),
        ],
        compiler_params=pltpu.CompilerParams(vmem_limit_bytes=40 << 20),
        name="owner",
    )(qall, mall, pool)

    return pl.pallas_call(
        functools.partial(return_kernel, nz, ntp),
        out_shape=(
            jax.ShapeDtypeStruct((SLOTS, width), BF16),
            jax.ShapeDtypeStruct((SLOTS, width), BF16),
        ),
        in_specs=vmem(4) + [ANY] + vmem(2),
        out_specs=tuple(vmem(2)),
        scratch_shapes=[
            VM((PLANE, nz, 16, 128), BF16), VM((PLANE, 8, 128), F32), VM((PLANE, 8, 128), F32),
            VM((nz, 16, 128), F32), VM((nz, 16, 128), BF16), VM((nz, 1, 128), F32),
            VM((nz, 16, 128), BF16), VM((nz, 1, 128), F32), VM(o_weight.shape, BF16),
            VM((ntp, SLOTS, width), F32),
        ]
        + [DMA((PLANE - 1,))] * 4 + [DMA((nz - 1,))] * 4 + [DMA((ntp - 1,))] * 2 + [DMA((1,))],
        compiler_params=pltpu.CompilerParams(
            collective_id=1, has_side_effects=True, vmem_limit_bytes=24 << 20
        ),
        name="give_back",
    )(po, ps, queries, fresh_key_value, o_weight, resid_in, norm_gain.reshape(1, width))


def solution(mesh):
    nz, ntp = mesh.shape["req"] // PLANE, mesh.shape["tp"]
    placed = (
        P("req", "tp"), P("req", "tp"), P("req", None, "tp"), P("req", None), P("req"), P("req"),
        P("tp", None), P("req", None), P(),
    )
    return jax.shard_map(
        functools.partial(body, nz, ntp),
        mesh=mesh,
        in_specs=placed,
        out_specs=(P("req", None), P("req", None)),
        check_vma=False,
    )
```

```python
import functools

import jax
import jax.numpy as jnp
from jax import lax
from jax.experimental import pallas as pl
from jax.experimental.pallas import tpu as pltpu
from jax.sharding import PartitionSpec as P

F32, BF16, I32 = jnp.float32, jnp.bfloat16, jnp.int32
MESH = pl.DeviceIdType.MESH
NEG = -1e30
CAP = 8
CHUNK = 16
SLOTS = 4
PLANE = 8
VM = pltpu.VMEM


def iota(shape, dim):
    return lax.broadcasted_iota(I32, shape, dim)


def dot_nt(a, b):
    return lax.dot_general(a, b, (((1,), (1,)), ((), ())), preferred_element_type=F32)


def dot_nn(a, b):
    return jnp.dot(a, b, preferred_element_type=F32)


def head_pair_rows(q):
    return jnp.concatenate([q[s : s + 1, 128 * h : 128 * h + 128] for s in range(SLOTS) for h in range(4)], axis=0)


def remote(src, dst, send, recv, peer):
    return pltpu.make_async_remote_copy(
        src_ref=src, dst_ref=dst, send_sem=send, recv_sem=recv, device_id=peer, device_id_type=MESH
    )


def dispatch_kernel(
    nz, q_ref, owner_ref, page_ref, len_ref, qall_ref, mall_ref,
    zq, zsend, zm, ysend, qs_z, qr_z, ms_z, mr_z, qs_y, qr_y, ms_y, mr_y,
):
    me = lax.axis_index("req")
    z, yc = me // PLANE, me % PLANE
    zpeers = [(z + k) % nz for k in range(1, nz)]
    ypeers = [(yc + k) % PLANE for k in range(1, PLANE)]
    barrier = pltpu.get_barrier_semaphore()
    for p in zpeers:
        pl.semaphore_signal(barrier, inc=1, device_id={"req": p * PLANE + yc}, device_id_type=MESH)
    for p in ypeers:
        pl.semaphore_signal(barrier, inc=1, device_id={"req": z * PLANE + p}, device_id_type=MESH)

    zq[z] = head_pair_rows(q_ref[...].astype(F32)).astype(BF16)
    rows, lanes = iota((128, 128), 0), iota((128, 128), 1)
    tri = jnp.where(rows <= lanes, 1.0, 0.0).astype(BF16)
    ones = jnp.ones((128, 128), BF16)
    base = jnp.zeros((128, 128), F32)
    table = jnp.zeros((128, 128), F32)
    for s in range(SLOTS):
        live = jnp.clip(len_ref[s] - iota((1, 128), 1) * 128, 0, 128)
        hit = jnp.logical_and(rows == owner_ref[s : s + 1, :], live > 0)
        hot = jnp.where(hit, 1.0, 0.0).astype(BF16)
        rank = jnp.sum(jnp.where(hit, base + dot_nn(hot, tri) - 1.0, 0.0), axis=0, keepdims=True)
        base = base + dot_nn(hot, ones)
        kind = rows // CAP
        val = jnp.where(
            kind == 0, page_ref[s : s + 1, :].astype(F32),
            jnp.where(kind == 1, live.astype(F32), jnp.where(kind == 2, float(s), 0.0)),
        )
        place = jnp.where((rows % CAP).astype(F32) == rank, val, 0.0).astype(BF16)
        table = table + dot_nt(hot, place)
    zsend[...] = table.reshape(nz, PLANE, 128).astype(BF16)
    zm[z] = zsend[z]

    pl.semaphore_wait(barrier, nz - 1 + PLANE - 1)
    copies = []
    for i, p in enumerate(zpeers):
        to = {"req": p * PLANE + yc}
        copies.append(remote(zq.at[z], zq.at[z], qs_z.at[i], qr_z.at[i], to))
        copies.append(remote(zsend.at[p], zm.at[z], ms_z.at[i], mr_z.at[i], to))
    for c in copies:
        c.start()
    for c in copies:
        c.wait()
    got = zm[...].astype(F32)
    for d in range(PLANE):
        ysend[d] = jnp.concatenate([got[i, d : d + 1, :] for i in range(nz)], axis=0).astype(BF16)
    qall_ref[yc] = zq[...]
    mall_ref[yc] = ysend[yc]
    copies = []
    for i, p in enumerate(ypeers):
        to = {"req": z * PLANE + p}
        copies.append(remote(zq, qall_ref.at[yc], qs_y.at[i], qr_y.at[i], to))
        copies.append(remote(ysend.at[p], mall_ref.at[yc], ms_y.at[i], mr_y.at[i], to))
    for c in copies:
        c.start()
    for c in copies:
        c.wait()


def owner_kernel(
    nz, npages, qall_ref, mall_ref, pool, po_ref, ps_ref,
    qx, o_s, ml_s, wn_s, sg_s, s0, s1, p0, p1, lst_v, lst, sems,
):
    nsrc = nz * PLANE
    row8, lane8 = iota((8, 128), 0), iota((8, 128), 1)
    low, left = row8 < 4, lane8 < 64
    meta_b = mall_ref[...].reshape(nsrc, 128)
    meta = meta_b.astype(F32).T
    page, live, slot = meta[0:8], meta[8:16], meta[16:24]
    valid = live > 0.0

    prow = iota((npages, 128), 0).astype(F32)
    eqs = [
        jnp.where(jnp.logical_and(prow == page[r : r + 1], live[r : r + 1] > 0.0), 1.0, 0.0) for r in range(CAP)
    ]
    upto = jnp.where(iota((128, 256), 0) <= iota((128, 256), 1), 1.0, 0.0).astype(BF16)
    counts = dot_nn(jnp.concatenate(eqs, axis=0).astype(BF16), upto)
    run = jnp.zeros((npages, 128), F32)
    ranks = []
    for r in range(CAP):
        part = counts[npages * r : npages * r + npages]
        ranks.append(run + part[:, 0:128])
        run = run + part[:, 128:256]
    chunks = jnp.floor((run + (CHUNK - 1)) * (1.0 / CHUNK))
    below = jnp.where(iota((npages, npages), 1) < iota((npages, npages), 0), 1.0, 0.0).astype(BF16)
    first = dot_nn(below, chunks.astype(BF16))
    total = (first + chunks)[npages - 1 : npages]

    krow = iota((CHUNK, 128), 0).astype(F32)
    crow = iota((128, 128), 0).astype(F32)
    src = iota((1, 128), 1).astype(F32)
    lists = jnp.zeros((5 * CHUNK, 128), F32)
    for r in range(CAP):
        row = slice(r, r + 1)
        pos = jnp.sum(eqs[r] * (first * CHUNK + ranks[r] - 1.0), axis=0, keepdims=True)
        chunk = jnp.floor(pos * (1.0 / CHUNK))
        here = jnp.logical_and(krow == pos - chunk * CHUNK, live[row] > 0.0)
        pick = [jnp.where(here, v, 0.0) for v in (src, float(r + 1), live[row], slot[row], page[row])]
        col = jnp.where(crow == chunk, 1.0, 0.0)
        lists = lists + dot_nt(jnp.concatenate(pick, axis=0).astype(BF16), col.astype(BF16))
    srcs, nth = lists[0:CHUNK], lists[CHUNK : 2 * CHUNK]
    lst_v[0:16] = (srcs * SLOTS + lists[3 * CHUNK : 4 * CHUNK]).astype(I32)
    lst_v[16:32] = jnp.where(nth > 0.0, srcs * CAP + nth - 1.0, float(nsrc * CAP)).astype(I32)
    lst_v[32:48] = lists[2 * CHUNK : 3 * CHUNK].astype(I32)
    lst_v[48:56] = jnp.concatenate(
        [lists[4 * CHUNK : 4 * CHUNK + 1], total, jnp.zeros((6, 128), F32)], axis=0
    ).astype(I32)
    lst_copy = pltpu.make_async_copy(lst_v, lst, sems.at[0])
    lst_copy.start()

    keep = jnp.where(left, 0.125, 0.0)
    group = 8

    @pl.loop(0, nsrc // group)
    def _(g):
        for u in range(group):
            i = g * group + u
            q = qall_ref[i // nz, i % nz].astype(F32)
            for t in range(2):
                v = q[8 * t : 8 * t + 8]
                vs = pltpu.roll(v, 4, 0)
                qx[i * SLOTS + 2 * t] = jnp.where(low, v, pltpu.roll(vs, 64, 1)) * keep
                qx[i * SLOTS + 2 * t + 1] = jnp.where(low, vs, pltpu.roll(v, 64, 1)) * keep

    spread = jnp.where(iota((128, 128), 0) == 2 * CAP + iota((128, 128), 1) // 8 % CAP, 1.0, 0.0).astype(BF16)
    sg_s[...] = dot_nn(meta_b, spread)
    lst_copy.wait()

    def scores_of(c, out):
        c = jnp.clip(c, 0, 127)
        q = jnp.concatenate([qx[lst[k, c]] for k in range(CHUNK)], axis=0).astype(BF16)
        out[...] = dot_nt(q, pool[lst[48, c]])

    def probs_of(c, scores, out):
        c = jnp.clip(c, 0, 127)
        pair = []
        for k in range(CHUNK):
            sc = jnp.where(lane8 < lst[32 + k, c], scores[8 * k : 8 * k + 8], NEG)
            top = jnp.max(sc, axis=1, keepdims=True)
            pr = jnp.exp(sc - top)
            ml_s[lst[16 + k, c]] = jnp.where(left, top, jnp.sum(pr, axis=1, keepdims=True))
            pair.append(pr)
            if k % 2:
                out[8 * k - 8 : 8 * k + 8] = jnp.concatenate(pair, axis=0).astype(BF16)
                pair = []

    def values_of(c, probs):
        c = jnp.clip(c, 0, 127)
        out = dot_nn(probs[...], pool[lst[48, c]])
        for k in range(CHUNK):
            o_s[lst[16 + k, c]] = out[8 * k : 8 * k + 8]

    @pl.loop(0, (lst[49, 0] + 3) // 2)
    def _(step):
        c = 2 * step
        scores_of(c, s0)
        probs_of(c - 1, s1, p1)
        values_of(c - 2, p0)
        scores_of(c + 1, s1)
        probs_of(c, s0, p0)
        values_of(c - 1, p1)

    halves = []
    for h in range(2):

        def gather(g, accs, h=h):
            accs = list(accs)
            for u in range(8):
                i = g * 8 + u
                mask = lane8 % 64 == i
                for r in range(CAP):
                    accs[r] = jnp.where(mask, ml_s[(h * 64 + i) * CAP + r], accs[r])
            return tuple(accs)

        halves.append(lax.fori_loop(0, 8, gather, tuple(jnp.zeros((8, 128), F32) for _ in range(CAP))))
    mine = [[jnp.logical_and(live[r : r + 1] > 0.0, slot[r : r + 1] == float(s)) for s in range(SLOTS)] for r in range(CAP)]
    ms = [jnp.where(left, halves[0][r], pltpu.roll(halves[1][r], 64, 1)) for r in range(CAP)]
    ls = [jnp.where(left, pltpu.roll(halves[0][r], 64, 1), halves[1][r]) for r in range(CAP)]
    tops, dens = [], []
    for s in range(SLOTS):
        top = jnp.full((8, 128), NEG, F32)
        for r in range(CAP):
            top = jnp.maximum(top, jnp.where(mine[r][s], ms[r], NEG))
        tops.append(top)
    es = []
    for r in range(CAP):
        top = ms[r]
        for s in range(SLOTS):
            top = jnp.where(mine[r][s], tops[s], top)
        es.append(jnp.exp(ms[r] - top))
    lses, invs = [], []
    for s in range(SLOTS):
        den = jnp.zeros((8, 128), F32)
        for r in range(CAP):
            den = den + jnp.where(mine[r][s], es[r] * ls[r], 0.0)
        some = den > 0.0
        den = jnp.where(some, den, 1.0)
        invs.append(1.0 / den)
        lses.append(jnp.where(some, tops[s] + jnp.log(den), NEG))
    for r in range(CAP):
        w = jnp.zeros((8, 128), F32)
        for s in range(SLOTS):
            w = jnp.where(mine[r][s], es[r] * invs[s], w)
        wn_s[r] = w
    for d in range(PLANE):
        stat = jnp.full((8, 128), NEG, F32)
        for s in range(SLOTS):
            shift = (nz * (s - d)) % 128
            moved = pltpu.roll(lses[s], shift, 1) if shift else lses[s]
            stat = jnp.where(lane8 // nz == s, moved, stat)
        ps_ref[d] = stat

    ar, al = iota((64, 128), 0), iota((64, 128), 1)
    same = jnp.logical_and(ar // 32 == al // 64, ar // 16 % 2 * 4 + ar % 4 == al % 8)
    want = jnp.where(same, ar // 4 % 4, -1).astype(F32)
    left16 = iota((16, 128), 1) < 64

    @pl.loop(0, PLANE)
    def _(d):
        ws = [pltpu.roll(wn_s[r], (128 - nz * d) % 128, 1) for r in range(CAP)]
        for j in range(nz // 2):
            scaled = []
            for a in range(2):
                for r in range(CAP):
                    w = jnp.broadcast_to(ws[r][:, 2 * j + a : 2 * j + a + 1], (8, 128))
                    o = o_s[(d * nz + 2 * j + a) * CAP + r]
                    scaled.append(jnp.where(w > 0.0, o * w, 0.0))
            i = d * nz + 2 * j
            sg = jnp.where(lane8[0:1] < 64, sg_s[pl.ds(i, 1), :], sg_s[pl.ds(i + 1, 1), :])
            pickm = jnp.where(want == sg, 1.0, 0.0).astype(BF16)
            res = dot_nn(pickm, jnp.concatenate(scaled, axis=0).astype(BF16))
            for a in range(2):
                even, odd = res[32 * a : 32 * a + 16], res[32 * a + 16 : 32 * a + 32]
                po_ref[d, 2 * j + a] = jnp.where(left16, pltpu.roll(even, 64, 1), odd).astype(BF16)


def return_kernel(
    nz, ntp, po_ref, ps_ref, q_ref, fresh_ref, w_hbm, resid_ref, gain_ref, res_out, norm_out,
    ro, rs, wn, acc, o1, s1, ro2, rs2, wv, parts,
    os_y, or_y, ss_y, sr_y, os_z, or_z, ss_z, sr_z, ts, tr, wsem,
):
    me, tp = lax.axis_index("req"), lax.axis_index("tp")
    z, yc = me // PLANE, me % PLANE
    zpeers = [(z + k) % nz for k in range(1, nz)]
    ypeers = [(yc + k) % PLANE for k in range(1, PLANE)]
    tpeers = [(tp + k) % ntp for k in range(1, ntp)]
    barrier = pltpu.get_barrier_semaphore()
    for p in zpeers:
        pl.semaphore_signal(barrier, inc=1, device_id={"req": p * PLANE + yc}, device_id_type=MESH)
    for p in ypeers:
        pl.semaphore_signal(barrier, inc=1, device_id={"req": z * PLANE + p}, device_id_type=MESH)
    for p in tpeers:
        pl.semaphore_signal(barrier, inc=1, device_id={"tp": p}, device_id_type=MESH)
    w_copy = pltpu.make_async_copy(w_hbm, wv, wsem.at[0])
    w_copy.start()
    ro[yc] = po_ref[yc]
    rs[yc] = ps_ref[yc]
    pl.semaphore_wait(barrier, nz - 1 + PLANE - 1 + ntp - 1)

    copies = []
    for i, p in enumerate(ypeers):
        to = {"req": z * PLANE + p}
        copies.append(remote(po_ref.at[p], ro.at[yc], os_y.at[i], or_y.at[i], to))
        copies.append(remote(ps_ref.at[p], rs.at[yc], ss_y.at[i], sr_y.at[i], to))
    for c in copies:
        c.start()

    row8, lane8 = iota((8, 128), 0), iota((8, 128), 1)
    low, left = row8 < 4, lane8 < 64
    q16 = head_pair_rows(q_ref[...].astype(F32))
    fresh = fresh_ref[...].astype(F32)
    self_score, self_value = [], []
    for t in range(2):
        kv = jnp.concatenate([fresh[2 * t : 2 * t + 1]] * 4 + [fresh[2 * t + 1 : 2 * t + 2]] * 4, axis=0)
        other = pltpu.roll(kv, 64, 1)
        prod = q16[8 * t : 8 * t + 8] * jnp.where(left, kv, other)
        ls = jnp.sum(jnp.where(left, prod, 0.0), axis=1, keepdims=True)
        rsum = jnp.sum(jnp.where(left, 0.0, prod), axis=1, keepdims=True)
        self_score.append(jnp.where(left, ls, rsum) * 0.125)
        self_value.append(jnp.where(left, other, kv))

    for c in copies:
        c.wait()

    stats = [rs[p] for p in range(PLANE)]
    top = stats[0]
    for p in range(1, PLANE):
        top = jnp.maximum(top, stats[p])
    ws = [jnp.exp(s - top) for s in stats]
    wsum = ws[0]
    for p in range(1, PLANE):
        wsum = wsum + ws[p]
    for p in range(PLANE):
        wn[p] = ws[p] / wsum
    lse = top + jnp.log(wsum)
    acc[...] = jnp.zeros_like(acc)

    def add_part(p, carry):
        x = wn[p]
        xs = pltpu.roll(x, 4, 0)
        yl = jnp.where(low, x, pltpu.roll(xs, 128 - nz, 1))
        yr = jnp.where(low, xs, pltpu.roll(x, 128 - nz, 1))
        for zi in range(nz):
            part = ro[p, zi].astype(F32)
            for t in range(2):
                li = 2 * t * nz + zi
                w = jnp.where(left, yl[:, li : li + 1], yr[:, li : li + 1])
                acc[zi, 8 * t : 8 * t + 8] = acc[zi, 8 * t : 8 * t + 8] + w * part[8 * t : 8 * t + 8]
        return carry

    lax.fori_loop(0, PLANE, add_part, 0)
    o1[...] = acc[...].astype(BF16)
    by_slot = [pltpu.roll(lse, (128 - nz * s) % 128, 1) if s else lse for s in range(SLOTS)]
    rows = jnp.concatenate(by_slot + [jnp.zeros((96, 128), F32)], axis=0).T
    for zi in range(nz):
        s1[zi] = rows[zi : zi + 1]
    ro2[z] = o1[z]
    rs2[z] = s1[z]
    copies = []
    for i, p in enumerate(zpeers):
        to = {"req": p * PLANE + yc}
        copies.append(remote(o1.at[p], ro2.at[z], os_z.at[i], or_z.at[i], to))
        copies.append(remote(s1.at[p], rs2.at[z], ss_z.at[i], sr_z.at[i], to))
    for c in copies:
        c.start()
    for c in copies:
        c.wait()

    st = jnp.concatenate([rs2[zi] for zi in range(nz)], axis=0)
    top = jnp.max(st, axis=0, keepdims=True)
    cols = jnp.concatenate(
        [jnp.exp(st - top), jnp.broadcast_to(top, (8, 128)), jnp.zeros((120 - nz, 128), F32)], axis=0
    ).T
    att = []
    for t in range(2):
        x0, x1 = cols[16 * t : 16 * t + 8], cols[16 * t + 8 : 16 * t + 16]
        yl = jnp.where(low, x0, pltpu.roll(x1, 4, 0))
        yr = jnp.where(low, pltpu.roll(x0, 4, 0), x1)
        num = jnp.zeros((8, 128), F32)
        den = jnp.zeros((8, 128), F32)
        for zi in range(nz):
            w = jnp.where(left, yl[:, zi : zi + 1], yr[:, zi : zi + 1])
            num = num + w * ro2[zi, 8 * t : 8 * t + 8].astype(F32)
            den = den + w
        topm = jnp.where(left, yl[:, nz : nz + 1], yr[:, nz : nz + 1])
        best = jnp.maximum(topm, self_score[t])
        a, b = jnp.exp(topm - best), jnp.exp(self_score[t] - best)
        att.append((a * num + b * self_value[t]) / (a * den + b))
    att = jnp.concatenate(att, axis=0)
    r16 = iota((16, 128), 0)
    wide = jnp.concatenate([jnp.where(r16 % 4 == h, att, 0.0) for h in range(4)], axis=1).astype(BF16)
    sel = jnp.where(iota((16, 16), 1) // 4 == iota((16, 16), 0), 1.0, 0.0).astype(BF16)
    lhs = dot_nn(sel, wide).astype(BF16)
    w_copy.wait()
    parts[tp] = dot_nn(lhs, wv[...])[0:SLOTS]
    copies = []
    for i, p in enumerate(tpeers):
        copies.append(remote(parts.at[tp], parts.at[tp], ts.at[i], tr.at[i], {"tp": p}))
    for c in copies:
        c.start()
    for c in copies:
        c.wait()
    stream = parts[0]
    for p in range(1, ntp):
        stream = stream + parts[p]
    stream = resid_ref[...].astype(F32) + stream
    mean = jnp.mean(stream * stream, axis=1, keepdims=True)
    res_out[...] = stream.astype(BF16)
    norm_out[...] = (stream * lax.rsqrt(mean + 1e-5) * gain_ref[...].astype(F32)).astype(BF16)


def vmem(n):
    return [pl.BlockSpec(memory_space=pltpu.VMEM)] * n


ANY = pl.BlockSpec(memory_space=pl.ANY)


def owner_call(nz, qall, mall, pool):
    nsrc = nz * PLANE
    return pl.pallas_call(
        functools.partial(owner_kernel, nz, pool.shape[0]),
        out_shape=(
            jax.ShapeDtypeStruct((PLANE, nz, 16, 128), BF16),
            jax.ShapeDtypeStruct((PLANE, 8, 128), F32),
        ),
        in_specs=vmem(3),
        out_specs=tuple(vmem(2)),
        scratch_shapes=[
            VM((nsrc * SLOTS, 8, 128), F32),
            VM((nsrc * CAP + 1, 8, 128), F32), VM((nsrc * CAP + 1, 8, 128), F32),
            VM((CAP, 8, 128), F32), VM((nsrc, 128), F32),
            VM((128, 128), F32), VM((128, 128), F32), VM((128, 128), BF16), VM((128, 128), BF16),
            VM((56, 128), I32), pltpu.SMEM((56, 128), I32),
            pltpu.SemaphoreType.DMA((1,)),
        ],
        compiler_params=pltpu.CompilerParams(vmem_limit_bytes=20 << 20),
        name="owner",
    )(qall, mall, pool)


def body(nz, ntp, queries, fresh_key_value, pool, block_owner, block_page, lengths, o_weight, resid_in, norm_gain):
    width = o_weight.shape[1]
    DMA = pltpu.SemaphoreType.DMA
    qall, mall = pl.pallas_call(
        functools.partial(dispatch_kernel, nz),
        out_shape=(
            jax.ShapeDtypeStruct((PLANE, nz, 16, 128), BF16),
            jax.ShapeDtypeStruct((PLANE, nz, 128), BF16),
        ),
        in_specs=vmem(3) + [pl.BlockSpec(memory_space=pltpu.SMEM)],
        out_specs=tuple(vmem(2)),
        scratch_shapes=[
            VM((nz, 16, 128), BF16), VM((nz, PLANE, 128), BF16), VM((nz, PLANE, 128), BF16),
            VM((PLANE, nz, 128), BF16),
        ]
        + [DMA((nz - 1,))] * 4 + [DMA((PLANE - 1,))] * 4,
        compiler_params=pltpu.CompilerParams(
            collective_id=0, has_side_effects=True, vmem_limit_bytes=6 << 20
        ),
        name="dispatch",
    )(queries, block_owner.reshape(SLOTS, 128), block_page.reshape(SLOTS, 128), lengths)

    po, ps = owner_call(nz, qall, mall, pool)
    return pl.pallas_call(
        functools.partial(return_kernel, nz, ntp),
        out_shape=(
            jax.ShapeDtypeStruct((SLOTS, width), BF16),
            jax.ShapeDtypeStruct((SLOTS, width), BF16),
        ),
        in_specs=vmem(4) + [ANY] + vmem(2),
        out_specs=tuple(vmem(2)),
        scratch_shapes=[
            VM((PLANE, nz, 16, 128), BF16), VM((PLANE, 8, 128), F32), VM((PLANE, 8, 128), F32),
            VM((nz, 16, 128), F32), VM((nz, 16, 128), BF16), VM((nz, 1, 128), F32),
            VM((nz, 16, 128), BF16), VM((nz, 1, 128), F32), VM(o_weight.shape, BF16),
            VM((ntp, SLOTS, width), F32),
        ]
        + [DMA((PLANE - 1,))] * 4 + [DMA((nz - 1,))] * 4 + [DMA((ntp - 1,))] * 2 + [DMA((1,))],
        compiler_params=pltpu.CompilerParams(
            collective_id=1, has_side_effects=True, vmem_limit_bytes=12 << 20
        ),
        name="give_back",
    )(po, ps, queries, fresh_key_value, o_weight, resid_in, norm_gain.reshape(1, width))


def solution(mesh):
    nz, ntp = mesh.shape["req"] // PLANE, mesh.shape["tp"]
    placed = (
        P("req", "tp"), P("req", "tp"), P("req", None, "tp"), P("req", None), P("req"), P("req"),
        P("tp", None), P("req", None), P(),
    )
    return jax.shard_map(
        functools.partial(body, nz, ntp),
        mesh=mesh,
        in_specs=placed,
        out_specs=(P("req", None), P("req", None)),
        check_vma=False,
    )
```

```python
import functools

import jax
import jax.numpy as jnp
from jax import lax
from jax.experimental import pallas as pl
from jax.experimental.pallas import tpu as pltpu
from jax.sharding import PartitionSpec as P

F32, BF16, I32 = jnp.float32, jnp.bfloat16, jnp.int32
MESH = pl.DeviceIdType.MESH
NEG = -1e30
CAP = 8
CHUNK = 16
SLOTS = 4
PLANE = 8
VM = pltpu.VMEM


def iota(shape, dim):
    return lax.broadcasted_iota(I32, shape, dim)


def dot_nt(a, b):
    return lax.dot_general(a, b, (((1,), (1,)), ((), ())), preferred_element_type=F32)


def dot_nn(a, b):
    return jnp.dot(a, b, preferred_element_type=F32)


def head_pair_rows(q):
    return jnp.concatenate([q[s : s + 1, 128 * h : 128 * h + 128] for s in range(SLOTS) for h in range(4)], axis=0)


def remote(src, dst, send, recv, peer):
    return pltpu.make_async_remote_copy(
        src_ref=src, dst_ref=dst, send_sem=send, recv_sem=recv, device_id=peer, device_id_type=MESH
    )


def start_all(copies):
    for c in copies:
        c.start()


def wait_all(copies):
    for c in copies:
        c.wait()


def far_first(n):
    return sorted(range(1, n), key=lambda k: -min(k, n - k))


def sort_items(nsrc, npages, meta_b, lists_ref, items_ref, slots_ref):
    meta = meta_b.astype(F32).T
    page, live, slot = meta[0:8], meta[8:16], meta[16:24]
    items_ref[0:8] = live
    items_ref[8:16] = slot
    prow = iota((npages, 128), 0).astype(F32)
    eqs = [
        jnp.where(jnp.logical_and(prow == page[r : r + 1], live[r : r + 1] > 0.0), 1.0, 0.0) for r in range(CAP)
    ]
    upto = jnp.where(iota((128, 256), 0) <= iota((128, 256), 1), 1.0, 0.0).astype(BF16)
    counts = dot_nn(jnp.concatenate(eqs, axis=0).astype(BF16), upto)
    run = jnp.zeros((npages, 128), F32)
    ranks = []
    for r in range(CAP):
        part = counts[npages * r : npages * r + npages]
        ranks.append(run + part[:, 0:128])
        run = run + part[:, 128:256]
    chunks = jnp.floor((run + (CHUNK - 1)) * (1.0 / CHUNK))
    below = jnp.where(iota((npages, npages), 1) < iota((npages, npages), 0), 1.0, 0.0).astype(BF16)
    first = dot_nn(below, chunks.astype(BF16))
    total = (first + chunks)[npages - 1 : npages]

    krow = iota((CHUNK, 128), 0).astype(F32)
    crow = iota((128, 128), 0).astype(F32)
    src = iota((1, 128), 1).astype(F32)
    lists = jnp.zeros((5 * CHUNK, 128), F32)
    for r in range(CAP):
        row = slice(r, r + 1)
        pos = jnp.sum(eqs[r] * (first * CHUNK + ranks[r] - 1.0), axis=0, keepdims=True)
        chunk = jnp.floor(pos * (1.0 / CHUNK))
        here = jnp.logical_and(krow == pos - chunk * CHUNK, live[row] > 0.0)
        pick = [jnp.where(here, v, 0.0) for v in (src, float(r + 1), live[row], slot[row], page[row])]
        col = jnp.where(crow == chunk, 1.0, 0.0)
        lists = lists + dot_nt(jnp.concatenate(pick, axis=0).astype(BF16), col.astype(BF16))
    srcs, nth = lists[0:CHUNK], lists[CHUNK : 2 * CHUNK]
    lists_ref[0:16] = (srcs * SLOTS + lists[3 * CHUNK : 4 * CHUNK]).astype(I32)
    lists_ref[16:32] = jnp.where(nth > 0.0, srcs * CAP + nth - 1.0, float(nsrc * CAP)).astype(I32)
    lists_ref[32:48] = lists[2 * CHUNK : 3 * CHUNK].astype(I32)
    lists_ref[48:56] = jnp.concatenate(
        [lists[4 * CHUNK : 4 * CHUNK + 1], total, jnp.zeros((6, 128), F32)], axis=0
    ).astype(I32)
    spread = jnp.where(iota((128, 128), 0) == 2 * CAP + iota((128, 128), 1) // 8 % CAP, 1.0, 0.0).astype(BF16)
    slots_ref[...] = dot_nn(meta_b, spread)


def dispatch_kernel(
    nz, npages, q_hbm, owner_hbm, page_hbm, len_hbm, qall_ref, lists_ref, items_ref, slots_ref,
    q_v, owner_v, page_v, len_s, zq, zsend, zm, ysend, mall,
    in_sem, qs_z, qr_z, ms_z, mr_z, qs_y, qr_y, qs_c, qr_c, ms_y, mr_y,
):
    me = lax.axis_index("req")
    z, yc = me // PLANE, me % PLANE
    y, core = yc // 2, yc % 2
    sib = yc + 1 - 2 * core
    zpeers = [(z + k) % nz for k in far_first(nz)]
    plane = [(yc + k) % PLANE for k in range(1, PLANE)]
    ypeers = [(y + k) % 4 for k in (2, 1, 3)]
    barrier = pltpu.get_barrier_semaphore()
    for p in zpeers:
        pl.semaphore_signal(barrier, inc=1, device_id={"req": p * PLANE + yc}, device_id_type=MESH)
    for p in plane:
        pl.semaphore_signal(barrier, inc=1, device_id={"req": z * PLANE + p}, device_id_type=MESH)
    ins = [
        pltpu.make_async_copy(h, v, in_sem.at[i])
        for i, (h, v) in enumerate([(q_hbm, q_v), (owner_hbm, owner_v), (page_hbm, page_v), (len_hbm, len_s)])
    ]
    start_all(ins)
    ins[0].wait()
    zq[z] = head_pair_rows(q_v[...].astype(F32)).astype(BF16)
    pl.semaphore_wait(barrier, nz - 1 + PLANE - 1)
    q_z = [
        remote(zq.at[z], zq.at[z], qs_z.at[i], qr_z.at[i], {"req": p * PLANE + yc}) for i, p in enumerate(zpeers)
    ]
    start_all(q_z)

    wait_all(ins[1:])
    rows, lanes = iota((128, 128), 0), iota((128, 128), 1)
    tri = jnp.where(rows <= lanes, 1.0, 0.0).astype(BF16)
    ones = jnp.ones((128, 128), BF16)
    base = jnp.zeros((128, 128), F32)
    table = jnp.zeros((128, 128), F32)
    for s in range(SLOTS):
        live = jnp.clip(len_s[s] - iota((1, 128), 1) * 128, 0, 128)
        hit = jnp.logical_and(rows == owner_v[s : s + 1, :], live > 0)
        hot = jnp.where(hit, 1.0, 0.0).astype(BF16)
        rank = jnp.sum(jnp.where(hit, base + dot_nn(hot, tri) - 1.0, 0.0), axis=0, keepdims=True)
        base = base + dot_nn(hot, ones)
        kind = rows // CAP
        val = jnp.where(
            kind == 0, page_v[s : s + 1, :].astype(F32),
            jnp.where(kind == 1, live.astype(F32), jnp.where(kind == 2, float(s), 0.0)),
        )
        place = jnp.where((rows % CAP).astype(F32) == rank, val, 0.0).astype(BF16)
        table = table + dot_nt(hot, place)
    zsend[...] = table.reshape(nz, PLANE, 128).astype(BF16)
    zm[z] = zsend[z]
    m_z = [
        remote(zsend.at[p], zm.at[z], ms_z.at[i], mr_z.at[i], {"req": p * PLANE + yc}) for i, p in enumerate(zpeers)
    ]
    start_all(m_z)

    wait_all(q_z)
    q_y = [
        remote(zq, qall_ref.at[yc], qs_y.at[i], qr_y.at[i], {"req": z * PLANE + 2 * p + core})
        for i, p in enumerate(ypeers)
    ]
    q_c = [remote(zq, qall_ref.at[yc], qs_c.at[3], qr_c.at[3], {"req": z * PLANE + sib})]
    start_all(q_y + q_c)
    qall_ref[yc] = zq[...]

    wait_all(m_z)
    got = zm[...].astype(F32)
    for d in range(PLANE):
        ysend[d] = jnp.concatenate([got[i, d : d + 1, :] for i in range(nz)], axis=0).astype(BF16)
    mall[yc] = ysend[yc]
    m_y = [
        remote(ysend.at[p], mall.at[yc], ms_y.at[i], mr_y.at[i], {"req": z * PLANE + p}) for i, p in enumerate(plane)
    ]
    start_all(m_y)
    wait_all(m_y)
    sort_items(nz * PLANE, npages, mall[...].reshape(nz * PLANE, 128), lists_ref, items_ref, slots_ref)
    for i, p in enumerate((2, 3, 1)):
        q_y[i].wait()
        slot = (y + p) % 4 * 2 + core
        c = remote(qall_ref.at[slot], qall_ref.at[slot], qs_c.at[i], qr_c.at[i], {"req": z * PLANE + sib})
        c.start()
        q_c.append(c)
    wait_all(q_c)


def owner_kernel(
    nz, qall_ref, lists_ref, items_ref, sg_s, pool_hbm, po_ref, ps_ref,
    pool, qx, o_s, ml_s, wn_s, s0, s1, p0, p1, lst, sems,
):
    nsrc = nz * PLANE
    lst_copy = pltpu.make_async_copy(lists_ref, lst, sems.at[0])
    lst_copy.start()
    pool_copy = pltpu.make_async_copy(pool_hbm, pool, sems.at[1])
    pool_copy.start()
    row8, lane8 = iota((8, 128), 0), iota((8, 128), 1)
    low, left = row8 < 4, lane8 < 64
    live, slot = items_ref[0:8], items_ref[8:16]

    keep = jnp.where(left, 0.125, 0.0)
    group = 8

    @pl.loop(0, nsrc // group)
    def _(g):
        for u in range(group):
            i = g * group + u
            q = qall_ref[i // nz, i % nz].astype(F32)
            for t in range(2):
                v = q[8 * t : 8 * t + 8]
                vs = pltpu.roll(v, 4, 0)
                qx[i * SLOTS + 2 * t] = jnp.where(low, v, pltpu.roll(vs, 64, 1)) * keep
                qx[i * SLOTS + 2 * t + 1] = jnp.where(low, vs, pltpu.roll(v, 64, 1)) * keep

    lst_copy.wait()
    pool_copy.wait()

    def scores_of(c, out):
        c = jnp.clip(c, 0, 127)
        q = jnp.concatenate([qx[lst[k, c]] for k in range(CHUNK)], axis=0).astype(BF16)
        out[...] = dot_nt(q, pool[lst[48, c]])

    def probs_of(c, scores, out):
        c = jnp.clip(c, 0, 127)
        pair = []
        for k in range(CHUNK):
            sc = jnp.where(lane8 < lst[32 + k, c], scores[8 * k : 8 * k + 8], NEG)
            top = jnp.max(sc, axis=1, keepdims=True)
            pr = jnp.exp(sc - top)
            ml_s[lst[16 + k, c]] = jnp.where(left, top, jnp.sum(pr, axis=1, keepdims=True))
            pair.append(pr)
            if k % 2:
                out[8 * k - 8 : 8 * k + 8] = jnp.concatenate(pair, axis=0).astype(BF16)
                pair = []

    def values_of(c, probs):
        c = jnp.clip(c, 0, 127)
        out = dot_nn(probs[...], pool[lst[48, c]])
        for k in range(CHUNK):
            o_s[lst[16 + k, c]] = out[8 * k : 8 * k + 8]

    @pl.loop(0, (lst[49, 0] + 3) // 2)
    def _(step):
        c = 2 * step
        scores_of(c, s0)
        probs_of(c - 1, s1, p1)
        values_of(c - 2, p0)
        scores_of(c + 1, s1)
        probs_of(c, s0, p0)
        values_of(c - 1, p1)

    halves = []
    for h in range(2):

        def gather(g, accs, h=h):
            accs = list(accs)
            for u in range(8):
                i = g * 8 + u
                mask = lane8 % 64 == i
                for r in range(CAP):
                    accs[r] = jnp.where(mask, ml_s[(h * 64 + i) * CAP + r], accs[r])
            return tuple(accs)

        halves.append(lax.fori_loop(0, 8, gather, tuple(jnp.zeros((8, 128), F32) for _ in range(CAP))))
    mine = [[jnp.logical_and(live[r : r + 1] > 0.0, slot[r : r + 1] == float(s)) for s in range(SLOTS)] for r in range(CAP)]
    ms = [jnp.where(left, halves[0][r], pltpu.roll(halves[1][r], 64, 1)) for r in range(CAP)]
    ls = [jnp.where(left, pltpu.roll(halves[0][r], 64, 1), halves[1][r]) for r in range(CAP)]
    tops, dens = [], []
    for s in range(SLOTS):
        top = jnp.full((8, 128), NEG, F32)
        for r in range(CAP):
            top = jnp.maximum(top, jnp.where(mine[r][s], ms[r], NEG))
        tops.append(top)
    es = []
    for r in range(CAP):
        top = ms[r]
        for s in range(SLOTS):
            top = jnp.where(mine[r][s], tops[s], top)
        es.append(jnp.exp(ms[r] - top))
    lses, invs = [], []
    for s in range(SLOTS):
        den = jnp.zeros((8, 128), F32)
        for r in range(CAP):
            den = den + jnp.where(mine[r][s], es[r] * ls[r], 0.0)
        some = den > 0.0
        den = jnp.where(some, den, 1.0)
        invs.append(1.0 / den)
        lses.append(jnp.where(some, tops[s] + jnp.log(den), NEG))
    for r in range(CAP):
        w = jnp.zeros((8, 128), F32)
        for s in range(SLOTS):
            w = jnp.where(mine[r][s], es[r] * invs[s], w)
        wn_s[r] = w
    for d in range(PLANE):
        stat = jnp.full((8, 128), NEG, F32)
        for s in range(SLOTS):
            shift = (nz * (s - d)) % 128
            moved = pltpu.roll(lses[s], shift, 1) if shift else lses[s]
            stat = jnp.where(lane8 // nz == s, moved, stat)
        ps_ref[d] = stat

    ar, al = iota((64, 128), 0), iota((64, 128), 1)
    same = jnp.logical_and(ar // 32 == al // 64, ar // 16 % 2 * 4 + ar % 4 == al % 8)
    want = jnp.where(same, ar // 4 % 4, -1).astype(F32)
    left16 = iota((16, 128), 1) < 64

    @pl.loop(0, PLANE)
    def _(d):
        ws = [pltpu.roll(wn_s[r], (128 - nz * d) % 128, 1) for r in range(CAP)]
        for j in range(nz // 2):
            scaled = []
            for a in range(2):
                for r in range(CAP):
                    w = jnp.broadcast_to(ws[r][:, 2 * j + a : 2 * j + a + 1], (8, 128))
                    o = o_s[(d * nz + 2 * j + a) * CAP + r]
                    scaled.append(jnp.where(w > 0.0, o * w, 0.0))
            i = d * nz + 2 * j
            sg = jnp.where(lane8[0:1] < 64, sg_s[pl.ds(i, 1), :], sg_s[pl.ds(i + 1, 1), :])
            pickm = jnp.where(want == sg, 1.0, 0.0).astype(BF16)
            res = dot_nn(pickm, jnp.concatenate(scaled, axis=0).astype(BF16))
            for a in range(2):
                even, odd = res[32 * a : 32 * a + 16], res[32 * a + 16 : 32 * a + 32]
                po_ref[d, 2 * j + a] = jnp.where(left16, pltpu.roll(even, 64, 1), odd).astype(BF16)


def spread_weights(x, nz):
    low = iota((8, 128), 0) < 4
    xs = pltpu.roll(x, 4, 0)
    yl = jnp.where(low, x, pltpu.roll(xs, 128 - nz, 1))
    yr = jnp.where(low, xs, pltpu.roll(x, 128 - nz, 1))
    return yl, yr


def return_kernel(
    nz, ntp, po_ref, ps_ref, q_hbm, fresh_hbm, w_hbm, resid_hbm, gain_hbm, res_out, norm_out,
    q_ref, fresh_ref, wv, resid_ref, gain_ref, rc, rsc, ysnd, ystat, ry, rsy, o1, s1, ro2, rs2, parts,
    in_sem, os_c, or_c, ss_c, sr_c, os_y, or_y, ss_y, sr_y, os_z, or_z, ss_z, sr_z, ts, tr,
):
    me, tp = lax.axis_index("req"), lax.axis_index("tp")
    z, yc = me // PLANE, me % PLANE
    y, core = yc // 2, yc % 2
    sib = yc + 1 - 2 * core
    zpeers = [(z + k) % nz for k in far_first(nz)]
    yorder = [(y + k) % 4 for k in (2, 1, 3, 0)]
    tpeers = [(tp + k) % ntp for k in range(1, ntp)]
    barrier = pltpu.get_barrier_semaphore()
    pl.semaphore_signal(barrier, inc=1, device_id={"req": z * PLANE + sib}, device_id_type=MESH)
    for p in yorder[:3]:
        pl.semaphore_signal(barrier, inc=1, device_id={"req": z * PLANE + 2 * p + core}, device_id_type=MESH)
    for p in zpeers:
        pl.semaphore_signal(barrier, inc=1, device_id={"req": p * PLANE + yc}, device_id_type=MESH)
    for p in tpeers:
        pl.semaphore_signal(barrier, inc=1, device_id={"tp": p}, device_id_type=MESH)
    ins = [
        pltpu.make_async_copy(h, v, in_sem.at[i])
        for i, (h, v) in enumerate(
            [(q_hbm, q_ref), (fresh_hbm, fresh_ref), (w_hbm, wv), (resid_hbm, resid_ref), (gain_hbm, gain_ref)]
        )
    ]
    start_all(ins)
    pl.semaphore_wait(barrier, nz - 1 + 4 + ntp - 1)

    cores = []
    for i, p in enumerate(yorder):
        to = {"req": z * PLANE + sib}
        theirs = 2 * p + 1 - core
        cores.append(
            [
                remote(ps_ref.at[theirs], rsc.at[i], ss_c.at[i], sr_c.at[i], to),
                remote(po_ref.at[theirs], rc.at[i], os_c.at[i], or_c.at[i], to),
            ]
        )
        start_all(cores[-1])

    row8, lane8 = iota((8, 128), 0), iota((8, 128), 1)
    low, left = row8 < 4, lane8 < 64
    wait_all(ins[:2])
    q16 = head_pair_rows(q_ref[...].astype(F32))
    fresh = fresh_ref[...].astype(F32)
    self_score, self_value = [], []
    for t in range(2):
        kv = jnp.concatenate([fresh[2 * t : 2 * t + 1]] * 4 + [fresh[2 * t + 1 : 2 * t + 2]] * 4, axis=0)
        other = pltpu.roll(kv, 64, 1)
        prod = q16[8 * t : 8 * t + 8] * jnp.where(left, kv, other)
        ls = jnp.sum(jnp.where(left, prod, 0.0), axis=1, keepdims=True)
        rsum = jnp.sum(jnp.where(left, 0.0, prod), axis=1, keepdims=True)
        self_score.append(jnp.where(left, ls, rsum) * 0.125)
        self_value.append(jnp.where(left, other, kv))

    ys = []
    for i, p in enumerate(yorder):
        wait_all(cores[i])
        ours = 2 * p + core
        sa, sb = ps_ref[ours], rsc[i]
        top = jnp.maximum(sa, sb)
        ea, eb = jnp.exp(sa - top), jnp.exp(sb - top)
        both = ea + eb
        ystat[i] = top + jnp.log(both)
        yl, yr = spread_weights(ea / both, nz)
        for zi in range(nz):
            halves = []
            pa, pb = po_ref[ours, zi].astype(F32), rc[i, zi].astype(F32)
            for t in range(2):
                li = 2 * t * nz + zi
                w = jnp.where(left, yl[:, li : li + 1], yr[:, li : li + 1])
                b = pb[8 * t : 8 * t + 8]
                halves.append(b + w * (pa[8 * t : 8 * t + 8] - b))
            ysnd[i, zi] = jnp.concatenate(halves, axis=0).astype(BF16)
        if i < 3:
            to = {"req": z * PLANE + 2 * p + core}
            ys.append(remote(ystat.at[i], rsy.at[i], ss_y.at[i], sr_y.at[i], to))
            ys.append(remote(ysnd.at[i], ry.at[i], os_y.at[i], or_y.at[i], to))
            start_all(ys[-2:])
    wait_all(ys)

    stats = [rsy[p] for p in range(3)] + [ystat[3]]
    top = stats[0]
    for p in range(1, 4):
        top = jnp.maximum(top, stats[p])
    ws = [jnp.exp(s - top) for s in stats]
    wsum = ws[0]
    for p in range(1, 4):
        wsum = wsum + ws[p]
    lse = top + jnp.log(wsum)
    sides = [spread_weights(w / wsum, nz) for w in ws]
    for zi in range(nz):
        pieces = [ry[p, zi].astype(F32) for p in range(3)] + [ysnd[3, zi].astype(F32)]
        halves = []
        for t in range(2):
            li = 2 * t * nz + zi
            total = jnp.zeros((8, 128), F32)
            for p in range(4):
                yl, yr = sides[p]
                w = jnp.where(left, yl[:, li : li + 1], yr[:, li : li + 1])
                total = total + w * pieces[p][8 * t : 8 * t + 8]
            halves.append(total)
        o1[zi] = jnp.concatenate(halves, axis=0).astype(BF16)
    by_slot = [pltpu.roll(lse, (128 - nz * s) % 128, 1) if s else lse for s in range(SLOTS)]
    rows = jnp.concatenate(by_slot + [jnp.zeros((96, 128), F32)], axis=0).T
    for zi in range(nz):
        s1[zi] = rows[zi : zi + 1]
    ro2[z] = o1[z]
    rs2[z] = s1[z]
    copies = []
    for i, p in enumerate(zpeers):
        to = {"req": p * PLANE + yc}
        copies.append(remote(o1.at[p], ro2.at[z], os_z.at[i], or_z.at[i], to))
        copies.append(remote(s1.at[p], rs2.at[z], ss_z.at[i], sr_z.at[i], to))
    for c in copies:
        c.start()
    for c in copies:
        c.wait()

    st = jnp.concatenate([rs2[zi] for zi in range(nz)], axis=0)
    top = jnp.max(st, axis=0, keepdims=True)
    cols = jnp.concatenate(
        [jnp.exp(st - top), jnp.broadcast_to(top, (8, 128)), jnp.zeros((120 - nz, 128), F32)], axis=0
    ).T
    att = []
    for t in range(2):
        x0, x1 = cols[16 * t : 16 * t + 8], cols[16 * t + 8 : 16 * t + 16]
        yl = jnp.where(low, x0, pltpu.roll(x1, 4, 0))
        yr = jnp.where(low, pltpu.roll(x0, 4, 0), x1)
        num = jnp.zeros((8, 128), F32)
        den = jnp.zeros((8, 128), F32)
        for zi in range(nz):
            w = jnp.where(left, yl[:, zi : zi + 1], yr[:, zi : zi + 1])
            num = num + w * ro2[zi, 8 * t : 8 * t + 8].astype(F32)
            den = den + w
        topm = jnp.where(left, yl[:, nz : nz + 1], yr[:, nz : nz + 1])
        best = jnp.maximum(topm, self_score[t])
        a, b = jnp.exp(topm - best), jnp.exp(self_score[t] - best)
        att.append((a * num + b * self_value[t]) / (a * den + b))
    att = jnp.concatenate(att, axis=0)
    r16 = iota((16, 128), 0)
    wide = jnp.concatenate([jnp.where(r16 % 4 == h, att, 0.0) for h in range(4)], axis=1).astype(BF16)
    sel = jnp.where(iota((16, 16), 1) // 4 == iota((16, 16), 0), 1.0, 0.0).astype(BF16)
    lhs = dot_nn(sel, wide).astype(BF16)
    wait_all(ins[2:])
    parts[tp] = dot_nn(lhs, wv[...])[0:SLOTS]
    copies = []
    for i, p in enumerate(tpeers):
        copies.append(remote(parts.at[tp], parts.at[tp], ts.at[i], tr.at[i], {"tp": p}))
    for c in copies:
        c.start()
    for c in copies:
        c.wait()
    stream = parts[0]
    for p in range(1, ntp):
        stream = stream + parts[p]
    stream = resid_ref[...].astype(F32) + stream
    mean = jnp.mean(stream * stream, axis=1, keepdims=True)
    res_out[...] = stream.astype(BF16)
    norm_out[...] = (stream * lax.rsqrt(mean + 1e-5) * gain_ref[...].astype(F32)).astype(BF16)


def vmem(n):
    return [pl.BlockSpec(memory_space=pltpu.VMEM)] * n


def in_hbm(x):
    return pltpu.with_memory_space_constraint(x, pltpu.HBM)


def hbm(n):
    return [pl.BlockSpec(memory_space=pltpu.HBM)] * n


def owner_call(nz, qall, lists, items, slots, pool):
    nsrc = nz * PLANE
    return pl.pallas_call(
        functools.partial(owner_kernel, nz),
        out_shape=(
            jax.ShapeDtypeStruct((PLANE, nz, 16, 128), BF16),
            jax.ShapeDtypeStruct((PLANE, 8, 128), F32),
        ),
        in_specs=vmem(4) + hbm(1),
        out_specs=tuple(vmem(2)),
        scratch_shapes=[
            VM(pool.shape, BF16),
            VM((nsrc * SLOTS, 8, 128), F32),
            VM((nsrc * CAP + 1, 8, 128), F32), VM((nsrc * CAP + 1, 8, 128), F32),
            VM((CAP, 8, 128), F32),
            VM((128, 128), F32), VM((128, 128), F32), VM((128, 128), BF16), VM((128, 128), BF16),
            pltpu.SMEM((56, 128), I32),
            pltpu.SemaphoreType.DMA((2,)),
        ],
        compiler_params=pltpu.CompilerParams(vmem_limit_bytes=24 << 20),
        name="owner",
    )(qall, lists, items, slots, in_hbm(pool))


def dispatch_call(nz, npages, queries, block_owner, block_page, lengths):
    DMA = pltpu.SemaphoreType.DMA
    return pl.pallas_call(
        functools.partial(dispatch_kernel, nz, npages),
        out_shape=(
            jax.ShapeDtypeStruct((PLANE, nz, 16, 128), BF16),
            jax.ShapeDtypeStruct((56, 128), I32),
            jax.ShapeDtypeStruct((16, 128), F32),
            jax.ShapeDtypeStruct((nz * PLANE, 128), F32),
        ),
        in_specs=hbm(4),
        out_specs=tuple(vmem(4)),
        scratch_shapes=[
            VM(queries.shape, BF16), VM((SLOTS, 128), I32), VM((SLOTS, 128), I32), pltpu.SMEM((SLOTS,), I32),
            VM((nz, 16, 128), BF16), VM((nz, PLANE, 128), BF16), VM((nz, PLANE, 128), BF16),
            VM((PLANE, nz, 128), BF16), VM((PLANE, nz, 128), BF16),
        ]
        + [DMA((4,))] + [DMA((nz - 1,))] * 4 + [DMA((3,))] * 2 + [DMA((4,))] * 2 + [DMA((PLANE - 1,))] * 2,
        compiler_params=pltpu.CompilerParams(
            collective_id=0, has_side_effects=True, vmem_limit_bytes=6 << 20
        ),
        name="dispatch",
    )(*map(in_hbm, (queries, block_owner.reshape(SLOTS, 128), block_page.reshape(SLOTS, 128), lengths)))


def return_call(nz, ntp, po, ps, queries, fresh_key_value, o_weight, resid_in, norm_gain):
    width = o_weight.shape[1]
    DMA = pltpu.SemaphoreType.DMA
    block = (nz, 16, 128)
    return pl.pallas_call(
        functools.partial(return_kernel, nz, ntp),
        out_shape=(
            jax.ShapeDtypeStruct((SLOTS, width), BF16),
            jax.ShapeDtypeStruct((SLOTS, width), BF16),
        ),
        in_specs=vmem(2) + hbm(5),
        out_specs=tuple(vmem(2)),
        scratch_shapes=[
            VM(queries.shape, BF16), VM(fresh_key_value.shape, BF16), VM(o_weight.shape, BF16),
            VM(resid_in.shape, BF16), VM((1, width), BF16),
            VM((4,) + block, BF16), VM((4, 8, 128), F32), VM((4,) + block, BF16), VM((4, 8, 128), F32),
            VM((3,) + block, BF16), VM((3, 8, 128), F32),
            VM(block, BF16), VM((nz, 1, 128), F32), VM(block, BF16), VM((nz, 1, 128), F32),
            VM((ntp, SLOTS, width), F32),
        ]
        + [DMA((5,))] + [DMA((4,))] * 4 + [DMA((3,))] * 4 + [DMA((nz - 1,))] * 4 + [DMA((ntp - 1,))] * 2,
        compiler_params=pltpu.CompilerParams(
            collective_id=1, has_side_effects=True, vmem_limit_bytes=12 << 20
        ),
        name="give_back",
    )(po, ps, *map(in_hbm, (queries, fresh_key_value, o_weight, resid_in, norm_gain.reshape(1, width))))


def body(nz, ntp, queries, fresh_key_value, pool, block_owner, block_page, lengths, o_weight, resid_in, norm_gain):
    qall, lists, items, slots = dispatch_call(nz, pool.shape[0], queries, block_owner, block_page, lengths)
    po, ps = owner_call(nz, qall, lists, items, slots, pool)
    return return_call(nz, ntp, po, ps, queries, fresh_key_value, o_weight, resid_in, norm_gain)


def solution(mesh):
    nz, ntp = mesh.shape["req"] // PLANE, mesh.shape["tp"]
    placed = (
        P("req", "tp"), P("req", "tp"), P("req", None, "tp"), P("req", None), P("req"), P("req"),
        P("tp", None), P("req", None), P(),
    )
    return jax.shard_map(
        functools.partial(body, nz, ntp),
        mesh=mesh,
        in_specs=placed,
        out_specs=(P("req", None), P("req", None)),
        check_vma=False,
    )
```

```python
import functools

import jax
import jax.numpy as jnp
from jax import lax
from jax.experimental import pallas as pl
from jax.experimental.pallas import tpu as pltpu
from jax.sharding import PartitionSpec as P

F32, BF16, I32 = jnp.float32, jnp.bfloat16, jnp.int32
MESH = pl.DeviceIdType.MESH
NEG = -1e30
CAP = 8
CHUNK = 16
UNROLL = 4
COLUMNS = 128
SLOTS = 4
PLANE = 8
VM = pltpu.VMEM


def iota(shape, dim):
    return lax.broadcasted_iota(I32, shape, dim)


def dot_nt(a, b):
    return lax.dot_general(a, b, (((1,), (1,)), ((), ())), preferred_element_type=F32)


def dot_nn(a, b):
    return jnp.dot(a, b, preferred_element_type=F32)


def head_pair_rows(q):
    return jnp.concatenate([q[s : s + 1, 128 * h : 128 * h + 128] for s in range(SLOTS) for h in range(4)], axis=0)


def remote(src, dst, send, recv, peer):
    return pltpu.make_async_remote_copy(
        src_ref=src, dst_ref=dst, send_sem=send, recv_sem=recv, device_id=peer, device_id_type=MESH
    )


def start_all(copies):
    for c in copies:
        c.start()


def wait_all(copies):
    for c in copies:
        c.wait()


def far_first(n):
    return sorted(range(1, n), key=lambda k: -min(k, n - k))


def sort_items(nsrc, npages, meta_b, lists_ref, items_ref, slots_ref):
    meta = meta_b.astype(F32).T
    page, live, slot = meta[0:8], meta[8:16], meta[16:24]
    items_ref[0:8] = live
    items_ref[8:16] = slot
    prow = iota((npages, 128), 0).astype(F32)
    eqs = [
        jnp.where(jnp.logical_and(prow == page[r : r + 1], live[r : r + 1] > 0.0), 1.0, 0.0) for r in range(CAP)
    ]
    upto = jnp.where(iota((128, 256), 0) <= iota((128, 256), 1), 1.0, 0.0).astype(BF16)
    counts = dot_nn(jnp.concatenate(eqs, axis=0).astype(BF16), upto)
    run = jnp.zeros((npages, 128), F32)
    ranks = []
    for r in range(CAP):
        part = counts[npages * r : npages * r + npages]
        ranks.append(run + part[:, 0:128])
        run = run + part[:, 128:256]
    chunks = jnp.floor((run + (CHUNK - 1)) * (1.0 / CHUNK))
    below = jnp.where(iota((npages, npages), 1) < iota((npages, npages), 0), 1.0, 0.0).astype(BF16)
    first = dot_nn(below, chunks.astype(BF16))
    total = (first + chunks)[npages - 1 : npages]

    krow = iota((CHUNK, 128), 0).astype(F32)
    crow = iota((COLUMNS, 128), 0).astype(F32)
    src = iota((1, 128), 1).astype(F32)
    lists = jnp.zeros((5 * CHUNK, COLUMNS), F32)
    for r in range(CAP):
        row = slice(r, r + 1)
        pos = jnp.sum(eqs[r] * (first * CHUNK + ranks[r] - 1.0), axis=0, keepdims=True)
        chunk = jnp.floor(pos * (1.0 / CHUNK))
        here = jnp.logical_and(krow == pos - chunk * CHUNK, live[row] > 0.0)
        pick = [jnp.where(here, v, 0.0) for v in (src, float(r + 1), live[row], slot[row], page[row])]
        col = jnp.where(crow == chunk, 1.0, 0.0)
        lists = lists + dot_nt(jnp.concatenate(pick, axis=0).astype(BF16), col.astype(BF16))
    srcs, nth = lists[0:CHUNK], lists[CHUNK : 2 * CHUNK]
    lists_ref[0:CHUNK] = (srcs * SLOTS + lists[3 * CHUNK : 4 * CHUNK]).astype(I32)
    lists_ref[CHUNK : 2 * CHUNK] = jnp.where(nth > 0.0, srcs * CAP + nth - 1.0, float(nsrc * CAP)).astype(I32)
    lists_ref[2 * CHUNK : 3 * CHUNK] = lists[2 * CHUNK : 3 * CHUNK].astype(I32)
    lists_ref[3 * CHUNK : 3 * CHUNK + 8] = jnp.concatenate(
        [lists[4 * CHUNK : 4 * CHUNK + 1], jnp.tile(total, (1, COLUMNS // 128)), jnp.zeros((6, COLUMNS), F32)], axis=0
    ).astype(I32)
    spread = jnp.where(iota((128, 128), 0) == 2 * CAP + iota((128, 128), 1) // 8 % CAP, 1.0, 0.0).astype(BF16)
    slots_ref[...] = dot_nn(meta_b, spread)


def dispatch_kernel(
    nz, npages, q_hbm, owner_hbm, page_hbm, len_hbm, qall_ref, lists_ref, items_ref, slots_ref,
    q_v, owner_v, page_v, len_s, zq, zsend, zm, ysend, mall,
    in_sem, qs_z, qr_z, ms_z, mr_z, qs_y, qr_y, qs_c, qr_c, ms_y, mr_y,
):
    me = lax.axis_index("req")
    z, yc = me // PLANE, me % PLANE
    y, core = yc // 2, yc % 2
    sib = yc + 1 - 2 * core
    zpeers = [(z + k) % nz for k in far_first(nz)]
    plane = [(yc + k) % PLANE for k in range(1, PLANE)]
    ypeers = [(y + k) % 4 for k in (2, 1, 3)]
    barrier = pltpu.get_barrier_semaphore()
    for p in zpeers:
        pl.semaphore_signal(barrier, inc=1, device_id={"req": p * PLANE + yc}, device_id_type=MESH)
    for p in plane:
        pl.semaphore_signal(barrier, inc=1, device_id={"req": z * PLANE + p}, device_id_type=MESH)
    ins = [
        pltpu.make_async_copy(h, v, in_sem.at[i])
        for i, (h, v) in enumerate([(q_hbm, q_v), (owner_hbm, owner_v), (page_hbm, page_v), (len_hbm, len_s)])
    ]
    start_all(ins)
    ins[0].wait()
    zq[z] = head_pair_rows(q_v[...].astype(F32)).astype(BF16)
    pl.semaphore_wait(barrier, nz - 1 + PLANE - 1)
    q_z = [
        remote(zq.at[z], zq.at[z], qs_z.at[i], qr_z.at[i], {"req": p * PLANE + yc}) for i, p in enumerate(zpeers)
    ]
    start_all(q_z)

    wait_all(ins[1:])
    rows, lanes = iota((128, 128), 0), iota((128, 128), 1)
    tri = jnp.where(rows <= lanes, 1.0, 0.0).astype(BF16)
    ones = jnp.ones((128, 128), BF16)
    base = jnp.zeros((128, 128), F32)
    table = jnp.zeros((128, 128), F32)
    for s in range(SLOTS):
        live = jnp.clip(len_s[s] - iota((1, 128), 1) * 128, 0, 128)
        hit = jnp.logical_and(rows == owner_v[s : s + 1, :], live > 0)
        hot = jnp.where(hit, 1.0, 0.0).astype(BF16)
        rank = jnp.sum(jnp.where(hit, base + dot_nn(hot, tri) - 1.0, 0.0), axis=0, keepdims=True)
        base = base + dot_nn(hot, ones)
        kind = rows // CAP
        val = jnp.where(
            kind == 0, page_v[s : s + 1, :].astype(F32),
            jnp.where(kind == 1, live.astype(F32), jnp.where(kind == 2, float(s), 0.0)),
        )
        place = jnp.where((rows % CAP).astype(F32) == rank, val, 0.0).astype(BF16)
        table = table + dot_nt(hot, place)
    zsend[...] = table.reshape(nz, PLANE, 128).astype(BF16)
    zm[z] = zsend[z]
    m_z = [
        remote(zsend.at[p], zm.at[z], ms_z.at[i], mr_z.at[i], {"req": p * PLANE + yc}) for i, p in enumerate(zpeers)
    ]
    start_all(m_z)

    wait_all(q_z)
    q_y = [
        remote(zq, qall_ref.at[yc], qs_y.at[i], qr_y.at[i], {"req": z * PLANE + 2 * p + core})
        for i, p in enumerate(ypeers)
    ]
    q_c = [remote(zq, qall_ref.at[yc], qs_c.at[3], qr_c.at[3], {"req": z * PLANE + sib})]
    start_all(q_y + q_c)
    qall_ref[yc] = zq[...]

    wait_all(m_z)
    got = zm[...].astype(F32)
    for d in range(PLANE):
        ysend[d] = jnp.concatenate([got[i, d : d + 1, :] for i in range(nz)], axis=0).astype(BF16)
    mall[yc] = ysend[yc]
    m_y = [
        remote(ysend.at[p], mall.at[yc], ms_y.at[i], mr_y.at[i], {"req": z * PLANE + p}) for i, p in enumerate(plane)
    ]
    start_all(m_y)
    wait_all(m_y)
    sort_items(nz * PLANE, npages, mall[...].reshape(nz * PLANE, 128), lists_ref, items_ref, slots_ref)
    for i, p in enumerate((2, 3, 1)):
        q_y[i].wait()
        slot = (y + p) % 4 * 2 + core
        c = remote(qall_ref.at[slot], qall_ref.at[slot], qs_c.at[i], qr_c.at[i], {"req": z * PLANE + sib})
        c.start()
        q_c.append(c)
    wait_all(q_c)


def owner_kernel(
    nz, qall_ref, lists_ref, items_ref, sg_s, pool_hbm, po_ref, ps_ref,
    pool, qx, o_s, ml_s, wn_s, s0, p0, lst, sems,
):
    nsrc = nz * PLANE
    lst_copy = pltpu.make_async_copy(lists_ref, lst, sems.at[0])
    lst_copy.start()
    pool_copy = pltpu.make_async_copy(pool_hbm, pool, sems.at[1])
    pool_copy.start()
    row8, lane8 = iota((8, 128), 0), iota((8, 128), 1)
    low, left = row8 < 4, lane8 < 64
    live, slot = items_ref[0:8], items_ref[8:16]

    keep = jnp.where(left, 0.125, 0.0)
    group = 8

    @pl.loop(0, nsrc // group)
    def _(g):
        for u in range(group):
            i = g * group + u
            q = qall_ref[i // nz, i % nz].astype(F32)
            for r in range(CAP):
                o_s[i * CAP + r] = jnp.zeros((8, 128), F32)
            for t in range(2):
                v = q[8 * t : 8 * t + 8]
                vs = pltpu.roll(v, 4, 0)
                qx[i * SLOTS + 2 * t] = jnp.where(low, v, pltpu.roll(vs, 64, 1)) * keep
                qx[i * SLOTS + 2 * t + 1] = jnp.where(low, vs, pltpu.roll(v, 64, 1)) * keep

    lst_copy.wait()
    pool_copy.wait()

    def scores_of(c, out):
        c = jnp.clip(c, 0, COLUMNS - 1)
        q = jnp.concatenate([qx[lst[k, c]] for k in range(CHUNK)], axis=0).astype(BF16)
        out[...] = dot_nt(q, pool[lst[3 * CHUNK, c]])

    def probs_of(c, scores, out):
        c = jnp.clip(c, 0, COLUMNS - 1)
        pair = []
        for k in range(CHUNK):
            sc = jnp.where(lane8 < lst[2 * CHUNK + k, c], scores[8 * k : 8 * k + 8], NEG)
            top = jnp.max(sc, axis=1, keepdims=True)
            pr = jnp.exp(sc - top)
            ml_s[lst[CHUNK + k, c]] = jnp.where(left, top, jnp.sum(pr, axis=1, keepdims=True))
            pair.append(pr)
            if k % 2:
                out[8 * k - 8 : 8 * k + 8] = jnp.concatenate(pair, axis=0).astype(BF16)
                pair = []

    def values_of(c, probs):
        c = jnp.clip(c, 0, COLUMNS - 1)
        out = dot_nn(probs[...], pool[lst[3 * CHUNK, c]])
        for k in range(CHUNK):
            o_s[lst[CHUNK + k, c]] = out[8 * k : 8 * k + 8]

    @pl.loop(0, (lst[3 * CHUNK + 1, 0] + UNROLL - 1) // UNROLL + 2)
    def _(step):
        c = step * UNROLL
        for u in range(UNROLL):
            values_of(c - 2 * UNROLL + u, p0.at[u])
        for u in range(UNROLL):
            probs_of(c - UNROLL + u, s0.at[u], p0.at[u])
        for u in range(UNROLL):
            scores_of(c + u, s0.at[u])

    halves = []
    for h in range(2):

        def gather(g, accs, h=h):
            accs = list(accs)
            for u in range(8):
                i = g * 8 + u
                mask = lane8 % 64 == i
                for r in range(CAP):
                    accs[r] = jnp.where(mask, ml_s[(h * 64 + i) * CAP + r], accs[r])
            return tuple(accs)

        halves.append(lax.fori_loop(0, 8, gather, tuple(jnp.zeros((8, 128), F32) for _ in range(CAP))))
    mine = [[jnp.logical_and(live[r : r + 1] > 0.0, slot[r : r + 1] == float(s)) for s in range(SLOTS)] for r in range(CAP)]
    ms = [jnp.where(left, halves[0][r], pltpu.roll(halves[1][r], 64, 1)) for r in range(CAP)]
    ls = [jnp.where(left, pltpu.roll(halves[0][r], 64, 1), halves[1][r]) for r in range(CAP)]
    tops, dens = [], []
    for s in range(SLOTS):
        top = jnp.full((8, 128), NEG, F32)
        for r in range(CAP):
            top = jnp.maximum(top, jnp.where(mine[r][s], ms[r], NEG))
        tops.append(top)
    es = []
    for r in range(CAP):
        top = ms[r]
        for s in range(SLOTS):
            top = jnp.where(mine[r][s], tops[s], top)
        es.append(jnp.exp(ms[r] - top))
    lses, invs = [], []
    for s in range(SLOTS):
        den = jnp.zeros((8, 128), F32)
        for r in range(CAP):
            den = den + jnp.where(mine[r][s], es[r] * ls[r], 0.0)
        some = den > 0.0
        den = jnp.where(some, den, 1.0)
        invs.append(1.0 / den)
        lses.append(jnp.where(some, tops[s] + jnp.log(den), NEG))
    weights = []
    for r in range(CAP):
        w = jnp.zeros((8, 128), F32)
        for s in range(SLOTS):
            w = jnp.where(mine[r][s], es[r] * invs[s], w)
        weights.append(w)
    wide = jnp.concatenate(weights + weights, axis=0).T
    high = wide.astype(BF16).astype(F32)
    left128 = iota((nsrc, 128), 1) < 64

    def pairs(x):
        return jnp.where(left128, x, pltpu.roll(x, nsrc - 1, 0))

    wn_s[0] = pairs(high)
    wn_s[1] = pairs(wide - high)
    wn_s[2] = pairs(sg_s[...])
    for d in range(PLANE):
        stat = jnp.full((8, 128), NEG, F32)
        for s in range(SLOTS):
            shift = (nz * (s - d)) % 128
            moved = pltpu.roll(lses[s], shift, 1) if shift else lses[s]
            stat = jnp.where(lane8 // nz == s, moved, stat)
        ps_ref[d] = stat

    ar, al = iota((64, 128), 0), iota((64, 128), 1)
    same = jnp.logical_and(ar // 32 == al // 64, ar // 16 % 2 * 4 + ar % 4 == al % 8)
    want = jnp.where(same, ar // 4 % 4, -1).astype(F32)
    left16 = iota((16, 128), 1) < 64

    @pl.loop(0, PLANE)
    def _(d):
        for j in range(nz // 2):
            i = d * nz + 2 * j
            o = jnp.concatenate([o_s[i * CAP + k] for k in range(2 * CAP)], axis=0).astype(BF16)
            hit = want == wn_s[2, pl.ds(i, 1), :]
            pick = [jnp.where(hit, wn_s[k, pl.ds(i, 1), :], 0.0) for k in range(2)]
            res = dot_nn(jnp.concatenate(pick, axis=0).astype(BF16), o)
            res = res[0:64] + res[64:128]
            for a in range(2):
                even, odd = res[32 * a : 32 * a + 16], res[32 * a + 16 : 32 * a + 32]
                po_ref[d, 2 * j + a] = jnp.where(left16, pltpu.roll(even, 64, 1), odd).astype(BF16)


def spread_weights(x, nz):
    low = iota((8, 128), 0) < 4
    xs = pltpu.roll(x, 4, 0)
    yl = jnp.where(low, x, pltpu.roll(xs, 128 - nz, 1))
    yr = jnp.where(low, xs, pltpu.roll(x, 128 - nz, 1))
    return yl, yr


def return_kernel(
    nz, ntp, po_ref, ps_ref, q_hbm, fresh_hbm, w_hbm, resid_hbm, res_out, norm_out,
    q_ref, fresh_ref, wv, resid_ref, rc, rsc, ysnd, ystat, ry, rsy, o1, s1, ro2, rs2, parts,
    in_sem, os_c, or_c, ss_c, sr_c, os_y, or_y, ss_y, sr_y, os_z, or_z, ss_z, sr_z, ts, tr,
):
    me, tp = lax.axis_index("req"), lax.axis_index("tp")
    z, yc = me // PLANE, me % PLANE
    y, core = yc // 2, yc % 2
    sib = yc + 1 - 2 * core
    zpeers = [(z + k) % nz for k in far_first(nz)]
    yorder = [(y + k) % 4 for k in (2, 1, 3, 0)]
    tpeers = [(tp + k) % ntp for k in range(1, ntp)]
    barrier = pltpu.get_barrier_semaphore()
    pl.semaphore_signal(barrier, inc=1, device_id={"req": z * PLANE + sib}, device_id_type=MESH)
    for p in yorder[:3]:
        pl.semaphore_signal(barrier, inc=1, device_id={"req": z * PLANE + 2 * p + core}, device_id_type=MESH)
    for p in zpeers:
        pl.semaphore_signal(barrier, inc=1, device_id={"req": p * PLANE + yc}, device_id_type=MESH)
    for p in tpeers:
        pl.semaphore_signal(barrier, inc=1, device_id={"tp": p}, device_id_type=MESH)
    ins = [
        pltpu.make_async_copy(h, v, in_sem.at[i])
        for i, (h, v) in enumerate(
            [(q_hbm, q_ref), (fresh_hbm, fresh_ref), (w_hbm, wv), (resid_hbm, resid_ref)]
        )
    ]
    start_all(ins)
    pl.semaphore_wait(barrier, nz - 1 + 4 + ntp - 1)

    cores = []
    for i, p in enumerate(yorder):
        to = {"req": z * PLANE + sib}
        theirs = 2 * p + 1 - core
        cores.append(
            [
                remote(ps_ref.at[theirs], rsc.at[i], ss_c.at[i], sr_c.at[i], to),
                remote(po_ref.at[theirs], rc.at[i], os_c.at[i], or_c.at[i], to),
            ]
        )
        start_all(cores[-1])

    row8, lane8 = iota((8, 128), 0), iota((8, 128), 1)
    low, left = row8 < 4, lane8 < 64
    wait_all(ins[:2])
    q16 = head_pair_rows(q_ref[...].astype(F32))
    fresh = fresh_ref[...].astype(F32)
    self_score, self_value = [], []
    for t in range(2):
        kv = jnp.concatenate([fresh[2 * t : 2 * t + 1]] * 4 + [fresh[2 * t + 1 : 2 * t + 2]] * 4, axis=0)
        other = pltpu.roll(kv, 64, 1)
        prod = q16[8 * t : 8 * t + 8] * jnp.where(left, kv, other)
        ls = jnp.sum(jnp.where(left, prod, 0.0), axis=1, keepdims=True)
        rsum = jnp.sum(jnp.where(left, 0.0, prod), axis=1, keepdims=True)
        self_score.append(jnp.where(left, ls, rsum) * 0.125)
        self_value.append(jnp.where(left, other, kv))

    ys = []
    for i, p in enumerate(yorder):
        wait_all(cores[i])
        ours = 2 * p + core
        sa, sb = ps_ref[ours], rsc[i]
        top = jnp.maximum(sa, sb)
        ea, eb = jnp.exp(sa - top), jnp.exp(sb - top)
        both = ea + eb
        ystat[i] = top + jnp.log(both)
        yl, yr = spread_weights(ea / both, nz)
        for zi in range(nz):
            halves = []
            pa, pb = po_ref[ours, zi].astype(F32), rc[i, zi].astype(F32)
            for t in range(2):
                li = 2 * t * nz + zi
                w = jnp.where(left, yl[:, li : li + 1], yr[:, li : li + 1])
                b = pb[8 * t : 8 * t + 8]
                halves.append(b + w * (pa[8 * t : 8 * t + 8] - b))
            ysnd[i, zi] = jnp.concatenate(halves, axis=0).astype(BF16)
        if i < 3:
            to = {"req": z * PLANE + 2 * p + core}
            ys.append(remote(ystat.at[i], rsy.at[i], ss_y.at[i], sr_y.at[i], to))
            ys.append(remote(ysnd.at[i], ry.at[i], os_y.at[i], or_y.at[i], to))
            start_all(ys[-2:])
    wait_all(ys)

    stats = [rsy[p] for p in range(3)] + [ystat[3]]
    top = stats[0]
    for p in range(1, 4):
        top = jnp.maximum(top, stats[p])
    ws = [jnp.exp(s - top) for s in stats]
    wsum = ws[0]
    for p in range(1, 4):
        wsum = wsum + ws[p]
    lse = top + jnp.log(wsum)
    sides = [spread_weights(w / wsum, nz) for w in ws]
    for zi in range(nz):
        pieces = [ry[p, zi].astype(F32) for p in range(3)] + [ysnd[3, zi].astype(F32)]
        halves = []
        for t in range(2):
            li = 2 * t * nz + zi
            total = jnp.zeros((8, 128), F32)
            for p in range(4):
                yl, yr = sides[p]
                w = jnp.where(left, yl[:, li : li + 1], yr[:, li : li + 1])
                total = total + w * pieces[p][8 * t : 8 * t + 8]
            halves.append(total)
        o1[zi] = jnp.concatenate(halves, axis=0).astype(BF16)
    by_slot = [pltpu.roll(lse, (128 - nz * s) % 128, 1) if s else lse for s in range(SLOTS)]
    rows = jnp.concatenate(by_slot + [jnp.zeros((96, 128), F32)], axis=0).T
    for zi in range(nz):
        s1[zi] = rows[zi : zi + 1]
    ro2[z] = o1[z]
    rs2[z] = s1[z]
    copies = []
    for i, p in enumerate(zpeers):
        to = {"req": p * PLANE + yc}
        copies.append(remote(o1.at[p], ro2.at[z], os_z.at[i], or_z.at[i], to))
        copies.append(remote(s1.at[p], rs2.at[z], ss_z.at[i], sr_z.at[i], to))
    for c in copies:
        c.start()
    for c in copies:
        c.wait()

    st = jnp.concatenate([rs2[zi] for zi in range(nz)], axis=0)
    top = jnp.max(st, axis=0, keepdims=True)
    cols = jnp.concatenate(
        [jnp.exp(st - top), jnp.broadcast_to(top, (8, 128)), jnp.zeros((120 - nz, 128), F32)], axis=0
    ).T
    att = []
    for t in range(2):
        x0, x1 = cols[16 * t : 16 * t + 8], cols[16 * t + 8 : 16 * t + 16]
        yl = jnp.where(low, x0, pltpu.roll(x1, 4, 0))
        yr = jnp.where(low, pltpu.roll(x0, 4, 0), x1)
        num = jnp.zeros((8, 128), F32)
        den = jnp.zeros((8, 128), F32)
        for zi in range(nz):
            w = jnp.where(left, yl[:, zi : zi + 1], yr[:, zi : zi + 1])
            num = num + w * ro2[zi, 8 * t : 8 * t + 8].astype(F32)
            den = den + w
        topm = jnp.where(left, yl[:, nz : nz + 1], yr[:, nz : nz + 1])
        best = jnp.maximum(topm, self_score[t])
        a, b = jnp.exp(topm - best), jnp.exp(self_score[t] - best)
        att.append((a * num + b * self_value[t]) / (a * den + b))
    att = jnp.concatenate(att, axis=0)
    r16 = iota((16, 128), 0)
    wide = jnp.concatenate([jnp.where(r16 % 4 == h, att, 0.0) for h in range(4)], axis=1).astype(BF16)
    sel = jnp.where(iota((16, 16), 1) // 4 == iota((16, 16), 0), 1.0, 0.0).astype(BF16)
    lhs = dot_nn(sel, wide).astype(BF16)
    wait_all(ins[2:])
    parts[tp] = dot_nn(lhs, wv[...])[0:SLOTS]
    copies = []
    for i, p in enumerate(tpeers):
        copies.append(remote(parts.at[tp], parts.at[tp], ts.at[i], tr.at[i], {"tp": p}))
    for c in copies:
        c.start()
    for c in copies:
        c.wait()
    stream = parts[0]
    for p in range(1, ntp):
        stream = stream + parts[p]
    stream = resid_ref[...].astype(F32) + stream
    mean = jnp.mean(stream * stream, axis=1, keepdims=True)
    res_out[...] = stream
    norm_out[...] = stream * lax.rsqrt(mean + 1e-5)


def vmem(n):
    return [pl.BlockSpec(memory_space=pltpu.VMEM)] * n


def in_hbm(x):
    return pltpu.with_memory_space_constraint(x, pltpu.HBM)


def hbm(n):
    return [pl.BlockSpec(memory_space=pltpu.HBM)] * n


def owner_call(nz, qall, lists, items, slots, pool):
    nsrc = nz * PLANE
    return pl.pallas_call(
        functools.partial(owner_kernel, nz),
        out_shape=(
            jax.ShapeDtypeStruct((PLANE, nz, 16, 128), BF16),
            jax.ShapeDtypeStruct((PLANE, 8, 128), F32),
        ),
        in_specs=vmem(4) + hbm(1),
        out_specs=tuple(vmem(2)),
        scratch_shapes=[
            VM(pool.shape, BF16),
            VM((nsrc * SLOTS, 8, 128), F32),
            VM((nsrc * CAP + 1, 8, 128), F32), VM((nsrc * CAP + 1, 8, 128), F32),
            VM((3, nsrc, 128), F32),
            VM((UNROLL, 8 * CHUNK, 128), F32), VM((UNROLL, 8 * CHUNK, 128), BF16),
            pltpu.SMEM((3 * CHUNK + 8, COLUMNS), I32),
            pltpu.SemaphoreType.DMA((2,)),
        ],
        compiler_params=pltpu.CompilerParams(vmem_limit_bytes=24 << 20),
        name="owner",
    )(qall, lists, items, slots, in_hbm(pool))


def dispatch_call(nz, npages, queries, block_owner, block_page, lengths):
    DMA = pltpu.SemaphoreType.DMA
    return pl.pallas_call(
        functools.partial(dispatch_kernel, nz, npages),
        out_shape=(
            jax.ShapeDtypeStruct((PLANE, nz, 16, 128), BF16),
            jax.ShapeDtypeStruct((3 * CHUNK + 8, COLUMNS), I32),
            jax.ShapeDtypeStruct((16, 128), F32),
            jax.ShapeDtypeStruct((nz * PLANE, 128), F32),
        ),
        in_specs=hbm(4),
        out_specs=tuple(vmem(4)),
        scratch_shapes=[
            VM(queries.shape, BF16), VM((SLOTS, 128), I32), VM((SLOTS, 128), I32), pltpu.SMEM((SLOTS,), I32),
            VM((nz, 16, 128), BF16), VM((nz, PLANE, 128), BF16), VM((nz, PLANE, 128), BF16),
            VM((PLANE, nz, 128), BF16), VM((PLANE, nz, 128), BF16),
        ]
        + [DMA((4,))] + [DMA((nz - 1,))] * 4 + [DMA((3,))] * 2 + [DMA((4,))] * 2 + [DMA((PLANE - 1,))] * 2,
        compiler_params=pltpu.CompilerParams(
            collective_id=0, has_side_effects=True, vmem_limit_bytes=6 << 20
        ),
        name="dispatch",
    )(*map(in_hbm, (queries, block_owner.reshape(SLOTS, 128), block_page.reshape(SLOTS, 128), lengths)))


def return_call(nz, ntp, po, ps, queries, fresh_key_value, o_weight, resid_in, norm_gain):
    width = o_weight.shape[1]
    DMA = pltpu.SemaphoreType.DMA
    block = (nz, 16, 128)
    stream, scaled = pl.pallas_call(
        functools.partial(return_kernel, nz, ntp),
        out_shape=(
            jax.ShapeDtypeStruct((SLOTS, width), F32),
            jax.ShapeDtypeStruct((SLOTS, width), F32),
        ),
        in_specs=vmem(2) + hbm(4),
        out_specs=tuple(vmem(2)),
        scratch_shapes=[
            VM(queries.shape, BF16), VM(fresh_key_value.shape, BF16), VM(o_weight.shape, BF16),
            VM(resid_in.shape, BF16),
            VM((4,) + block, BF16), VM((4, 8, 128), F32), VM((4,) + block, BF16), VM((4, 8, 128), F32),
            VM((3,) + block, BF16), VM((3, 8, 128), F32),
            VM(block, BF16), VM((nz, 1, 128), F32), VM(block, BF16), VM((nz, 1, 128), F32),
            VM((ntp, SLOTS, width), F32),
        ]
        + [DMA((4,))] + [DMA((4,))] * 4 + [DMA((3,))] * 4 + [DMA((nz - 1,))] * 4 + [DMA((ntp - 1,))] * 2,
        compiler_params=pltpu.CompilerParams(
            collective_id=1, has_side_effects=True, vmem_limit_bytes=12 << 20
        ),
        name="give_back",
    )(po, ps, *map(in_hbm, (queries, fresh_key_value, o_weight, resid_in)))
    return stream.astype(BF16), (scaled * norm_gain.astype(F32)).astype(BF16)


def body(nz, ntp, queries, fresh_key_value, pool, block_owner, block_page, lengths, o_weight, resid_in, norm_gain):
    qall, lists, items, slots = dispatch_call(nz, pool.shape[0], queries, block_owner, block_page, lengths)
    po, ps = owner_call(nz, qall, lists, items, slots, pool)
    return return_call(nz, ntp, po, ps, queries, fresh_key_value, o_weight, resid_in, norm_gain)


def solution(mesh):
    nz, ntp = mesh.shape["req"] // PLANE, mesh.shape["tp"]
    placed = (
        P("req", "tp"), P("req", "tp"), P("req", None, "tp"), P("req", None), P("req"), P("req"),
        P("tp", None), P("req", None), P(),
    )
    return jax.shard_map(
        functools.partial(body, nz, ntp),
        mesh=mesh,
        in_specs=placed,
        out_specs=(P("req", None), P("req", None)),
        check_vma=False,
    )
```

```python
import functools

import jax
import jax.numpy as jnp
from jax import lax
from jax.experimental import pallas as pl
from jax.experimental.pallas import tpu as pltpu
from jax.sharding import PartitionSpec as P

F32, BF16, I32 = jnp.float32, jnp.bfloat16, jnp.int32
MESH = pl.DeviceIdType.MESH
NEG = -1e30
CAP = 8
CHUNK = 16
UNROLL = 4
COLUMNS = 128
SLOTS = 4
PLANE = 8
VM = pltpu.VMEM


def iota(shape, dim):
    return lax.broadcasted_iota(I32, shape, dim)


def dot_nt(a, b):
    return lax.dot_general(a, b, (((1,), (1,)), ((), ())), preferred_element_type=F32)


def dot_nn(a, b):
    return jnp.dot(a, b, preferred_element_type=F32)


def head_pair_rows(q):
    return jnp.concatenate([q[s : s + 1, 128 * h : 128 * h + 128] for s in range(SLOTS) for h in range(4)], axis=0)


def remote(src, dst, send, recv, peer):
    return pltpu.make_async_remote_copy(
        src_ref=src, dst_ref=dst, send_sem=send, recv_sem=recv, device_id=peer, device_id_type=MESH
    )


def start_all(copies):
    for c in copies:
        c.start()


def wait_all(copies):
    for c in copies:
        c.wait()


def far_first(n):
    return sorted(range(1, n), key=lambda k: -min(k, n - k))


def sort_items(nsrc, npages, meta_b, lists_ref, items_ref, slots_ref):
    meta = meta_b.astype(F32).T
    page, live, slot = meta[0:8], meta[8:16], meta[16:24]
    items_ref[0:8] = live
    items_ref[8:16] = slot
    prow = iota((npages, 128), 0).astype(F32)
    eqs = [
        jnp.where(jnp.logical_and(prow == page[r : r + 1], live[r : r + 1] > 0.0), 1.0, 0.0) for r in range(CAP)
    ]
    upto = jnp.where(iota((128, 256), 0) <= iota((128, 256), 1), 1.0, 0.0).astype(BF16)
    counts = dot_nn(jnp.concatenate(eqs, axis=0).astype(BF16), upto)
    run = jnp.zeros((npages, 128), F32)
    ranks = []
    for r in range(CAP):
        part = counts[npages * r : npages * r + npages]
        ranks.append(run + part[:, 0:128])
        run = run + part[:, 128:256]
    chunks = jnp.floor((run + (CHUNK - 1)) * (1.0 / CHUNK))
    below = jnp.where(iota((npages, npages), 1) < iota((npages, npages), 0), 1.0, 0.0).astype(BF16)
    first = dot_nn(below, chunks.astype(BF16))
    total = (first + chunks)[npages - 1 : npages]

    krow = iota((CHUNK, 128), 0).astype(F32)
    crow = iota((COLUMNS, 128), 0).astype(F32)
    src = iota((1, 128), 1).astype(F32)
    lists = jnp.zeros((5 * CHUNK, COLUMNS), F32)
    for r in range(CAP):
        row = slice(r, r + 1)
        pos = jnp.sum(eqs[r] * (first * CHUNK + ranks[r] - 1.0), axis=0, keepdims=True)
        chunk = jnp.floor(pos * (1.0 / CHUNK))
        here = jnp.logical_and(krow == pos - chunk * CHUNK, live[row] > 0.0)
        pick = [jnp.where(here, v, 0.0) for v in (src, float(r + 1), live[row], slot[row], page[row])]
        col = jnp.where(crow == chunk, 1.0, 0.0)
        lists = lists + dot_nt(jnp.concatenate(pick, axis=0).astype(BF16), col.astype(BF16))
    srcs, nth = lists[0:CHUNK], lists[CHUNK : 2 * CHUNK]
    lists_ref[0:CHUNK] = (srcs * SLOTS + lists[3 * CHUNK : 4 * CHUNK]).astype(I32)
    lists_ref[CHUNK : 2 * CHUNK] = jnp.where(nth > 0.0, srcs * CAP + nth - 1.0, float(nsrc * CAP)).astype(I32)
    lists_ref[2 * CHUNK : 3 * CHUNK] = lists[2 * CHUNK : 3 * CHUNK].astype(I32)
    lists_ref[3 * CHUNK : 3 * CHUNK + 8] = jnp.concatenate(
        [lists[4 * CHUNK : 4 * CHUNK + 1], jnp.tile(total, (1, COLUMNS // 128)), jnp.zeros((6, COLUMNS), F32)], axis=0
    ).astype(I32)
    spread = jnp.where(iota((128, 128), 0) == 2 * CAP + iota((128, 128), 1) // 8 % CAP, 1.0, 0.0).astype(BF16)
    slots_ref[...] = dot_nn(meta_b, spread)


def dispatch_kernel(
    nz, npages, q_hbm, owner_hbm, page_hbm, len_hbm, qall_ref, lists_ref, items_ref, slots_ref,
    q_v, owner_v, page_v, len_s, zq, zsend, zm, ysend, mall,
    in_sem, qs_z, qr_z, ms_z, mr_z, qs_y, qr_y, qs_c, qr_c, ms_y, mr_y,
):
    me = lax.axis_index("req")
    z, yc = me // PLANE, me % PLANE
    y, core = yc // 2, yc % 2
    sib = yc + 1 - 2 * core
    zpeers = [(z + k) % nz for k in far_first(nz)]
    plane = [(yc + k) % PLANE for k in range(1, PLANE)]
    ypeers = [(y + k) % 4 for k in (2, 1, 3)]
    barrier = pltpu.get_barrier_semaphore()
    for p in zpeers:
        pl.semaphore_signal(barrier, inc=1, device_id={"req": p * PLANE + yc}, device_id_type=MESH)
    for p in plane:
        pl.semaphore_signal(barrier, inc=1, device_id={"req": z * PLANE + p}, device_id_type=MESH)
    ins = [
        pltpu.make_async_copy(h, v, in_sem.at[i])
        for i, (h, v) in enumerate([(q_hbm, q_v), (owner_hbm, owner_v), (page_hbm, page_v), (len_hbm, len_s)])
    ]
    start_all(ins)
    ins[0].wait()
    zq[z % 2, z // 2] = head_pair_rows(q_v[...].astype(F32)).astype(BF16)
    pl.semaphore_wait(barrier, nz - 1 + PLANE - 1)
    mine = zq.at[z % 2, z // 2]
    q_z = [
        [
            remote(mine, mine, qs_z.at[k - 1], qr_z.at[k - 1], {"req": (z + k) % nz * PLANE + yc})
            for k in far_first(nz)
            if k % 2 == h
        ]
        for h in range(2)
    ]
    start_all(q_z[0] + q_z[1])

    wait_all(ins[1:])
    rows, lanes = iota((128, 128), 0), iota((128, 128), 1)
    tri = jnp.where(rows <= lanes, 1.0, 0.0).astype(BF16)
    ones = jnp.ones((128, 128), BF16)
    base = jnp.zeros((128, 128), F32)
    table = jnp.zeros((32, 128), F32)
    for s in range(SLOTS):
        live = jnp.clip(len_s[s] - iota((1, 128), 1) * 128, 0, 128)
        hit = jnp.logical_and(rows == owner_v[s : s + 1, :], live > 0)
        hot = jnp.where(hit, 1.0, 0.0).astype(BF16)
        rank = jnp.sum(jnp.where(hit, base + dot_nn(hot, tri) - 1.0, 0.0), axis=0, keepdims=True)
        base = base + dot_nn(hot, ones)
        kind = rows % 32 // CAP
        quarter = rows // 32 == owner_v[s : s + 1, :] % 4
        val = jnp.where(
            kind == 0, page_v[s : s + 1, :].astype(F32),
            jnp.where(kind == 1, live.astype(F32), jnp.where(kind == 2, float(s), 0.0)),
        )
        place = jnp.where(jnp.logical_and(quarter, (rows % CAP).astype(F32) == rank), val, 0.0).astype(BF16)
        four = jnp.logical_and(rows[0:32] == owner_v[s : s + 1, :] // 4, live > 0)
        table = table + dot_nt(jnp.where(four, 1.0, 0.0).astype(BF16), place)
    for i in range(nz):
        zsend[i] = table[2 * i : 2 * i + 2].astype(BF16)
    zm[z] = zsend[z]
    m_z = [
        remote(zsend.at[p], zm.at[z], ms_z.at[i], mr_z.at[i], {"req": p * PLANE + yc}) for i, p in enumerate(zpeers)
    ]
    start_all(m_z)

    q_y, q_c = [], []
    for h in range(2):
        wait_all(q_z[h])
        part = (z + h) % 2
        for i, p in enumerate(ypeers):
            to = {"req": z * PLANE + 2 * p + core}
            q_y.append(remote(zq.at[part], qall_ref.at[yc, part], qs_y.at[3 * h + i], qr_y.at[3 * h + i], to))
        q_c.append(
            remote(zq.at[part], qall_ref.at[yc, part], qs_c.at[6 + h], qr_c.at[6 + h], {"req": z * PLANE + sib})
        )
        start_all(q_y[-3:] + q_c[-1:])
    qall_ref[yc] = zq[...]

    wait_all(m_z)
    got = [zm[i].astype(F32) for i in range(nz)]
    for d in range(PLANE):
        half = jnp.concatenate([g[d // 4 : d // 4 + 1, :] for g in got], axis=0)
        if d % 4:
            half = pltpu.roll(half, 128 - 32 * (d % 4), 1)
        ysend[d] = half.astype(BF16)
    mall[yc] = ysend[yc]
    m_y = [
        remote(ysend.at[p], mall.at[yc], ms_y.at[i], mr_y.at[i], {"req": z * PLANE + p}) for i, p in enumerate(plane)
    ]
    start_all(m_y)
    wait_all(m_y)
    sort_items(nz * PLANE, npages, mall[...].reshape(nz * PLANE, 128), lists_ref, items_ref, slots_ref)
    for h in range(2):
        for i, p in enumerate((2, 3, 1)):
            q_y[3 * h + i].wait()
            here = qall_ref.at[(y + p) % 4 * 2 + core, (z + h) % 2]
            c = remote(here, here, qs_c.at[3 * h + i], qr_c.at[3 * h + i], {"req": z * PLANE + sib})
            c.start()
            q_c.append(c)
    wait_all(q_c)


def owner_kernel(
    nz, qall_ref, lists_ref, items_ref, sg_s, pool_hbm, po_ref, ps_ref,
    pool, qx, o_s, ml_s, wn_s, s0, p0, lst, sems,
):
    nsrc = nz * PLANE
    lst_copy = pltpu.make_async_copy(lists_ref, lst, sems.at[0])
    lst_copy.start()
    pool_copy = pltpu.make_async_copy(pool_hbm, pool, sems.at[1])
    pool_copy.start()
    row8, lane8 = iota((8, 128), 0), iota((8, 128), 1)
    low, left = row8 < 4, lane8 < 64
    live, slot = items_ref[0:8], items_ref[8:16]

    keep = jnp.where(left, 0.125, 0.0)
    group = 8

    @pl.loop(0, nsrc // group)
    def _(g):
        for u in range(group):
            i = g * group + u
            q = qall_ref[i // nz, i % 2, i % nz // 2].astype(F32)
            for r in range(CAP):
                o_s[i * CAP + r] = jnp.zeros((8, 128), F32)
            for t in range(2):
                v = q[8 * t : 8 * t + 8]
                vs = pltpu.roll(v, 4, 0)
                qx[i * SLOTS + 2 * t] = jnp.where(low, v, pltpu.roll(vs, 64, 1)) * keep
                qx[i * SLOTS + 2 * t + 1] = jnp.where(low, vs, pltpu.roll(v, 64, 1)) * keep

    lst_copy.wait()
    pool_copy.wait()

    def scores_of(c, out):
        c = jnp.clip(c, 0, COLUMNS - 1)
        q = jnp.concatenate([qx[lst[k, c]] for k in range(CHUNK)], axis=0).astype(BF16)
        out[...] = dot_nt(q, pool[lst[3 * CHUNK, c]])

    def probs_of(c, scores, out):
        c = jnp.clip(c, 0, COLUMNS - 1)
        pair = []
        for k in range(CHUNK):
            sc = jnp.where(lane8 < lst[2 * CHUNK + k, c], scores[8 * k : 8 * k + 8], NEG)
            top = jnp.max(sc, axis=1, keepdims=True)
            pr = jnp.exp(sc - top)
            ml_s[lst[CHUNK + k, c]] = jnp.where(left, top, jnp.sum(pr, axis=1, keepdims=True))
            pair.append(pr)
            if k % 2:
                out[8 * k - 8 : 8 * k + 8] = jnp.concatenate(pair, axis=0).astype(BF16)
                pair = []

    def values_of(c, probs):
        c = jnp.clip(c, 0, COLUMNS - 1)
        out = dot_nn(probs[...], pool[lst[3 * CHUNK, c]])
        for k in range(CHUNK):
            o_s[lst[CHUNK + k, c]] = out[8 * k : 8 * k + 8]

    @pl.loop(0, (lst[3 * CHUNK + 1, 0] + UNROLL - 1) // UNROLL + 2)
    def _(step):
        c = step * UNROLL
        for u in range(UNROLL):
            values_of(c - 2 * UNROLL + u, p0.at[u])
        for u in range(UNROLL):
            probs_of(c - UNROLL + u, s0.at[u], p0.at[u])
        for u in range(UNROLL):
            scores_of(c + u, s0.at[u])

    halves = []
    for h in range(2):

        def gather(g, accs, h=h):
            accs = list(accs)
            for u in range(8):
                i = g * 8 + u
                mask = lane8 % 64 == i
                for r in range(CAP):
                    accs[r] = jnp.where(mask, ml_s[(h * 64 + i) * CAP + r], accs[r])
            return tuple(accs)

        halves.append(lax.fori_loop(0, 8, gather, tuple(jnp.zeros((8, 128), F32) for _ in range(CAP))))
    mine = [[jnp.logical_and(live[r : r + 1] > 0.0, slot[r : r + 1] == float(s)) for s in range(SLOTS)] for r in range(CAP)]
    ms = [jnp.where(left, halves[0][r], pltpu.roll(halves[1][r], 64, 1)) for r in range(CAP)]
    ls = [jnp.where(left, pltpu.roll(halves[0][r], 64, 1), halves[1][r]) for r in range(CAP)]
    tops, dens = [], []
    for s in range(SLOTS):
        top = jnp.full((8, 128), NEG, F32)
        for r in range(CAP):
            top = jnp.maximum(top, jnp.where(mine[r][s], ms[r], NEG))
        tops.append(top)
    es = []
    for r in range(CAP):
        top = ms[r]
        for s in range(SLOTS):
            top = jnp.where(mine[r][s], tops[s], top)
        es.append(jnp.exp(ms[r] - top))
    lses, invs = [], []
    for s in range(SLOTS):
        den = jnp.zeros((8, 128), F32)
        for r in range(CAP):
            den = den + jnp.where(mine[r][s], es[r] * ls[r], 0.0)
        some = den > 0.0
        den = jnp.where(some, den, 1.0)
        invs.append(1.0 / den)
        lses.append(jnp.where(some, tops[s] + jnp.log(den), NEG))
    weights = []
    for r in range(CAP):
        w = jnp.zeros((8, 128), F32)
        for s in range(SLOTS):
            w = jnp.where(mine[r][s], es[r] * invs[s], w)
        weights.append(w)
    wide = jnp.concatenate(weights + weights, axis=0).T
    high = wide.astype(BF16).astype(F32)
    left128 = iota((nsrc, 128), 1) < 64

    def pairs(x):
        return jnp.where(left128, x, pltpu.roll(x, nsrc - 1, 0))

    wn_s[0] = pairs(high)
    wn_s[1] = pairs(wide - high)
    wn_s[2] = pairs(sg_s[...])
    for d in range(PLANE):
        stat = jnp.full((8, 128), NEG, F32)
        for s in range(SLOTS):
            shift = (nz * (s - d)) % 128
            moved = pltpu.roll(lses[s], shift, 1) if shift else lses[s]
            stat = jnp.where(lane8 // nz == s, moved, stat)
        ps_ref[d] = stat

    ar, al = iota((64, 128), 0), iota((64, 128), 1)
    same = jnp.logical_and(ar // 32 == al // 64, ar // 16 % 2 * 4 + ar % 4 == al % 8)
    want = jnp.where(same, ar // 4 % 4, -1).astype(F32)
    left16 = iota((16, 128), 1) < 64

    @pl.loop(0, PLANE)
    def _(d):
        for j in range(nz // 2):
            i = d * nz + 2 * j
            o = jnp.concatenate([o_s[i * CAP + k] for k in range(2 * CAP)], axis=0).astype(BF16)
            hit = want == wn_s[2, pl.ds(i, 1), :]
            pick = [jnp.where(hit, wn_s[k, pl.ds(i, 1), :], 0.0) for k in range(2)]
            res = dot_nn(jnp.concatenate(pick, axis=0).astype(BF16), o)
            res = res[0:64] + res[64:128]
            for a in range(2):
                even, odd = res[32 * a : 32 * a + 16], res[32 * a + 16 : 32 * a + 32]
                po_ref[d, 2 * j + a] = jnp.where(left16, pltpu.roll(even, 64, 1), odd).astype(BF16)


def spread_weights(x, nz):
    low = iota((8, 128), 0) < 4
    xs = pltpu.roll(x, 4, 0)
    yl = jnp.where(low, x, pltpu.roll(xs, 128 - nz, 1))
    yr = jnp.where(low, xs, pltpu.roll(x, 128 - nz, 1))
    return yl, yr


def return_kernel(
    nz, ntp, po_ref, ps_ref, q_hbm, fresh_hbm, w_hbm, resid_hbm, res_out, norm_out,
    q_ref, fresh_ref, wv, resid_ref, rc, rsc, ysnd, ystat, ry, rsy, o1, s1, ro2, rs2, parts,
    in_sem, os_c, or_c, ss_c, sr_c, os_y, or_y, ss_y, sr_y, os_z, or_z, ss_z, sr_z, ts, tr,
):
    me, tp = lax.axis_index("req"), lax.axis_index("tp")
    z, yc = me // PLANE, me % PLANE
    y, core = yc // 2, yc % 2
    sib = yc + 1 - 2 * core
    zpeers = [(z + k) % nz for k in far_first(nz)]
    yorder = [(y + k) % 4 for k in (2, 1, 3, 0)]
    tpeers = [(tp + k) % ntp for k in range(1, ntp)]
    barrier = pltpu.get_barrier_semaphore()
    pl.semaphore_signal(barrier, inc=1, device_id={"req": z * PLANE + sib}, device_id_type=MESH)
    for p in yorder[:3]:
        pl.semaphore_signal(barrier, inc=1, device_id={"req": z * PLANE + 2 * p + core}, device_id_type=MESH)
    for p in zpeers:
        pl.semaphore_signal(barrier, inc=1, device_id={"req": p * PLANE + yc}, device_id_type=MESH)
    for p in tpeers:
        pl.semaphore_signal(barrier, inc=1, device_id={"tp": p}, device_id_type=MESH)
    ins = [
        pltpu.make_async_copy(h, v, in_sem.at[i])
        for i, (h, v) in enumerate(
            [(q_hbm, q_ref), (fresh_hbm, fresh_ref), (w_hbm, wv), (resid_hbm, resid_ref)]
        )
    ]
    start_all(ins)
    pl.semaphore_wait(barrier, nz - 1 + 4 + ntp - 1)

    cores = []
    for i, p in enumerate(yorder):
        to = {"req": z * PLANE + sib}
        theirs = 2 * p + 1 - core
        cores.append(
            [
                remote(ps_ref.at[theirs], rsc.at[i], ss_c.at[i], sr_c.at[i], to),
                remote(po_ref.at[theirs], rc.at[i], os_c.at[i], or_c.at[i], to),
            ]
        )
        start_all(cores[-1])

    row8, lane8 = iota((8, 128), 0), iota((8, 128), 1)
    low, left = row8 < 4, lane8 < 64
    wait_all(ins[:2])
    q16 = head_pair_rows(q_ref[...].astype(F32))
    fresh = fresh_ref[...].astype(F32)
    self_score, self_value = [], []
    for t in range(2):
        kv = jnp.concatenate([fresh[2 * t : 2 * t + 1]] * 4 + [fresh[2 * t + 1 : 2 * t + 2]] * 4, axis=0)
        other = pltpu.roll(kv, 64, 1)
        prod = q16[8 * t : 8 * t + 8] * jnp.where(left, kv, other)
        ls = jnp.sum(jnp.where(left, prod, 0.0), axis=1, keepdims=True)
        rsum = jnp.sum(jnp.where(left, 0.0, prod), axis=1, keepdims=True)
        self_score.append(jnp.where(left, ls, rsum) * 0.125)
        self_value.append(jnp.where(left, other, kv))

    def from_here(x):
        ahead = pltpu.roll(x, (128 - z) % 128, 1)
        behind = pltpu.roll(x, nz - z, 1)
        return jnp.where(lane8 % nz + z < nz, ahead, behind)

    ys = [[], []]
    sides, stats = [], []
    for h in range(2):
        for i, p in enumerate(yorder):
            ours = 2 * p + core
            if h == 0:
                wait_all(cores[i])
                sa, sb = ps_ref[ours], rsc[i]
                top = jnp.maximum(sa, sb)
                ea, eb = jnp.exp(sa - top), jnp.exp(sb - top)
                both = ea + eb
                ystat[i] = from_here(top + jnp.log(both))
                sides.append(spread_weights(from_here(ea / both), nz))
            yl, yr = sides[i]
            for j in range(nz // 2):
                k = 2 * j + h
                halves = []
                zi = (z + k) % nz
                pa, pb = po_ref[ours, zi].astype(F32), rc[i, zi].astype(F32)
                for t in range(2):
                    li = 2 * t * nz + k
                    w = jnp.where(left, yl[:, li : li + 1], yr[:, li : li + 1])
                    b = pb[8 * t : 8 * t + 8]
                    halves.append(b + w * (pa[8 * t : 8 * t + 8] - b))
                ysnd[i, h, j] = jnp.concatenate(halves, axis=0).astype(BF16)
            if i < 3:
                to = {"req": z * PLANE + 2 * p + core}
                if h == 0:
                    ys[h].append(remote(ystat.at[i], rsy.at[i], ss_y.at[i], sr_y.at[i], to))
                    ys[h][-1].start()
                ys[h].append(
                    remote(ysnd.at[i, h], ry.at[i, h], os_y.at[3 * h + i], or_y.at[3 * h + i], to)
                )
                ys[h][-1].start()

    zs = []
    for h in range(2):
        wait_all(ys[h])
        if h == 0:
            stats = [rsy[p] for p in range(3)] + [ystat[3]]
            top = stats[0]
            for p in range(1, 4):
                top = jnp.maximum(top, stats[p])
            ws = [jnp.exp(s - top) for s in stats]
            wsum = ws[0]
            for p in range(1, 4):
                wsum = wsum + ws[p]
            lse = top + jnp.log(wsum)
            sides = [spread_weights(w / wsum, nz) for w in ws]
            by_slot = [pltpu.roll(lse, (128 - nz * s) % 128, 1) if s else lse for s in range(SLOTS)]
            rows = jnp.concatenate(by_slot + [jnp.zeros((96, 128), F32)], axis=0).T
            for k in range(nz):
                s1[k] = rows[k : k + 1]
        for j in range(nz // 2):
            k = 2 * j + h
            pieces = [ry[p, h, j].astype(F32) for p in range(3)] + [ysnd[3, h, j].astype(F32)]
            halves = []
            for t in range(2):
                li = 2 * t * nz + k
                total = jnp.zeros((8, 128), F32)
                for p in range(4):
                    yl, yr = sides[p]
                    w = jnp.where(left, yl[:, li : li + 1], yr[:, li : li + 1])
                    total = total + w * pieces[p][8 * t : 8 * t + 8]
                halves.append(total)
            o1[k] = jnp.concatenate(halves, axis=0).astype(BF16)
        for k in far_first(nz):
            if k % 2 == h:
                to = {"req": (z + k) % nz * PLANE + yc}
                zs.append(remote(s1.at[k], rs2.at[z], ss_z.at[k - 1], sr_z.at[k - 1], to))
                zs.append(remote(o1.at[k], ro2.at[z], os_z.at[k - 1], or_z.at[k - 1], to))
                start_all(zs[-2:])
    ro2[z] = o1[0]
    rs2[z] = s1[0]
    wait_all(zs)

    st = jnp.concatenate([rs2[zi] for zi in range(nz)], axis=0)
    top = jnp.max(st, axis=0, keepdims=True)
    cols = jnp.concatenate(
        [jnp.exp(st - top), jnp.broadcast_to(top, (8, 128)), jnp.zeros((120 - nz, 128), F32)], axis=0
    ).T
    att = []
    for t in range(2):
        x0, x1 = cols[16 * t : 16 * t + 8], cols[16 * t + 8 : 16 * t + 16]
        yl = jnp.where(low, x0, pltpu.roll(x1, 4, 0))
        yr = jnp.where(low, pltpu.roll(x0, 4, 0), x1)
        num = jnp.zeros((8, 128), F32)
        den = jnp.zeros((8, 128), F32)
        for zi in range(nz):
            w = jnp.where(left, yl[:, zi : zi + 1], yr[:, zi : zi + 1])
            num = num + w * ro2[zi, 8 * t : 8 * t + 8].astype(F32)
            den = den + w
        topm = jnp.where(left, yl[:, nz : nz + 1], yr[:, nz : nz + 1])
        best = jnp.maximum(topm, self_score[t])
        a, b = jnp.exp(topm - best), jnp.exp(self_score[t] - best)
        att.append((a * num + b * self_value[t]) / (a * den + b))
    att = jnp.concatenate(att, axis=0)
    r16 = iota((16, 128), 0)
    wide = jnp.concatenate([jnp.where(r16 % 4 == h, att, 0.0) for h in range(4)], axis=1).astype(BF16)
    sel = jnp.where(iota((16, 16), 1) // 4 == iota((16, 16), 0), 1.0, 0.0).astype(BF16)
    lhs = dot_nn(sel, wide).astype(BF16)
    wait_all(ins[2:])
    parts[tp] = dot_nn(lhs, wv[...])[0:SLOTS]
    copies = []
    for i, p in enumerate(tpeers):
        copies.append(remote(parts.at[tp], parts.at[tp], ts.at[i], tr.at[i], {"tp": p}))
    for c in copies:
        c.start()
    for c in copies:
        c.wait()
    stream = parts[0]
    for p in range(1, ntp):
        stream = stream + parts[p]
    stream = resid_ref[...].astype(F32) + stream
    mean = jnp.mean(stream * stream, axis=1, keepdims=True)
    res_out[...] = stream
    norm_out[...] = stream * lax.rsqrt(mean + 1e-5)


def vmem(n):
    return [pl.BlockSpec(memory_space=pltpu.VMEM)] * n


def in_hbm(x):
    return pltpu.with_memory_space_constraint(x, pltpu.HBM)


def hbm(n):
    return [pl.BlockSpec(memory_space=pltpu.HBM)] * n


def owner_call(nz, qall, lists, items, slots, pool):
    nsrc = nz * PLANE
    return pl.pallas_call(
        functools.partial(owner_kernel, nz),
        out_shape=(
            jax.ShapeDtypeStruct((PLANE, nz, 16, 128), BF16),
            jax.ShapeDtypeStruct((PLANE, 8, 128), F32),
        ),
        in_specs=vmem(4) + hbm(1),
        out_specs=tuple(vmem(2)),
        scratch_shapes=[
            VM(pool.shape, BF16),
            VM((nsrc * SLOTS, 8, 128), F32),
            VM((nsrc * CAP + 1, 8, 128), F32), VM((nsrc * CAP + 1, 8, 128), F32),
            VM((3, nsrc, 128), F32),
            VM((UNROLL, 8 * CHUNK, 128), F32), VM((UNROLL, 8 * CHUNK, 128), BF16),
            pltpu.SMEM((3 * CHUNK + 8, COLUMNS), I32),
            pltpu.SemaphoreType.DMA((2,)),
        ],
        compiler_params=pltpu.CompilerParams(vmem_limit_bytes=24 << 20),
        name="owner",
    )(qall, lists, items, slots, in_hbm(pool))


def dispatch_call(nz, npages, queries, block_owner, block_page, lengths):
    DMA = pltpu.SemaphoreType.DMA
    return pl.pallas_call(
        functools.partial(dispatch_kernel, nz, npages),
        out_shape=(
            jax.ShapeDtypeStruct((PLANE, 2, nz // 2, 16, 128), BF16),
            jax.ShapeDtypeStruct((3 * CHUNK + 8, COLUMNS), I32),
            jax.ShapeDtypeStruct((16, 128), F32),
            jax.ShapeDtypeStruct((nz * PLANE, 128), F32),
        ),
        in_specs=hbm(4),
        out_specs=tuple(vmem(4)),
        scratch_shapes=[
            VM(queries.shape, BF16), VM((SLOTS, 128), I32), VM((SLOTS, 128), I32), pltpu.SMEM((SLOTS,), I32),
            VM((2, nz // 2, 16, 128), BF16), VM((nz, 2, 128), BF16), VM((nz, 2, 128), BF16),
            VM((PLANE, nz, 128), BF16), VM((PLANE, nz, 128), BF16),
        ]
        + [DMA((4,))] + [DMA((nz - 1,))] * 4 + [DMA((6,))] * 2 + [DMA((8,))] * 2 + [DMA((PLANE - 1,))] * 2,
        compiler_params=pltpu.CompilerParams(
            collective_id=0, has_side_effects=True, vmem_limit_bytes=6 << 20
        ),
        name="dispatch",
    )(*map(in_hbm, (queries, block_owner.reshape(SLOTS, 128), block_page.reshape(SLOTS, 128), lengths)))


def return_call(nz, ntp, po, ps, queries, fresh_key_value, o_weight, resid_in, norm_gain):
    width = o_weight.shape[1]
    DMA = pltpu.SemaphoreType.DMA
    block, half = (nz, 16, 128), (2, nz // 2, 16, 128)
    stream, scaled = pl.pallas_call(
        functools.partial(return_kernel, nz, ntp),
        out_shape=(
            jax.ShapeDtypeStruct((SLOTS, width), F32),
            jax.ShapeDtypeStruct((SLOTS, width), F32),
        ),
        in_specs=vmem(2) + hbm(4),
        out_specs=tuple(vmem(2)),
        scratch_shapes=[
            VM(queries.shape, BF16), VM(fresh_key_value.shape, BF16), VM(o_weight.shape, BF16),
            VM(resid_in.shape, BF16),
            VM((4,) + block, BF16), VM((4, 8, 128), F32), VM((4,) + half, BF16), VM((4, 8, 128), F32),
            VM((3,) + half, BF16), VM((3, 8, 128), F32),
            VM(block, BF16), VM((nz, 1, 128), F32), VM(block, BF16), VM((nz, 1, 128), F32),
            VM((ntp, SLOTS, width), F32),
        ]
        + [DMA((4,))] + [DMA((4,))] * 4 + [DMA((6,))] * 2 + [DMA((3,))] * 2 + [DMA((nz - 1,))] * 4 + [DMA((ntp - 1,))] * 2,
        compiler_params=pltpu.CompilerParams(
            collective_id=1, has_side_effects=True, vmem_limit_bytes=12 << 20
        ),
        name="give_back",
    )(po, ps, *map(in_hbm, (queries, fresh_key_value, o_weight, resid_in)))
    return stream.astype(BF16), (scaled * norm_gain.astype(F32)).astype(BF16)


def body(nz, ntp, queries, fresh_key_value, pool, block_owner, block_page, lengths, o_weight, resid_in, norm_gain):
    qall, lists, items, slots = dispatch_call(nz, pool.shape[0], queries, block_owner, block_page, lengths)
    po, ps = owner_call(nz, qall, lists, items, slots, pool)
    return return_call(nz, ntp, po, ps, queries, fresh_key_value, o_weight, resid_in, norm_gain)


def solution(mesh):
    nz, ntp = mesh.shape["req"] // PLANE, mesh.shape["tp"]
    placed = (
        P("req", "tp"), P("req", "tp"), P("req", None, "tp"), P("req", None), P("req"), P("req"),
        P("tp", None), P("req", None), P(),
    )
    return jax.shard_map(
        functools.partial(body, nz, ntp),
        mesh=mesh,
        in_specs=placed,
        out_specs=(P("req", None), P("req", None)),
        check_vma=False,
    )
```

```python
import functools

import jax
import jax.numpy as jnp
from jax import lax
from jax.experimental import pallas as pl
from jax.experimental.pallas import tpu as pltpu
from jax.sharding import PartitionSpec as P

F32, BF16, I32 = jnp.float32, jnp.bfloat16, jnp.int32
MESH = pl.DeviceIdType.MESH
NEG = -1e30
CAP = 8
CHUNK = 16
UNROLL = 4
COLUMNS = 128
SLOTS = 4
PLANE = 8
VM = pltpu.VMEM


def iota(shape, dim):
    return lax.broadcasted_iota(I32, shape, dim)


def dot_nt(a, b):
    return lax.dot_general(a, b, (((1,), (1,)), ((), ())), preferred_element_type=F32)


def dot_nn(a, b):
    return jnp.dot(a, b, preferred_element_type=F32)


def head_pair_rows(q):
    return jnp.concatenate([q[s : s + 1, 128 * h : 128 * h + 128] for s in range(SLOTS) for h in range(4)], axis=0)


def remote(src, dst, send, recv, peer):
    return pltpu.make_async_remote_copy(
        src_ref=src, dst_ref=dst, send_sem=send, recv_sem=recv, device_id=peer, device_id_type=MESH
    )


def start_all(copies):
    for c in copies:
        c.start()


def wait_all(copies):
    for c in copies:
        c.wait()


def far_first(n):
    return sorted(range(1, n), key=lambda k: -min(k, n - k))


def sort_items(nsrc, npages, meta_b, lists_ref, items_ref, slots_ref):
    meta = meta_b.astype(F32).T
    page, live, slot = meta[0:8], meta[8:16], meta[16:24]
    items_ref[0:8] = live
    items_ref[8:16] = slot
    prow = iota((npages, 128), 0).astype(F32)
    eqs = [
        jnp.where(jnp.logical_and(prow == page[r : r + 1], live[r : r + 1] > 0.0), 1.0, 0.0) for r in range(CAP)
    ]
    upto = jnp.where(iota((128, 256), 0) <= iota((128, 256), 1), 1.0, 0.0).astype(BF16)
    counts = dot_nn(jnp.concatenate(eqs, axis=0).astype(BF16), upto)
    run = jnp.zeros((npages, 128), F32)
    ranks = []
    for r in range(CAP):
        part = counts[npages * r : npages * r + npages]
        ranks.append(run + part[:, 0:128])
        run = run + part[:, 128:256]
    chunks = jnp.floor((run + (CHUNK - 1)) * (1.0 / CHUNK))
    below = jnp.where(iota((npages, npages), 1) < iota((npages, npages), 0), 1.0, 0.0).astype(BF16)
    first = dot_nn(below, chunks.astype(BF16))
    total = (first + chunks)[npages - 1 : npages]

    krow = iota((CHUNK, 128), 0).astype(F32)
    crow = iota((COLUMNS, 128), 0).astype(F32)
    src = iota((1, 128), 1).astype(F32)
    lists = jnp.zeros((5 * CHUNK, COLUMNS), F32)
    for r in range(CAP):
        row = slice(r, r + 1)
        pos = jnp.sum(eqs[r] * (first * CHUNK + ranks[r] - 1.0), axis=0, keepdims=True)
        chunk = jnp.floor(pos * (1.0 / CHUNK))
        here = jnp.logical_and(krow == pos - chunk * CHUNK, live[row] > 0.0)
        pick = [jnp.where(here, v, 0.0) for v in (src, float(r + 1), live[row], slot[row], page[row])]
        col = jnp.where(crow == chunk, 1.0, 0.0)
        lists = lists + dot_nt(jnp.concatenate(pick, axis=0).astype(BF16), col.astype(BF16))
    srcs, nth = lists[0:CHUNK], lists[CHUNK : 2 * CHUNK]
    lists_ref[0:CHUNK] = (srcs * SLOTS + lists[3 * CHUNK : 4 * CHUNK]).astype(I32)
    lists_ref[CHUNK : 2 * CHUNK] = jnp.where(nth > 0.0, srcs * CAP + nth - 1.0, float(nsrc * CAP)).astype(I32)
    lists_ref[2 * CHUNK : 3 * CHUNK] = lists[2 * CHUNK : 3 * CHUNK].astype(I32)
    lists_ref[3 * CHUNK : 3 * CHUNK + 8] = jnp.concatenate(
        [lists[4 * CHUNK : 4 * CHUNK + 1], jnp.tile(total, (1, COLUMNS // 128)), jnp.zeros((6, COLUMNS), F32)], axis=0
    ).astype(I32)
    spread = jnp.where(iota((128, 128), 0) == 2 * CAP + iota((128, 128), 1) // 8 % CAP, 1.0, 0.0).astype(BF16)
    slots_ref[...] = dot_nn(meta_b, spread)


def dispatch_kernel(
    nz, npages, q_hbm, owner_hbm, page_hbm, len_hbm, qall_ref, lists_ref, items_ref, slots_ref,
    q_v, owner_v, page_v, len_s, zq, zsend, zm, ysend, mall,
    in_sem, qs_z, qr_z, ms_z, mr_z, qs_y, qr_y, qs_c, qr_c, ms_y, mr_y,
):
    me = lax.axis_index("req")
    z, yc = me // PLANE, me % PLANE
    y, core = yc // 2, yc % 2
    sib = yc + 1 - 2 * core
    zpeers = [(z + k) % nz for k in far_first(nz)]
    plane = [(yc + k) % PLANE for k in range(1, PLANE)]
    barrier = pltpu.get_barrier_semaphore()
    for p in zpeers:
        pl.semaphore_signal(barrier, inc=1, device_id={"req": p * PLANE + yc}, device_id_type=MESH)
    for p in plane:
        pl.semaphore_signal(barrier, inc=1, device_id={"req": z * PLANE + p}, device_id_type=MESH)
    ins = [
        pltpu.make_async_copy(h, v, in_sem.at[i])
        for i, (h, v) in enumerate([(q_hbm, q_v), (owner_hbm, owner_v), (page_hbm, page_v), (len_hbm, len_s)])
    ]
    start_all(ins)
    ins[0].wait()
    zq[z % 2, z // 2] = head_pair_rows(q_v[...].astype(F32)).astype(BF16)
    pl.semaphore_wait(barrier, nz - 1 + PLANE - 1)
    mine = zq.at[z % 2, z // 2]
    q_z = [
        [
            remote(mine, mine, qs_z.at[k - 1], qr_z.at[k - 1], {"req": (z + k) % nz * PLANE + yc})
            for k in far_first(nz)
            if k % 2 == h
        ]
        for h in range(2)
    ]
    start_all(q_z[0] + q_z[1])

    wait_all(ins[1:])
    rows, lanes = iota((128, 128), 0), iota((128, 128), 1)
    tri = jnp.where(rows <= lanes, 1.0, 0.0).astype(BF16)
    ones = jnp.ones((128, 128), BF16)
    base = jnp.zeros((128, 128), F32)
    table = jnp.zeros((32, 128), F32)
    for s in range(SLOTS):
        live = jnp.clip(len_s[s] - iota((1, 128), 1) * 128, 0, 128)
        hit = jnp.logical_and(rows == owner_v[s : s + 1, :], live > 0)
        hot = jnp.where(hit, 1.0, 0.0).astype(BF16)
        rank = jnp.sum(jnp.where(hit, base + dot_nn(hot, tri) - 1.0, 0.0), axis=0, keepdims=True)
        base = base + dot_nn(hot, ones)
        kind = rows % 32 // CAP
        quarter = rows // 32 == owner_v[s : s + 1, :] % 4
        val = jnp.where(
            kind == 0, page_v[s : s + 1, :].astype(F32),
            jnp.where(kind == 1, live.astype(F32), jnp.where(kind == 2, float(s), 0.0)),
        )
        place = jnp.where(jnp.logical_and(quarter, (rows % CAP).astype(F32) == rank), val, 0.0).astype(BF16)
        four = jnp.logical_and(rows[0:32] == owner_v[s : s + 1, :] // 4, live > 0)
        table = table + dot_nt(jnp.where(four, 1.0, 0.0).astype(BF16), place)
    for i in range(nz):
        zsend[i] = table[2 * i : 2 * i + 2].astype(BF16)
    zm[z] = zsend[z]
    m_z = [
        remote(zsend.at[p], zm.at[z], ms_z.at[i], mr_z.at[i], {"req": p * PLANE + yc}) for i, p in enumerate(zpeers)
    ]
    start_all(m_z)

    def over_y(k, src, sem):
        to = {"req": z * PLANE + (y + k) % 4 * 2 + core}
        return lambda dst: remote(src, dst, qs_y.at[sem], qr_y.at[sem], to)

    def cross(ref, sem):
        c = remote(ref, ref, qs_c.at[sem], qr_c.at[sem], {"req": z * PLANE + sib})
        c.start()
        q_c.append(c)

    def from_y(k, h):
        return qall_ref.at[(y + k) % 4 * 2 + core, (z + h) % 2]

    q_up, q_down, q_c = [], [], []
    for h in range(2):
        wait_all(q_z[h])
        part = (z + h) % 2
        q_up.append(over_y(1, zq.at[part], 2 * h)(from_y(0, h)))
        q_down.append(over_y(3, zq.at[part], 2 * h + 1)(from_y(0, h)))
        start_all([q_up[h], q_down[h]])
        c = remote(zq.at[part], from_y(0, h), qs_c.at[6 + h], qr_c.at[6 + h], {"req": z * PLANE + sib})
        c.start()
        q_c.append(c)
    qall_ref[yc] = zq[...]
    q_up[0].wait()
    relay = [over_y(1, from_y(3, 0), 4)(from_y(3, 0))]
    relay[0].start()
    cross(from_y(3, 0), 0)

    wait_all(m_z)
    got = [zm[i].astype(F32) for i in range(nz)]
    for d in range(PLANE):
        half = jnp.concatenate([g[d // 4 : d // 4 + 1, :] for g in got], axis=0)
        if d % 4:
            half = pltpu.roll(half, 128 - 32 * (d % 4), 1)
        ysend[d] = half.astype(BF16)
    mall[yc] = ysend[yc]
    m_y = [
        remote(ysend.at[p], mall.at[yc], ms_y.at[i], mr_y.at[i], {"req": z * PLANE + p}) for i, p in enumerate(plane)
    ]
    start_all(m_y)
    q_down[1].wait()
    relay.append(over_y(3, from_y(1, 1), 5)(from_y(1, 1)))
    relay[1].start()
    cross(from_y(1, 1), 1)
    wait_all(m_y)
    sort_items(nz * PLANE, npages, mall[...].reshape(nz * PLANE, 128), lists_ref, items_ref, slots_ref)
    q_down[0].wait()
    cross(from_y(1, 0), 2)
    q_up[1].wait()
    cross(from_y(3, 1), 3)
    for h in range(2):
        relay[h].wait()
        cross(from_y(2, h), 4 + h)
    wait_all(q_c)


def owner_kernel(
    nz, qall_ref, lists_ref, items_ref, sg_s, pool_hbm, po_ref, ps_ref,
    pool, qx, o_s, ml_s, wn_s, s0, p0, lst, sems,
):
    nsrc = nz * PLANE
    lst_copy = pltpu.make_async_copy(lists_ref, lst, sems.at[0])
    lst_copy.start()
    pool_copy = pltpu.make_async_copy(pool_hbm, pool, sems.at[1])
    pool_copy.start()
    row8, lane8 = iota((8, 128), 0), iota((8, 128), 1)
    low, left = row8 < 4, lane8 < 64
    live, slot = items_ref[0:8], items_ref[8:16]

    keep = jnp.where(left, 0.125, 0.0)

    @pl.loop(0, 2 * PLANE)
    def _(g):
        for j in range(nz // 2):
            i = g // 2 * nz + 2 * j + g % 2
            q = qall_ref[g // 2, g % 2, j].astype(F32)
            for r in range(CAP):
                o_s[i * CAP + r] = jnp.zeros((8, 128), F32)
            for t in range(2):
                v = q[8 * t : 8 * t + 8]
                vs = pltpu.roll(v, 4, 0)
                qx[i * SLOTS + 2 * t] = jnp.where(low, v, pltpu.roll(vs, 64, 1)) * keep
                qx[i * SLOTS + 2 * t + 1] = jnp.where(low, vs, pltpu.roll(v, 64, 1)) * keep

    lst_copy.wait()
    pool_copy.wait()

    def scores_of(c, out):
        c = jnp.clip(c, 0, COLUMNS - 1)
        q = jnp.concatenate([qx[lst[k, c]] for k in range(CHUNK)], axis=0).astype(BF16)
        out[...] = dot_nt(q, pool[lst[3 * CHUNK, c]])

    def probs_of(c, scores, out):
        c = jnp.clip(c, 0, COLUMNS - 1)
        pair = []
        for k in range(CHUNK):
            sc = jnp.where(lane8 < lst[2 * CHUNK + k, c], scores[8 * k : 8 * k + 8], NEG)
            top = jnp.max(sc, axis=1, keepdims=True)
            pr = jnp.exp(sc - top)
            ml_s[lst[CHUNK + k, c]] = jnp.where(left, top, jnp.sum(pr, axis=1, keepdims=True))
            pair.append(pr)
            if k % 2:
                out[8 * k - 8 : 8 * k + 8] = jnp.concatenate(pair, axis=0).astype(BF16)
                pair = []

    def values_of(c, probs):
        c = jnp.clip(c, 0, COLUMNS - 1)
        out = dot_nn(probs[...], pool[lst[3 * CHUNK, c]])
        for k in range(CHUNK):
            o_s[lst[CHUNK + k, c]] = out[8 * k : 8 * k + 8]

    @pl.loop(0, (lst[3 * CHUNK + 1, 0] + UNROLL - 1) // UNROLL + 2)
    def _(step):
        c = step * UNROLL
        for u in range(UNROLL):
            values_of(c - 2 * UNROLL + u, p0.at[u])
        for u in range(UNROLL):
            probs_of(c - UNROLL + u, s0.at[u], p0.at[u])
        for u in range(UNROLL):
            scores_of(c + u, s0.at[u])

    halves = []
    for h in range(2):

        def gather(g, accs, h=h):
            accs = list(accs)
            for u in range(8):
                i = g * 8 + u
                mask = lane8 % 64 == i
                for r in range(CAP):
                    accs[r] = jnp.where(mask, ml_s[(h * 64 + i) * CAP + r], accs[r])
            return tuple(accs)

        halves.append(lax.fori_loop(0, 8, gather, tuple(jnp.zeros((8, 128), F32) for _ in range(CAP))))
    mine = [[jnp.logical_and(live[r : r + 1] > 0.0, slot[r : r + 1] == float(s)) for s in range(SLOTS)] for r in range(CAP)]
    ms = [jnp.where(left, halves[0][r], pltpu.roll(halves[1][r], 64, 1)) for r in range(CAP)]
    ls = [jnp.where(left, pltpu.roll(halves[0][r], 64, 1), halves[1][r]) for r in range(CAP)]
    tops, dens = [], []
    for s in range(SLOTS):
        top = jnp.full((8, 128), NEG, F32)
        for r in range(CAP):
            top = jnp.maximum(top, jnp.where(mine[r][s], ms[r], NEG))
        tops.append(top)
    es = []
    for r in range(CAP):
        top = ms[r]
        for s in range(SLOTS):
            top = jnp.where(mine[r][s], tops[s], top)
        es.append(jnp.exp(ms[r] - top))
    lses, invs = [], []
    for s in range(SLOTS):
        den = jnp.zeros((8, 128), F32)
        for r in range(CAP):
            den = den + jnp.where(mine[r][s], es[r] * ls[r], 0.0)
        some = den > 0.0
        den = jnp.where(some, den, 1.0)
        invs.append(1.0 / den)
        lses.append(jnp.where(some, tops[s] + jnp.log(den), NEG))
    weights = []
    for r in range(CAP):
        w = jnp.zeros((8, 128), F32)
        for s in range(SLOTS):
            w = jnp.where(mine[r][s], es[r] * invs[s], w)
        weights.append(w)
    wide = jnp.concatenate(weights + weights, axis=0).T
    high = wide.astype(BF16).astype(F32)
    left128 = iota((nsrc, 128), 1) < 64

    def pairs(x):
        return jnp.where(left128, x, pltpu.roll(x, nsrc - 1, 0))

    wn_s[0] = pairs(high)
    wn_s[1] = pairs(wide - high)
    wn_s[2] = pairs(sg_s[...])
    for d in range(PLANE):
        stat = jnp.full((8, 128), NEG, F32)
        for s in range(SLOTS):
            shift = (nz * (s - d)) % 128
            moved = pltpu.roll(lses[s], shift, 1) if shift else lses[s]
            stat = jnp.where(lane8 // nz == s, moved, stat)
        ps_ref[d] = stat

    ar, al = iota((64, 128), 0), iota((64, 128), 1)
    same = jnp.logical_and(ar // 32 == al // 64, ar // 16 % 2 * 4 + ar % 4 == al % 8)
    want = jnp.where(same, ar // 4 % 4, -1).astype(F32)
    left16 = iota((16, 128), 1) < 64

    @pl.loop(0, PLANE)
    def _(d):
        for j in range(nz // 2):
            i = d * nz + 2 * j
            o = jnp.concatenate([o_s[i * CAP + k] for k in range(2 * CAP)], axis=0).astype(BF16)
            hit = want == wn_s[2, pl.ds(i, 1), :]
            pick = [jnp.where(hit, wn_s[k, pl.ds(i, 1), :], 0.0) for k in range(2)]
            res = dot_nn(jnp.concatenate(pick, axis=0).astype(BF16), o)
            res = res[0:64] + res[64:128]
            for a in range(2):
                even, odd = res[32 * a : 32 * a + 16], res[32 * a + 16 : 32 * a + 32]
                po_ref[d, 2 * j + a] = jnp.where(left16, pltpu.roll(even, 64, 1), odd).astype(BF16)


def spread_weights(x, nz):
    low = iota((8, 128), 0) < 4
    xs = pltpu.roll(x, 4, 0)
    yl = jnp.where(low, x, pltpu.roll(xs, 128 - nz, 1))
    yr = jnp.where(low, xs, pltpu.roll(x, 128 - nz, 1))
    return yl, yr


def return_kernel(
    nz, ntp, po_ref, ps_ref, q_hbm, fresh_hbm, w_hbm, resid_hbm, res_out, norm_out,
    q_ref, fresh_ref, wv, resid_ref, rc, rsc, ysnd, ystat, ry, rsy, o1, s1, ro2, rs2, parts,
    in_sem, os_c, or_c, ss_c, sr_c, os_y, or_y, ss_y, sr_y, os_z, or_z, ss_z, sr_z, ts, tr,
):
    me, tp = lax.axis_index("req"), lax.axis_index("tp")
    z, yc = me // PLANE, me % PLANE
    y, core = yc // 2, yc % 2
    sib = yc + 1 - 2 * core
    zpeers = [(z + k) % nz for k in far_first(nz)]
    yorder = [(y + k) % 4 for k in (2, 1, 3, 0)]
    tpeers = [(tp + k) % ntp for k in range(1, ntp)]
    barrier = pltpu.get_barrier_semaphore()
    pl.semaphore_signal(barrier, inc=1, device_id={"req": z * PLANE + sib}, device_id_type=MESH)
    for p in yorder[:3]:
        pl.semaphore_signal(barrier, inc=1, device_id={"req": z * PLANE + 2 * p + core}, device_id_type=MESH)
    for p in zpeers:
        pl.semaphore_signal(barrier, inc=1, device_id={"req": p * PLANE + yc}, device_id_type=MESH)
    for p in tpeers:
        pl.semaphore_signal(barrier, inc=1, device_id={"tp": p}, device_id_type=MESH)
    ins = [
        pltpu.make_async_copy(h, v, in_sem.at[i])
        for i, (h, v) in enumerate(
            [(q_hbm, q_ref), (fresh_hbm, fresh_ref), (w_hbm, wv), (resid_hbm, resid_ref)]
        )
    ]
    start_all(ins)
    pl.semaphore_wait(barrier, nz - 1 + 4 + ntp - 1)

    cores = []
    for i, p in enumerate(yorder):
        to = {"req": z * PLANE + sib}
        theirs = 2 * p + 1 - core
        cores.append(
            [
                remote(ps_ref.at[theirs], rsc.at[i], ss_c.at[i], sr_c.at[i], to),
                remote(po_ref.at[theirs], rc.at[i], os_c.at[i], or_c.at[i], to),
            ]
        )
        start_all(cores[-1])

    row8, lane8 = iota((8, 128), 0), iota((8, 128), 1)
    low, left = row8 < 4, lane8 < 64
    wait_all(ins[:2])
    q16 = head_pair_rows(q_ref[...].astype(F32))
    fresh = fresh_ref[...].astype(F32)
    self_score, self_value = [], []
    for t in range(2):
        kv = jnp.concatenate([fresh[2 * t : 2 * t + 1]] * 4 + [fresh[2 * t + 1 : 2 * t + 2]] * 4, axis=0)
        other = pltpu.roll(kv, 64, 1)
        prod = q16[8 * t : 8 * t + 8] * jnp.where(left, kv, other)
        ls = jnp.sum(jnp.where(left, prod, 0.0), axis=1, keepdims=True)
        rsum = jnp.sum(jnp.where(left, 0.0, prod), axis=1, keepdims=True)
        self_score.append(jnp.where(left, ls, rsum) * 0.125)
        self_value.append(jnp.where(left, other, kv))

    def from_here(x):
        ahead = pltpu.roll(x, (128 - z) % 128, 1)
        behind = pltpu.roll(x, nz - z, 1)
        return jnp.where(lane8 % nz + z < nz, ahead, behind)

    ys = [[], []]
    sides, stats = [], []
    for h in range(2):
        for i, p in enumerate(yorder):
            ours = 2 * p + core
            if h == 0:
                wait_all(cores[i])
                sa, sb = ps_ref[ours], rsc[i]
                top = jnp.maximum(sa, sb)
                ea, eb = jnp.exp(sa - top), jnp.exp(sb - top)
                both = ea + eb
                ystat[i] = from_here(top + jnp.log(both))
                sides.append(spread_weights(from_here(ea / both), nz))
            yl, yr = sides[i]
            for j in range(nz // 2):
                k = 2 * j + h
                halves = []
                zi = (z + k) % nz
                pa, pb = po_ref[ours, zi].astype(F32), rc[i, zi].astype(F32)
                for t in range(2):
                    li = 2 * t * nz + k
                    w = jnp.where(left, yl[:, li : li + 1], yr[:, li : li + 1])
                    b = pb[8 * t : 8 * t + 8]
                    halves.append(b + w * (pa[8 * t : 8 * t + 8] - b))
                ysnd[i, h, j] = jnp.concatenate(halves, axis=0).astype(BF16)
            if i < 3:
                to = {"req": z * PLANE + 2 * p + core}
                if h == 0:
                    ys[h].append(remote(ystat.at[i], rsy.at[i], ss_y.at[i], sr_y.at[i], to))
                    ys[h][-1].start()
                ys[h].append(
                    remote(ysnd.at[i, h], ry.at[i, h], os_y.at[3 * h + i], or_y.at[3 * h + i], to)
                )
                ys[h][-1].start()

    zs = []
    for h in range(2):
        wait_all(ys[h])
        if h == 0:
            stats = [rsy[p] for p in range(3)] + [ystat[3]]
            top = stats[0]
            for p in range(1, 4):
                top = jnp.maximum(top, stats[p])
            ws = [jnp.exp(s - top) for s in stats]
            wsum = ws[0]
            for p in range(1, 4):
                wsum = wsum + ws[p]
            lse = top + jnp.log(wsum)
            sides = [spread_weights(w / wsum, nz) for w in ws]
            by_slot = [pltpu.roll(lse, (128 - nz * s) % 128, 1) if s else lse for s in range(SLOTS)]
            rows = jnp.concatenate(by_slot + [jnp.zeros((96, 128), F32)], axis=0).T
            for k in range(nz):
                s1[k] = rows[k : k + 1]
        for j in range(nz // 2):
            k = 2 * j + h
            pieces = [ry[p, h, j].astype(F32) for p in range(3)] + [ysnd[3, h, j].astype(F32)]
            halves = []
            for t in range(2):
                li = 2 * t * nz + k
                total = jnp.zeros((8, 128), F32)
                for p in range(4):
                    yl, yr = sides[p]
                    w = jnp.where(left, yl[:, li : li + 1], yr[:, li : li + 1])
                    total = total + w * pieces[p][8 * t : 8 * t + 8]
                halves.append(total)
            o1[k] = jnp.concatenate(halves, axis=0).astype(BF16)
        for k in far_first(nz):
            if k % 2 == h:
                to = {"req": (z + k) % nz * PLANE + yc}
                zs.append(remote(s1.at[k], rs2.at[z], ss_z.at[k - 1], sr_z.at[k - 1], to))
                zs.append(remote(o1.at[k], ro2.at[z], os_z.at[k - 1], or_z.at[k - 1], to))
                start_all(zs[-2:])
    ro2[z] = o1[0]
    rs2[z] = s1[0]
    wait_all(zs)

    st = jnp.concatenate([rs2[zi] for zi in range(nz)], axis=0)
    top = jnp.max(st, axis=0, keepdims=True)
    cols = jnp.concatenate(
        [jnp.exp(st - top), jnp.broadcast_to(top, (8, 128)), jnp.zeros((120 - nz, 128), F32)], axis=0
    ).T
    att = []
    for t in range(2):
        x0, x1 = cols[16 * t : 16 * t + 8], cols[16 * t + 8 : 16 * t + 16]
        yl = jnp.where(low, x0, pltpu.roll(x1, 4, 0))
        yr = jnp.where(low, pltpu.roll(x0, 4, 0), x1)
        num = jnp.zeros((8, 128), F32)
        den = jnp.zeros((8, 128), F32)
        for zi in range(nz):
            w = jnp.where(left, yl[:, zi : zi + 1], yr[:, zi : zi + 1])
            num = num + w * ro2[zi, 8 * t : 8 * t + 8].astype(F32)
            den = den + w
        topm = jnp.where(left, yl[:, nz : nz + 1], yr[:, nz : nz + 1])
        best = jnp.maximum(topm, self_score[t])
        a, b = jnp.exp(topm - best), jnp.exp(self_score[t] - best)
        att.append((a * num + b * self_value[t]) / (a * den + b))
    att = jnp.concatenate(att, axis=0)
    r16 = iota((16, 128), 0)
    wide = jnp.concatenate([jnp.where(r16 % 4 == h, att, 0.0) for h in range(4)], axis=1).astype(BF16)
    sel = jnp.where(iota((16, 16), 1) // 4 == iota((16, 16), 0), 1.0, 0.0).astype(BF16)
    lhs = dot_nn(sel, wide).astype(BF16)
    wait_all(ins[2:])
    parts[tp] = dot_nn(lhs, wv[...])[0:SLOTS].astype(BF16)
    copies = []
    for i, p in enumerate(tpeers):
        copies.append(remote(parts.at[tp], parts.at[tp], ts.at[i], tr.at[i], {"tp": p}))
    for c in copies:
        c.start()
    for c in copies:
        c.wait()
    stream = parts[0].astype(F32)
    for p in range(1, ntp):
        stream = stream + parts[p].astype(F32)
    stream = resid_ref[...].astype(F32) + stream
    mean = jnp.mean(stream * stream, axis=1, keepdims=True)
    res_out[...] = stream
    norm_out[...] = stream * lax.rsqrt(mean + 1e-5)


def vmem(n):
    return [pl.BlockSpec(memory_space=pltpu.VMEM)] * n


def in_hbm(x):
    return pltpu.with_memory_space_constraint(x, pltpu.HBM)


def hbm(n):
    return [pl.BlockSpec(memory_space=pltpu.HBM)] * n


def owner_call(nz, qall, lists, items, slots, pool):
    nsrc = nz * PLANE
    return pl.pallas_call(
        functools.partial(owner_kernel, nz),
        out_shape=(
            jax.ShapeDtypeStruct((PLANE, nz, 16, 128), BF16),
            jax.ShapeDtypeStruct((PLANE, 8, 128), F32),
        ),
        in_specs=vmem(4) + hbm(1),
        out_specs=tuple(vmem(2)),
        scratch_shapes=[
            VM(pool.shape, BF16),
            VM((nsrc * SLOTS, 8, 128), F32),
            VM((nsrc * CAP + 1, 8, 128), F32), VM((nsrc * CAP + 1, 8, 128), F32),
            VM((3, nsrc, 128), F32),
            VM((UNROLL, 8 * CHUNK, 128), F32), VM((UNROLL, 8 * CHUNK, 128), BF16),
            pltpu.SMEM((3 * CHUNK + 8, COLUMNS), I32),
            pltpu.SemaphoreType.DMA((2,)),
        ],
        compiler_params=pltpu.CompilerParams(vmem_limit_bytes=24 << 20),
        name="owner",
    )(qall, lists, items, slots, in_hbm(pool))


def dispatch_call(nz, npages, queries, block_owner, block_page, lengths):
    DMA = pltpu.SemaphoreType.DMA
    return pl.pallas_call(
        functools.partial(dispatch_kernel, nz, npages),
        out_shape=(
            jax.ShapeDtypeStruct((PLANE, 2, nz // 2, 16, 128), BF16),
            jax.ShapeDtypeStruct((3 * CHUNK + 8, COLUMNS), I32),
            jax.ShapeDtypeStruct((16, 128), F32),
            jax.ShapeDtypeStruct((nz * PLANE, 128), F32),
        ),
        in_specs=hbm(4),
        out_specs=tuple(vmem(4)),
        scratch_shapes=[
            VM(queries.shape, BF16), VM((SLOTS, 128), I32), VM((SLOTS, 128), I32), pltpu.SMEM((SLOTS,), I32),
            VM((2, nz // 2, 16, 128), BF16), VM((nz, 2, 128), BF16), VM((nz, 2, 128), BF16),
            VM((PLANE, nz, 128), BF16), VM((PLANE, nz, 128), BF16),
        ]
        + [DMA((4,))] + [DMA((nz - 1,))] * 4 + [DMA((6,))] * 2 + [DMA((8,))] * 2 + [DMA((PLANE - 1,))] * 2,
        compiler_params=pltpu.CompilerParams(
            collective_id=0, has_side_effects=True, vmem_limit_bytes=6 << 20
        ),
        name="dispatch",
    )(*map(in_hbm, (queries, block_owner.reshape(SLOTS, 128), block_page.reshape(SLOTS, 128), lengths)))


def return_call(nz, ntp, po, ps, queries, fresh_key_value, o_weight, resid_in, norm_gain):
    width = o_weight.shape[1]
    DMA = pltpu.SemaphoreType.DMA
    block, half = (nz, 16, 128), (2, nz // 2, 16, 128)
    stream, scaled = pl.pallas_call(
        functools.partial(return_kernel, nz, ntp),
        out_shape=(
            jax.ShapeDtypeStruct((SLOTS, width), F32),
            jax.ShapeDtypeStruct((SLOTS, width), F32),
        ),
        in_specs=vmem(2) + hbm(4),
        out_specs=tuple(vmem(2)),
        scratch_shapes=[
            VM(queries.shape, BF16), VM(fresh_key_value.shape, BF16), VM(o_weight.shape, BF16),
            VM(resid_in.shape, BF16),
            VM((4,) + block, BF16), VM((4, 8, 128), F32), VM((4,) + half, BF16), VM((4, 8, 128), F32),
            VM((3,) + half, BF16), VM((3, 8, 128), F32),
            VM(block, BF16), VM((nz, 1, 128), F32), VM(block, BF16), VM((nz, 1, 128), F32),
            VM((ntp, SLOTS, width), BF16),
        ]
        + [DMA((4,))] + [DMA((4,))] * 4 + [DMA((6,))] * 2 + [DMA((3,))] * 2 + [DMA((nz - 1,))] * 4 + [DMA((ntp - 1,))] * 2,
        compiler_params=pltpu.CompilerParams(
            collective_id=1, has_side_effects=True, vmem_limit_bytes=12 << 20
        ),
        name="give_back",
    )(po, ps, *map(in_hbm, (queries, fresh_key_value, o_weight, resid_in)))
    return stream.astype(BF16), (scaled * norm_gain.astype(F32)).astype(BF16)


def body(nz, ntp, queries, fresh_key_value, pool, block_owner, block_page, lengths, o_weight, resid_in, norm_gain):
    qall, lists, items, slots = dispatch_call(nz, pool.shape[0], queries, block_owner, block_page, lengths)
    po, ps = owner_call(nz, qall, lists, items, slots, pool)
    return return_call(nz, ntp, po, ps, queries, fresh_key_value, o_weight, resid_in, norm_gain)


def solution(mesh):
    nz, ntp = mesh.shape["req"] // PLANE, mesh.shape["tp"]
    placed = (
        P("req", "tp"), P("req", "tp"), P("req", None, "tp"), P("req", None), P("req"), P("req"),
        P("tp", None), P("req", None), P(),
    )
    return jax.shard_map(
        functools.partial(body, nz, ntp),
        mesh=mesh,
        in_specs=placed,
        out_specs=(P("req", None), P("req", None)),
        check_vma=False,
    )
```

```python
import functools

import jax
import jax.numpy as jnp
from jax import lax
from jax.experimental import pallas as pl
from jax.experimental.pallas import tpu as pltpu
from jax.sharding import PartitionSpec as P

F32, BF16, I32 = jnp.float32, jnp.bfloat16, jnp.int32
MESH = pl.DeviceIdType.MESH
NEG = -1e30
CAP = 8
CHUNK = 16
UNROLL = 4
COLUMNS = 128
SLOTS = 4
PLANE = 8
VM = pltpu.VMEM


def iota(shape, dim):
    return lax.broadcasted_iota(I32, shape, dim)


def dot_nt(a, b):
    return lax.dot_general(a, b, (((1,), (1,)), ((), ())), preferred_element_type=F32)


def dot_nn(a, b):
    return jnp.dot(a, b, preferred_element_type=F32)


def head_pair_rows(q):
    return jnp.concatenate([q[s : s + 1, 128 * h : 128 * h + 128] for s in range(SLOTS) for h in range(4)], axis=0)


def remote(src, dst, send, recv, peer):
    return pltpu.make_async_remote_copy(
        src_ref=src, dst_ref=dst, send_sem=send, recv_sem=recv, device_id=peer, device_id_type=MESH
    )


def start_all(copies):
    for c in copies:
        c.start()


def wait_all(copies):
    for c in copies:
        c.wait()


def far_first(n):
    return sorted(range(1, n), key=lambda k: -min(k, n - k))


def sort_items(nsrc, npages, meta_b, lists_ref, items_ref, slots_ref):
    meta = meta_b.astype(F32).T
    page, live, slot = meta[0:8], meta[8:16], meta[16:24]
    items_ref[0:8] = live
    items_ref[8:16] = slot
    prow = iota((npages, 128), 0).astype(F32)
    eqs = [
        jnp.where(jnp.logical_and(prow == page[r : r + 1], live[r : r + 1] > 0.0), 1.0, 0.0) for r in range(CAP)
    ]
    upto = jnp.where(iota((128, 256), 0) <= iota((128, 256), 1), 1.0, 0.0).astype(BF16)
    counts = dot_nn(jnp.concatenate(eqs, axis=0).astype(BF16), upto)
    run = jnp.zeros((npages, 128), F32)
    ranks = []
    for r in range(CAP):
        part = counts[npages * r : npages * r + npages]
        ranks.append(run + part[:, 0:128])
        run = run + part[:, 128:256]
    chunks = jnp.floor((run + (CHUNK - 1)) * (1.0 / CHUNK))
    below = jnp.where(iota((npages, npages), 1) < iota((npages, npages), 0), 1.0, 0.0).astype(BF16)
    first = dot_nn(below, chunks.astype(BF16))
    total = (first + chunks)[npages - 1 : npages]

    krow = iota((CHUNK, 128), 0).astype(F32)
    crow = iota((COLUMNS, 128), 0).astype(F32)
    src = iota((1, 128), 1).astype(F32)
    lists = jnp.zeros((5 * CHUNK, COLUMNS), F32)
    for r in range(CAP):
        row = slice(r, r + 1)
        pos = jnp.sum(eqs[r] * (first * CHUNK + ranks[r] - 1.0), axis=0, keepdims=True)
        chunk = jnp.floor(pos * (1.0 / CHUNK))
        here = jnp.logical_and(krow == pos - chunk * CHUNK, live[row] > 0.0)
        pick = [jnp.where(here, v, 0.0) for v in (src, float(r + 1), live[row], slot[row], page[row])]
        col = jnp.where(crow == chunk, 1.0, 0.0)
        lists = lists + dot_nt(jnp.concatenate(pick, axis=0).astype(BF16), col.astype(BF16))
    srcs, nth = lists[0:CHUNK], lists[CHUNK : 2 * CHUNK]
    lists_ref[0:CHUNK] = (srcs * SLOTS + lists[3 * CHUNK : 4 * CHUNK]).astype(I32)
    lists_ref[CHUNK : 2 * CHUNK] = jnp.where(nth > 0.0, srcs * CAP + nth - 1.0, float(nsrc * CAP)).astype(I32)
    lists_ref[2 * CHUNK : 3 * CHUNK] = lists[2 * CHUNK : 3 * CHUNK].astype(I32)
    lists_ref[3 * CHUNK : 3 * CHUNK + 8] = jnp.concatenate(
        [lists[4 * CHUNK : 4 * CHUNK + 1], jnp.tile(total, (1, COLUMNS // 128)), jnp.zeros((6, COLUMNS), F32)], axis=0
    ).astype(I32)
    spread = jnp.where(iota((128, 128), 0) == 2 * CAP + iota((128, 128), 1) // 8 % CAP, 1.0, 0.0).astype(BF16)
    slots_ref[...] = dot_nn(meta_b, spread)


def dispatch_kernel(
    nz, npages, q_hbm, owner_hbm, page_hbm, len_hbm, qall_ref, lists_ref, items_ref, slots_ref,
    q_v, owner_v, page_v, len_s, zq, zsend, zm, ysend, mall,
    in_sem, qs_z, qr_z, ms_z, mr_z, qs_y, qr_y, qs_c, qr_c, ms_y, mr_y,
):
    me = lax.axis_index("req")
    z, yc = me // PLANE, me % PLANE
    y, core = yc // 2, yc % 2
    sib = yc + 1 - 2 * core
    zpeers = [(z + k) % nz for k in far_first(nz)]
    plane = [(yc + k) % PLANE for k in range(1, PLANE)]
    ypeers = [(y + k) % 4 for k in (2, 1, 3)]
    barrier = pltpu.get_barrier_semaphore()
    for p in zpeers:
        pl.semaphore_signal(barrier, inc=1, device_id={"req": p * PLANE + yc}, device_id_type=MESH)
    for p in plane:
        pl.semaphore_signal(barrier, inc=1, device_id={"req": z * PLANE + p}, device_id_type=MESH)
    ins = [
        pltpu.make_async_copy(h, v, in_sem.at[i])
        for i, (h, v) in enumerate([(q_hbm, q_v), (owner_hbm, owner_v), (page_hbm, page_v), (len_hbm, len_s)])
    ]
    start_all(ins)
    ins[0].wait()
    zq[z % 2, z // 2] = head_pair_rows(q_v[...].astype(F32)).astype(BF16)
    pl.semaphore_wait(barrier, nz - 1 + PLANE - 1)
    mine = zq.at[z % 2, z // 2]
    q_z = [
        [
            remote(mine, mine, qs_z.at[k - 1], qr_z.at[k - 1], {"req": (z + k) % nz * PLANE + yc})
            for k in far_first(nz)
            if k % 2 == h
        ]
        for h in range(2)
    ]
    start_all(q_z[0] + q_z[1])

    wait_all(ins[1:])
    rows, lanes = iota((128, 128), 0), iota((128, 128), 1)
    tri = jnp.where(rows <= lanes, 1.0, 0.0).astype(BF16)
    ones = jnp.ones((128, 128), BF16)
    base = jnp.zeros((128, 128), F32)
    table = jnp.zeros((32, 128), F32)
    for s in range(SLOTS):
        live = jnp.clip(len_s[s] - iota((1, 128), 1) * 128, 0, 128)
        hit = jnp.logical_and(rows == owner_v[s : s + 1, :], live > 0)
        hot = jnp.where(hit, 1.0, 0.0).astype(BF16)
        rank = jnp.sum(jnp.where(hit, base + dot_nn(hot, tri) - 1.0, 0.0), axis=0, keepdims=True)
        base = base + dot_nn(hot, ones)
        kind = rows % 32 // CAP
        quarter = rows // 32 == owner_v[s : s + 1, :] % 4
        val = jnp.where(
            kind == 0, page_v[s : s + 1, :].astype(F32),
            jnp.where(kind == 1, live.astype(F32), jnp.where(kind == 2, float(s), 0.0)),
        )
        place = jnp.where(jnp.logical_and(quarter, (rows % CAP).astype(F32) == rank), val, 0.0).astype(BF16)
        four = jnp.logical_and(rows[0:32] == owner_v[s : s + 1, :] // 4, live > 0)
        table = table + dot_nt(jnp.where(four, 1.0, 0.0).astype(BF16), place)
    for i in range(nz):
        zsend[i] = table[2 * i : 2 * i + 2].astype(BF16)
    zm[z] = zsend[z]
    m_z = [
        remote(zsend.at[p], zm.at[z], ms_z.at[i], mr_z.at[i], {"req": p * PLANE + yc}) for i, p in enumerate(zpeers)
    ]
    start_all(m_z)

    q_y, q_c = [], []
    for h in range(2):
        wait_all(q_z[h])
        part = (z + h) % 2
        for i, p in enumerate(ypeers):
            to = {"req": z * PLANE + 2 * p + core}
            q_y.append(remote(zq.at[part], qall_ref.at[yc, part], qs_y.at[3 * h + i], qr_y.at[3 * h + i], to))
        q_c.append(
            remote(zq.at[part], qall_ref.at[yc, part], qs_c.at[6 + h], qr_c.at[6 + h], {"req": z * PLANE + sib})
        )
        start_all(q_y[-3:] + q_c[-1:])
    qall_ref[yc] = zq[...]

    wait_all(m_z)
    got = [zm[i].astype(F32) for i in range(nz)]
    for d in range(PLANE):
        half = jnp.concatenate([g[d // 4 : d // 4 + 1, :] for g in got], axis=0)
        if d % 4:
            half = pltpu.roll(half, 128 - 32 * (d % 4), 1)
        ysend[d] = half.astype(BF16)
    mall[yc] = ysend[yc]
    m_y = [
        remote(ysend.at[p], mall.at[yc], ms_y.at[i], mr_y.at[i], {"req": z * PLANE + p}) for i, p in enumerate(plane)
    ]
    start_all(m_y)
    wait_all(m_y)
    sort_items(nz * PLANE, npages, mall[...].reshape(nz * PLANE, 128), lists_ref, items_ref, slots_ref)
    for h in range(2):
        for i, p in enumerate((2, 3, 1)):
            q_y[3 * h + i].wait()
            here = qall_ref.at[(y + p) % 4 * 2 + core, (z + h) % 2]
            c = remote(here, here, qs_c.at[3 * h + i], qr_c.at[3 * h + i], {"req": z * PLANE + sib})
            c.start()
            q_c.append(c)
    wait_all(q_c)


def owner_kernel(
    nz, qall_ref, lists_ref, items_ref, sg_s, pool_hbm, po_ref, ps_ref,
    pool, qx, o_s, ml_s, wn_s, s0, p0, lst, sems,
):
    nsrc = nz * PLANE
    lst_copy = pltpu.make_async_copy(lists_ref, lst, sems.at[0])
    lst_copy.start()
    pool_copy = pltpu.make_async_copy(pool_hbm, pool, sems.at[1])
    pool_copy.start()
    row8, lane8 = iota((8, 128), 0), iota((8, 128), 1)
    low, left = row8 < 4, lane8 < 64
    live, slot = items_ref[0:8], items_ref[8:16]

    keep = jnp.where(left, 0.125, 0.0)

    @pl.loop(0, 2 * PLANE)
    def _(g):
        for j in range(nz // 2):
            i = g // 2 * nz + 2 * j + g % 2
            q = qall_ref[g // 2, g % 2, j].astype(F32)
            for r in range(CAP):
                o_s[i * CAP + r] = jnp.zeros((8, 128), F32)
            for t in range(2):
                v = q[8 * t : 8 * t + 8]
                vs = pltpu.roll(v, 4, 0)
                qx[i * SLOTS + 2 * t] = jnp.where(low, v, pltpu.roll(vs, 64, 1)) * keep
                qx[i * SLOTS + 2 * t + 1] = jnp.where(low, vs, pltpu.roll(v, 64, 1)) * keep

    lst_copy.wait()
    pool_copy.wait()

    def scores_of(c, out):
        c = jnp.clip(c, 0, COLUMNS - 1)
        q = jnp.concatenate([qx[lst[k, c]] for k in range(CHUNK)], axis=0).astype(BF16)
        out[...] = dot_nt(q, pool[lst[3 * CHUNK, c]])

    def probs_of(c, scores, out):
        c = jnp.clip(c, 0, COLUMNS - 1)
        pair = []
        for k in range(CHUNK):
            sc = jnp.where(lane8 < lst[2 * CHUNK + k, c], scores[8 * k : 8 * k + 8], NEG)
            top = jnp.max(sc, axis=1, keepdims=True)
            pr = jnp.exp(sc - top)
            ml_s[lst[CHUNK + k, c]] = jnp.where(left, top, jnp.sum(pr, axis=1, keepdims=True))
            pair.append(pr)
            if k % 2:
                out[8 * k - 8 : 8 * k + 8] = jnp.concatenate(pair, axis=0).astype(BF16)
                pair = []

    def values_of(c, probs):
        c = jnp.clip(c, 0, COLUMNS - 1)
        out = dot_nn(probs[...], pool[lst[3 * CHUNK, c]])
        for k in range(CHUNK):
            o_s[lst[CHUNK + k, c]] = out[8 * k : 8 * k + 8]

    @pl.loop(0, (lst[3 * CHUNK + 1, 0] + UNROLL - 1) // UNROLL + 2)
    def _(step):
        c = step * UNROLL
        for u in range(UNROLL):
            values_of(c - 2 * UNROLL + u, p0.at[u])
        for u in range(UNROLL):
            probs_of(c - UNROLL + u, s0.at[u], p0.at[u])
        for u in range(UNROLL):
            scores_of(c + u, s0.at[u])

    halves = []
    for h in range(2):

        def gather(g, accs, h=h):
            accs = list(accs)
            for u in range(8):
                i = g * 8 + u
                mask = lane8 % 64 == i
                for r in range(CAP):
                    accs[r] = jnp.where(mask, ml_s[(h * 64 + i) * CAP + r], accs[r])
            return tuple(accs)

        halves.append(lax.fori_loop(0, 8, gather, tuple(jnp.zeros((8, 128), F32) for _ in range(CAP))))
    mine = [[jnp.logical_and(live[r : r + 1] > 0.0, slot[r : r + 1] == float(s)) for s in range(SLOTS)] for r in range(CAP)]
    ms = [jnp.where(left, halves[0][r], pltpu.roll(halves[1][r], 64, 1)) for r in range(CAP)]
    ls = [jnp.where(left, pltpu.roll(halves[0][r], 64, 1), halves[1][r]) for r in range(CAP)]
    tops, dens = [], []
    for s in range(SLOTS):
        top = jnp.full((8, 128), NEG, F32)
        for r in range(CAP):
            top = jnp.maximum(top, jnp.where(mine[r][s], ms[r], NEG))
        tops.append(top)
    es = []
    for r in range(CAP):
        top = ms[r]
        for s in range(SLOTS):
            top = jnp.where(mine[r][s], tops[s], top)
        es.append(jnp.exp(ms[r] - top))
    lses, invs = [], []
    for s in range(SLOTS):
        den = jnp.zeros((8, 128), F32)
        for r in range(CAP):
            den = den + jnp.where(mine[r][s], es[r] * ls[r], 0.0)
        some = den > 0.0
        den = jnp.where(some, den, 1.0)
        invs.append(1.0 / den)
        lses.append(jnp.where(some, tops[s] + jnp.log(den), NEG))
    weights = []
    for r in range(CAP):
        w = jnp.zeros((8, 128), F32)
        for s in range(SLOTS):
            w = jnp.where(mine[r][s], es[r] * invs[s], w)
        weights.append(w)
    wide = jnp.concatenate(weights + weights, axis=0).T
    high = wide.astype(BF16).astype(F32)
    left128 = iota((nsrc, 128), 1) < 64

    def pairs(x):
        return jnp.where(left128, x, pltpu.roll(x, nsrc - 1, 0))

    wn_s[0] = pairs(high)
    wn_s[1] = pairs(wide - high)
    wn_s[2] = pairs(sg_s[...])
    for d in range(PLANE):
        stat = jnp.full((8, 128), NEG, F32)
        for s in range(SLOTS):
            shift = (nz * (s - d)) % 128
            moved = pltpu.roll(lses[s], shift, 1) if shift else lses[s]
            stat = jnp.where(lane8 // nz == s, moved, stat)
        ps_ref[d] = stat

    ar, al = iota((64, 128), 0), iota((64, 128), 1)
    same = jnp.logical_and(ar // 32 == al // 64, ar // 16 % 2 * 4 + ar % 4 == al % 8)
    want = jnp.where(same, ar // 4 % 4, -1).astype(F32)
    left16 = iota((16, 128), 1) < 64

    @pl.loop(0, PLANE)
    def _(d):
        for j in range(nz // 2):
            i = d * nz + 2 * j
            o = jnp.concatenate([o_s[i * CAP + k] for k in range(2 * CAP)], axis=0).astype(BF16)
            hit = want == wn_s[2, pl.ds(i, 1), :]
            pick = [jnp.where(hit, wn_s[k, pl.ds(i, 1), :], 0.0) for k in range(2)]
            res = dot_nn(jnp.concatenate(pick, axis=0).astype(BF16), o)
            res = res[0:64] + res[64:128]
            for a in range(2):
                even, odd = res[32 * a : 32 * a + 16], res[32 * a + 16 : 32 * a + 32]
                po_ref[d, 2 * j + a] = jnp.where(left16, pltpu.roll(even, 64, 1), odd).astype(BF16)


def spread_weights(x, nz):
    low = iota((8, 128), 0) < 4
    xs = pltpu.roll(x, 4, 0)
    yl = jnp.where(low, x, pltpu.roll(xs, 128 - nz, 1))
    yr = jnp.where(low, xs, pltpu.roll(x, 128 - nz, 1))
    return yl, yr


def return_kernel(
    nz, ntp, po_ref, ps_ref, q_hbm, fresh_hbm, w_hbm, resid_hbm, res_out, norm_out,
    q_ref, fresh_ref, wv, resid_ref, rc, rsc, ysnd, ystat, ry, rsy, o1, s1, ro2, rs2, parts,
    in_sem, os_c, or_c, ss_c, sr_c, os_y, or_y, ss_y, sr_y, os_z, or_z, ss_z, sr_z, ts, tr,
):
    me, tp = lax.axis_index("req"), lax.axis_index("tp")
    z, yc = me // PLANE, me % PLANE
    y, core = yc // 2, yc % 2
    sib = yc + 1 - 2 * core
    zpeers = [(z + k) % nz for k in far_first(nz)]
    yorder = [(y + k) % 4 for k in (2, 1, 3, 0)]
    tpeers = [(tp + k) % ntp for k in range(1, ntp)]
    barrier = pltpu.get_barrier_semaphore()
    pl.semaphore_signal(barrier, inc=1, device_id={"req": z * PLANE + sib}, device_id_type=MESH)
    for p in yorder[:3]:
        pl.semaphore_signal(barrier, inc=1, device_id={"req": z * PLANE + 2 * p + core}, device_id_type=MESH)
    for p in zpeers:
        pl.semaphore_signal(barrier, inc=1, device_id={"req": p * PLANE + yc}, device_id_type=MESH)
    for p in tpeers:
        pl.semaphore_signal(barrier, inc=1, device_id={"tp": p}, device_id_type=MESH)
    ins = [
        pltpu.make_async_copy(h, v, in_sem.at[i])
        for i, (h, v) in enumerate(
            [(q_hbm, q_ref), (fresh_hbm, fresh_ref), (w_hbm, wv), (resid_hbm, resid_ref)]
        )
    ]
    start_all(ins)
    pl.semaphore_wait(barrier, nz - 1 + 4 + ntp - 1)

    cores = []
    for i, p in enumerate(yorder):
        to = {"req": z * PLANE + sib}
        theirs = 2 * p + 1 - core
        cores.append(
            [
                remote(ps_ref.at[theirs], rsc.at[i], ss_c.at[i], sr_c.at[i], to),
                remote(po_ref.at[theirs], rc.at[i], os_c.at[i], or_c.at[i], to),
            ]
        )
        start_all(cores[-1])

    row8, lane8 = iota((8, 128), 0), iota((8, 128), 1)
    low, left = row8 < 4, lane8 < 64
    wait_all(ins[:2])
    q16 = head_pair_rows(q_ref[...].astype(F32))
    fresh = fresh_ref[...].astype(F32)
    self_score, self_value = [], []
    for t in range(2):
        kv = jnp.concatenate([fresh[2 * t : 2 * t + 1]] * 4 + [fresh[2 * t + 1 : 2 * t + 2]] * 4, axis=0)
        other = pltpu.roll(kv, 64, 1)
        prod = q16[8 * t : 8 * t + 8] * jnp.where(left, kv, other)
        ls = jnp.sum(jnp.where(left, prod, 0.0), axis=1, keepdims=True)
        rsum = jnp.sum(jnp.where(left, 0.0, prod), axis=1, keepdims=True)
        self_score.append(jnp.where(left, ls, rsum) * 0.125)
        self_value.append(jnp.where(left, other, kv))

    def from_here(x):
        ahead = pltpu.roll(x, (128 - z) % 128, 1)
        behind = pltpu.roll(x, nz - z, 1)
        return jnp.where(lane8 % nz + z < nz, ahead, behind)

    ys = [[], []]
    sides, stats = [], []
    for h in range(2):
        for i, p in enumerate(yorder):
            ours = 2 * p + core
            if h == 0:
                wait_all(cores[i])
                sa, sb = ps_ref[ours], rsc[i]
                top = jnp.maximum(sa, sb)
                ea, eb = jnp.exp(sa - top), jnp.exp(sb - top)
                both = ea + eb
                ystat[i] = from_here(top + jnp.log(both))
                sides.append(spread_weights(from_here(ea / both), nz))
            yl, yr = sides[i]
            for j in range(nz // 2):
                k = 2 * j + h
                halves = []
                zi = (z + k) % nz
                pa, pb = po_ref[ours, zi].astype(F32), rc[i, zi].astype(F32)
                for t in range(2):
                    li = 2 * t * nz + k
                    w = jnp.where(left, yl[:, li : li + 1], yr[:, li : li + 1])
                    b = pb[8 * t : 8 * t + 8]
                    halves.append(b + w * (pa[8 * t : 8 * t + 8] - b))
                ysnd[i, h, j] = jnp.concatenate(halves, axis=0).astype(BF16)
            if i < 3:
                to = {"req": z * PLANE + 2 * p + core}
                if h == 0:
                    ys[h].append(remote(ystat.at[i], rsy.at[i], ss_y.at[i], sr_y.at[i], to))
                    ys[h][-1].start()
                ys[h].append(
                    remote(ysnd.at[i, h], ry.at[i, h], os_y.at[3 * h + i], or_y.at[3 * h + i], to)
                )
                ys[h][-1].start()

    zs = []
    for h in range(2):
        wait_all(ys[h])
        if h == 0:
            stats = [rsy[p] for p in range(3)] + [ystat[3]]
            top = stats[0]
            for p in range(1, 4):
                top = jnp.maximum(top, stats[p])
            ws = [jnp.exp(s - top) for s in stats]
            wsum = ws[0]
            for p in range(1, 4):
                wsum = wsum + ws[p]
            lse = top + jnp.log(wsum)
            sides = [spread_weights(w / wsum, nz) for w in ws]
            by_slot = [pltpu.roll(lse, (128 - nz * s) % 128, 1) if s else lse for s in range(SLOTS)]
            rows = jnp.concatenate(by_slot + [jnp.zeros((96, 128), F32)], axis=0).T
            for k in range(nz):
                s1[k] = rows[k : k + 1]
        for j in range(nz // 2):
            k = 2 * j + h
            pieces = [ry[p, h, j].astype(F32) for p in range(3)] + [ysnd[3, h, j].astype(F32)]
            halves = []
            for t in range(2):
                li = 2 * t * nz + k
                total = jnp.zeros((8, 128), F32)
                for p in range(4):
                    yl, yr = sides[p]
                    w = jnp.where(left, yl[:, li : li + 1], yr[:, li : li + 1])
                    total = total + w * pieces[p][8 * t : 8 * t + 8]
                halves.append(total)
            o1[k] = jnp.concatenate(halves, axis=0).astype(BF16)
        for k in far_first(nz):
            if k % 2 == h:
                to = {"req": (z + k) % nz * PLANE + yc}
                zs.append(remote(s1.at[k], rs2.at[z], ss_z.at[k - 1], sr_z.at[k - 1], to))
                zs.append(remote(o1.at[k], ro2.at[z], os_z.at[k - 1], or_z.at[k - 1], to))
                start_all(zs[-2:])
    ro2[z] = o1[0]
    rs2[z] = s1[0]
    wait_all(zs)

    st = jnp.concatenate([rs2[zi] for zi in range(nz)], axis=0)
    top = jnp.max(st, axis=0, keepdims=True)
    cols = jnp.concatenate(
        [jnp.exp(st - top), jnp.broadcast_to(top, (8, 128)), jnp.zeros((120 - nz, 128), F32)], axis=0
    ).T
    att = []
    for t in range(2):
        x0, x1 = cols[16 * t : 16 * t + 8], cols[16 * t + 8 : 16 * t + 16]
        yl = jnp.where(low, x0, pltpu.roll(x1, 4, 0))
        yr = jnp.where(low, pltpu.roll(x0, 4, 0), x1)
        num = jnp.zeros((8, 128), F32)
        den = jnp.zeros((8, 128), F32)
        for zi in range(nz):
            w = jnp.where(left, yl[:, zi : zi + 1], yr[:, zi : zi + 1])
            num = num + w * ro2[zi, 8 * t : 8 * t + 8].astype(F32)
            den = den + w
        topm = jnp.where(left, yl[:, nz : nz + 1], yr[:, nz : nz + 1])
        best = jnp.maximum(topm, self_score[t])
        a, b = jnp.exp(topm - best), jnp.exp(self_score[t] - best)
        att.append((a * num + b * self_value[t]) / (a * den + b))
    att = jnp.concatenate(att, axis=0)
    r16 = iota((16, 128), 0)
    wide = jnp.concatenate([jnp.where(r16 % 4 == h, att, 0.0) for h in range(4)], axis=1).astype(BF16)
    sel = jnp.where(iota((16, 16), 1) // 4 == iota((16, 16), 0), 1.0, 0.0).astype(BF16)
    lhs = dot_nn(sel, wide).astype(BF16)
    wait_all(ins[2:])
    parts[tp] = dot_nn(lhs, wv[...])[0:SLOTS]
    copies = []
    for i, p in enumerate(tpeers):
        copies.append(remote(parts.at[tp], parts.at[tp], ts.at[i], tr.at[i], {"tp": p}))
    for c in copies:
        c.start()
    for c in copies:
        c.wait()
    stream = parts[0]
    for p in range(1, ntp):
        stream = stream + parts[p]
    stream = resid_ref[...].astype(F32) + stream
    mean = jnp.mean(stream * stream, axis=1, keepdims=True)
    res_out[...] = stream
    norm_out[...] = jnp.broadcast_to(lax.rsqrt(mean + 1e-5), stream.shape)


def vmem(n):
    return [pl.BlockSpec(memory_space=pltpu.VMEM)] * n


def in_hbm(x):
    return pltpu.with_memory_space_constraint(x, pltpu.HBM)


def hbm(n):
    return [pl.BlockSpec(memory_space=pltpu.HBM)] * n


def owner_call(nz, qall, lists, items, slots, pool):
    nsrc = nz * PLANE
    return pl.pallas_call(
        functools.partial(owner_kernel, nz),
        out_shape=(
            jax.ShapeDtypeStruct((PLANE, nz, 16, 128), BF16),
            jax.ShapeDtypeStruct((PLANE, 8, 128), F32),
        ),
        in_specs=vmem(4) + hbm(1),
        out_specs=tuple(vmem(2)),
        scratch_shapes=[
            VM(pool.shape, BF16),
            VM((nsrc * SLOTS, 8, 128), F32),
            VM((nsrc * CAP + 1, 8, 128), F32), VM((nsrc * CAP + 1, 8, 128), F32),
            VM((3, nsrc, 128), F32),
            VM((UNROLL, 8 * CHUNK, 128), F32), VM((UNROLL, 8 * CHUNK, 128), BF16),
            pltpu.SMEM((3 * CHUNK + 8, COLUMNS), I32),
            pltpu.SemaphoreType.DMA((2,)),
        ],
        compiler_params=pltpu.CompilerParams(vmem_limit_bytes=24 << 20),
        name="owner",
    )(qall, lists, items, slots, in_hbm(pool))


def dispatch_call(nz, npages, queries, block_owner, block_page, lengths):
    DMA = pltpu.SemaphoreType.DMA
    return pl.pallas_call(
        functools.partial(dispatch_kernel, nz, npages),
        out_shape=(
            jax.ShapeDtypeStruct((PLANE, 2, nz // 2, 16, 128), BF16),
            jax.ShapeDtypeStruct((3 * CHUNK + 8, COLUMNS), I32),
            jax.ShapeDtypeStruct((16, 128), F32),
            jax.ShapeDtypeStruct((nz * PLANE, 128), F32),
        ),
        in_specs=hbm(4),
        out_specs=tuple(vmem(4)),
        scratch_shapes=[
            VM(queries.shape, BF16), VM((SLOTS, 128), I32), VM((SLOTS, 128), I32), pltpu.SMEM((SLOTS,), I32),
            VM((2, nz // 2, 16, 128), BF16), VM((nz, 2, 128), BF16), VM((nz, 2, 128), BF16),
            VM((PLANE, nz, 128), BF16), VM((PLANE, nz, 128), BF16),
        ]
        + [DMA((4,))] + [DMA((nz - 1,))] * 4 + [DMA((6,))] * 2 + [DMA((8,))] * 2 + [DMA((PLANE - 1,))] * 2,
        compiler_params=pltpu.CompilerParams(
            collective_id=0, has_side_effects=True, vmem_limit_bytes=6 << 20
        ),
        name="dispatch",
    )(*map(in_hbm, (queries, block_owner.reshape(SLOTS, 128), block_page.reshape(SLOTS, 128), lengths)))


def return_call(nz, ntp, po, ps, queries, fresh_key_value, o_weight, resid_in, norm_gain):
    width = o_weight.shape[1]
    DMA = pltpu.SemaphoreType.DMA
    block, half = (nz, 16, 128), (2, nz // 2, 16, 128)
    stream, scale = pl.pallas_call(
        functools.partial(return_kernel, nz, ntp),
        out_shape=(
            jax.ShapeDtypeStruct((SLOTS, width), F32),
            jax.ShapeDtypeStruct((SLOTS, width), F32),
        ),
        in_specs=vmem(2) + hbm(4),
        out_specs=tuple(vmem(2)),
        scratch_shapes=[
            VM(queries.shape, BF16), VM(fresh_key_value.shape, BF16), VM(o_weight.shape, BF16),
            VM(resid_in.shape, BF16),
            VM((4,) + block, BF16), VM((4, 8, 128), F32), VM((4,) + half, BF16), VM((4, 8, 128), F32),
            VM((3,) + half, BF16), VM((3, 8, 128), F32),
            VM(block, BF16), VM((nz, 1, 128), F32), VM(block, BF16), VM((nz, 1, 128), F32),
            VM((ntp, SLOTS, width), F32),
        ]
        + [DMA((4,))] + [DMA((4,))] * 4 + [DMA((6,))] * 2 + [DMA((3,))] * 2 + [DMA((nz - 1,))] * 4 + [DMA((ntp - 1,))] * 2,
        compiler_params=pltpu.CompilerParams(
            collective_id=1, has_side_effects=True, vmem_limit_bytes=12 << 20
        ),
        name="give_back",
    )(po, ps, *map(in_hbm, (queries, fresh_key_value, o_weight, resid_in)))
    return stream.astype(BF16), (stream * scale * norm_gain.astype(F32)).astype(BF16)


def body(nz, ntp, queries, fresh_key_value, pool, block_owner, block_page, lengths, o_weight, resid_in, norm_gain):
    qall, lists, items, slots = dispatch_call(nz, pool.shape[0], queries, block_owner, block_page, lengths)
    po, ps = owner_call(nz, qall, lists, items, slots, pool)
    return return_call(nz, ntp, po, ps, queries, fresh_key_value, o_weight, resid_in, norm_gain)


def solution(mesh):
    nz, ntp = mesh.shape["req"] // PLANE, mesh.shape["tp"]
    placed = (
        P("req", "tp"), P("req", "tp"), P("req", None, "tp"), P("req", None), P("req"), P("req"),
        P("tp", None), P("req", None), P(),
    )
    return jax.shard_map(
        functools.partial(body, nz, ntp),
        mesh=mesh,
        in_specs=placed,
        out_specs=(P("req", None), P("req", None)),
        check_vma=False,
    )
```

```python
import functools

import jax
import jax.numpy as jnp
from jax import lax
from jax.experimental import pallas as pl
from jax.experimental.pallas import tpu as pltpu
from jax.sharding import PartitionSpec as P

F32, BF16, I32 = jnp.float32, jnp.bfloat16, jnp.int32
MESH = pl.DeviceIdType.MESH
NEG = -1e30
CAP = 8
CHUNK = 16
UNROLL = 4
COLUMNS = 128
SLOTS = 4
PLANE = 8
VM = pltpu.VMEM


def iota(shape, dim):
    return lax.broadcasted_iota(I32, shape, dim)


def dot_nt(a, b):
    return lax.dot_general(a, b, (((1,), (1,)), ((), ())), preferred_element_type=F32)


def dot_nn(a, b):
    return jnp.dot(a, b, preferred_element_type=F32)


def head_pair_rows(q):
    return jnp.concatenate([q[s : s + 1, 128 * h : 128 * h + 128] for s in range(SLOTS) for h in range(4)], axis=0)


def remote(src, dst, send, recv, peer):
    return pltpu.make_async_remote_copy(
        src_ref=src, dst_ref=dst, send_sem=send, recv_sem=recv, device_id=peer, device_id_type=MESH
    )


def start_all(copies):
    for c in copies:
        c.start()


def wait_all(copies):
    for c in copies:
        c.wait()


def far_first(n):
    return sorted(range(1, n), key=lambda k: -min(k, n - k))


def sort_items(nsrc, npages, meta_b, lists_ref, items_ref, slots_ref):
    meta = meta_b.astype(F32).T
    page, live, slot = meta[0:8], meta[8:16], meta[16:24]
    items_ref[0:8] = live
    items_ref[8:16] = slot
    prow = iota((npages, 128), 0).astype(F32)
    eqs = [
        jnp.where(jnp.logical_and(prow == page[r : r + 1], live[r : r + 1] > 0.0), 1.0, 0.0) for r in range(CAP)
    ]
    upto = jnp.where(iota((128, 256), 0) <= iota((128, 256), 1), 1.0, 0.0).astype(BF16)
    counts = dot_nn(jnp.concatenate(eqs, axis=0).astype(BF16), upto)
    run = jnp.zeros((npages, 128), F32)
    ranks = []
    for r in range(CAP):
        part = counts[npages * r : npages * r + npages]
        ranks.append(run + part[:, 0:128])
        run = run + part[:, 128:256]
    chunks = jnp.floor((run + (CHUNK - 1)) * (1.0 / CHUNK))
    below = jnp.where(iota((npages, npages), 1) < iota((npages, npages), 0), 1.0, 0.0).astype(BF16)
    first = dot_nn(below, chunks.astype(BF16))
    total = (first + chunks)[npages - 1 : npages]

    krow = iota((CHUNK, 128), 0).astype(F32)
    crow = iota((COLUMNS, 128), 0).astype(F32)
    src = iota((1, 128), 1).astype(F32)
    lists = jnp.zeros((5 * CHUNK, COLUMNS), F32)
    for r in range(CAP):
        row = slice(r, r + 1)
        pos = jnp.sum(eqs[r] * (first * CHUNK + ranks[r] - 1.0), axis=0, keepdims=True)
        chunk = jnp.floor(pos * (1.0 / CHUNK))
        here = jnp.logical_and(krow == pos - chunk * CHUNK, live[row] > 0.0)
        pick = [jnp.where(here, v, 0.0) for v in (src, float(r + 1), live[row], slot[row], page[row])]
        col = jnp.where(crow == chunk, 1.0, 0.0)
        lists = lists + dot_nt(jnp.concatenate(pick, axis=0).astype(BF16), col.astype(BF16))
    srcs, nth = lists[0:CHUNK], lists[CHUNK : 2 * CHUNK]
    lists_ref[0:CHUNK] = (srcs * SLOTS + lists[3 * CHUNK : 4 * CHUNK]).astype(I32)
    lists_ref[CHUNK : 2 * CHUNK] = jnp.where(nth > 0.0, srcs * CAP + nth - 1.0, float(nsrc * CAP)).astype(I32)
    lists_ref[2 * CHUNK : 3 * CHUNK] = lists[2 * CHUNK : 3 * CHUNK].astype(I32)
    lists_ref[3 * CHUNK : 3 * CHUNK + 8] = jnp.concatenate(
        [lists[4 * CHUNK : 4 * CHUNK + 1], jnp.tile(total, (1, COLUMNS // 128)), jnp.zeros((6, COLUMNS), F32)], axis=0
    ).astype(I32)
    spread = jnp.where(iota((128, 128), 0) == 2 * CAP + iota((128, 128), 1) // 8 % CAP, 1.0, 0.0).astype(BF16)
    slots_ref[...] = dot_nn(meta_b, spread)


def dispatch_kernel(
    nz, npages, q_hbm, owner_hbm, page_hbm, len_hbm, qall_ref, lists_ref, items_ref, slots_ref,
    q_v, owner_v, page_v, len_s, zq, zsend, zm, ysend, mall,
    in_sem, qs_z, qr_z, ms_z, mr_z, qs_y, qr_y, qs_c, qr_c, ms_y, mr_y,
):
    me = lax.axis_index("req")
    z, yc = me // PLANE, me % PLANE
    y, core = yc // 2, yc % 2
    sib = yc + 1 - 2 * core
    zpeers = [(z + k) % nz for k in far_first(nz)]
    plane = [(yc + k) % PLANE for k in range(1, PLANE)]
    ypeers = [(y + k) % 4 for k in (2, 1, 3)]
    barrier = pltpu.get_barrier_semaphore()
    for p in zpeers:
        pl.semaphore_signal(barrier, inc=1, device_id={"req": p * PLANE + yc}, device_id_type=MESH)
    for p in plane:
        pl.semaphore_signal(barrier, inc=1, device_id={"req": z * PLANE + p}, device_id_type=MESH)
    ins = [
        pltpu.make_async_copy(h, v, in_sem.at[i])
        for i, (h, v) in enumerate([(q_hbm, q_v), (owner_hbm, owner_v), (page_hbm, page_v), (len_hbm, len_s)])
    ]
    start_all(ins)
    ins[0].wait()
    zq[z % 2, z // 2] = head_pair_rows(q_v[...].astype(F32)).astype(BF16)
    pl.semaphore_wait(barrier, nz - 1 + PLANE - 1)
    mine = zq.at[z % 2, z // 2]
    q_z = [
        [
            remote(mine, mine, qs_z.at[k - 1], qr_z.at[k - 1], {"req": (z + k) % nz * PLANE + yc})
            for k in far_first(nz)
            if k % 2 == h
        ]
        for h in range(2)
    ]
    start_all(q_z[0] + q_z[1])

    wait_all(ins[1:])
    rows, lanes = iota((128, 128), 0), iota((128, 128), 1)
    tri = jnp.where(rows <= lanes, 1.0, 0.0).astype(BF16)
    ones = jnp.ones((128, 128), BF16)
    base = jnp.zeros((128, 128), F32)
    table = jnp.zeros((32, 128), F32)
    for s in range(SLOTS):
        live = jnp.clip(len_s[s] - iota((1, 128), 1) * 128, 0, 128)
        hit = jnp.logical_and(rows == owner_v[s : s + 1, :], live > 0)
        hot = jnp.where(hit, 1.0, 0.0).astype(BF16)
        rank = jnp.sum(jnp.where(hit, base + dot_nn(hot, tri) - 1.0, 0.0), axis=0, keepdims=True)
        base = base + dot_nn(hot, ones)
        kind = rows % 32 // CAP
        quarter = rows // 32 == owner_v[s : s + 1, :] % 4
        val = jnp.where(
            kind == 0, page_v[s : s + 1, :].astype(F32),
            jnp.where(kind == 1, live.astype(F32), jnp.where(kind == 2, float(s), 0.0)),
        )
        place = jnp.where(jnp.logical_and(quarter, (rows % CAP).astype(F32) == rank), val, 0.0).astype(BF16)
        four = jnp.logical_and(rows[0:32] == owner_v[s : s + 1, :] // 4, live > 0)
        table = table + dot_nt(jnp.where(four, 1.0, 0.0).astype(BF16), place)
    for i in range(nz):
        zsend[i] = table[2 * i : 2 * i + 2].astype(BF16)
    zm[z] = zsend[z]
    m_z = [
        remote(zsend.at[p], zm.at[z], ms_z.at[i], mr_z.at[i], {"req": p * PLANE + yc}) for i, p in enumerate(zpeers)
    ]
    start_all(m_z)

    q_y, q_c = [], []
    for h in range(2):
        wait_all(q_z[h])
        part = (z + h) % 2
        for i, p in enumerate(ypeers):
            to = {"req": z * PLANE + 2 * p + core}
            q_y.append(remote(zq.at[part], qall_ref.at[yc, part], qs_y.at[3 * h + i], qr_y.at[3 * h + i], to))
        q_c.append(
            remote(zq.at[part], qall_ref.at[yc, part], qs_c.at[6 + h], qr_c.at[6 + h], {"req": z * PLANE + sib})
        )
        start_all(q_y[-3:] + q_c[-1:])
    qall_ref[yc] = zq[...]

    wait_all(m_z)
    got = [zm[i].astype(F32) for i in range(nz)]
    for d in range(PLANE):
        half = jnp.concatenate([g[d // 4 : d // 4 + 1, :] for g in got], axis=0)
        if d % 4:
            half = pltpu.roll(half, 128 - 32 * (d % 4), 1)
        ysend[d] = half.astype(BF16)
    mall[yc] = ysend[yc]
    m_y = [
        remote(ysend.at[p], mall.at[yc], ms_y.at[i], mr_y.at[i], {"req": z * PLANE + p}) for i, p in enumerate(plane)
    ]
    start_all(m_y)
    wait_all(m_y)
    sort_items(nz * PLANE, npages, mall[...].reshape(nz * PLANE, 128), lists_ref, items_ref, slots_ref)
    for h in range(2):
        for i, p in enumerate((2, 3, 1)):
            q_y[3 * h + i].wait()
            here = qall_ref.at[(y + p) % 4 * 2 + core, (z + h) % 2]
            c = remote(here, here, qs_c.at[3 * h + i], qr_c.at[3 * h + i], {"req": z * PLANE + sib})
            c.start()
            q_c.append(c)
    wait_all(q_c)


def owner_kernel(
    nz, qall_ref, lists_ref, items_ref, sg_s, pool_hbm, po_ref, ps_ref,
    pool, qx, o_s, ml_s, wn_s, s0, p0, lst, sems,
):
    nsrc = nz * PLANE
    lst_copy = pltpu.make_async_copy(lists_ref, lst, sems.at[0])
    lst_copy.start()
    pool_copy = pltpu.make_async_copy(pool_hbm, pool, sems.at[1])
    pool_copy.start()
    row8, lane8 = iota((8, 128), 0), iota((8, 128), 1)
    low, left = row8 < 4, lane8 < 64
    live, slot = items_ref[0:8], items_ref[8:16]

    keep = jnp.where(left, 0.125, 0.0)

    @pl.loop(0, 2 * PLANE)
    def _(g):
        for j in range(nz // 2):
            i = g // 2 * nz + 2 * j + g % 2
            q = qall_ref[g // 2, g % 2, j].astype(F32)
            for r in range(CAP):
                o_s[i * CAP + r] = jnp.zeros((8, 128), F32)
            for t in range(2):
                v = q[8 * t : 8 * t + 8]
                vs = pltpu.roll(v, 4, 0)
                qx[i * SLOTS + 2 * t] = jnp.where(low, v, pltpu.roll(vs, 64, 1)) * keep
                qx[i * SLOTS + 2 * t + 1] = jnp.where(low, vs, pltpu.roll(v, 64, 1)) * keep

    lst_copy.wait()
    pool_copy.wait()

    def scores_of(c, out):
        c = jnp.clip(c, 0, COLUMNS - 1)
        q = jnp.concatenate([qx[lst[k, c]] for k in range(CHUNK)], axis=0).astype(BF16)
        out[...] = dot_nt(q, pool[lst[3 * CHUNK, c]])

    def probs_of(c, scores, out):
        c = jnp.clip(c, 0, COLUMNS - 1)
        pair = []
        for k in range(CHUNK):
            sc = jnp.where(lane8 < lst[2 * CHUNK + k, c], scores[8 * k : 8 * k + 8], NEG)
            top = jnp.max(sc, axis=1, keepdims=True)
            pr = jnp.exp(sc - top)
            ml_s[lst[CHUNK + k, c]] = jnp.where(left, top, jnp.sum(pr, axis=1, keepdims=True))
            pair.append(pr)
            if k % 2:
                out[8 * k - 8 : 8 * k + 8] = jnp.concatenate(pair, axis=0).astype(BF16)
                pair = []

    def values_of(c, probs):
        c = jnp.clip(c, 0, COLUMNS - 1)
        out = dot_nn(probs[...], pool[lst[3 * CHUNK, c]])
        for k in range(CHUNK):
            o_s[lst[CHUNK + k, c]] = out[8 * k : 8 * k + 8]

    @pl.loop(0, (lst[3 * CHUNK + 1, 0] + UNROLL - 1) // UNROLL + 2)
    def _(step):
        c = step * UNROLL
        for u in range(UNROLL):
            values_of(c - 2 * UNROLL + u, p0.at[u])
        for u in range(UNROLL):
            probs_of(c - UNROLL + u, s0.at[u], p0.at[u])
        for u in range(UNROLL):
            scores_of(c + u, s0.at[u])

    halves = []
    for h in range(2):

        def gather(g, accs, h=h):
            accs = list(accs)
            for u in range(8):
                i = g * 8 + u
                mask = lane8 % 64 == i
                for r in range(CAP):
                    accs[r] = jnp.where(mask, ml_s[(h * 64 + i) * CAP + r], accs[r])
            return tuple(accs)

        halves.append(lax.fori_loop(0, 8, gather, tuple(jnp.zeros((8, 128), F32) for _ in range(CAP))))
    mine = [[jnp.logical_and(live[r : r + 1] > 0.0, slot[r : r + 1] == float(s)) for s in range(SLOTS)] for r in range(CAP)]
    ms = [jnp.where(left, halves[0][r], pltpu.roll(halves[1][r], 64, 1)) for r in range(CAP)]
    ls = [jnp.where(left, pltpu.roll(halves[0][r], 64, 1), halves[1][r]) for r in range(CAP)]
    tops, dens = [], []
    for s in range(SLOTS):
        top = jnp.full((8, 128), NEG, F32)
        for r in range(CAP):
            top = jnp.maximum(top, jnp.where(mine[r][s], ms[r], NEG))
        tops.append(top)
    es = []
    for r in range(CAP):
        top = ms[r]
        for s in range(SLOTS):
            top = jnp.where(mine[r][s], tops[s], top)
        es.append(jnp.exp(ms[r] - top))
    lses, invs = [], []
    for s in range(SLOTS):
        den = jnp.zeros((8, 128), F32)
        for r in range(CAP):
            den = den + jnp.where(mine[r][s], es[r] * ls[r], 0.0)
        some = den > 0.0
        den = jnp.where(some, den, 1.0)
        invs.append(1.0 / den)
        lses.append(jnp.where(some, tops[s] + jnp.log(den), NEG))
    weights = []
    for r in range(CAP):
        w = jnp.zeros((8, 128), F32)
        for s in range(SLOTS):
            w = jnp.where(mine[r][s], es[r] * invs[s], w)
        weights.append(w)
    wide = jnp.concatenate(weights + weights, axis=0).T
    high = wide.astype(BF16).astype(F32)
    left128 = iota((nsrc, 128), 1) < 64

    def pairs(x):
        return jnp.where(left128, x, pltpu.roll(x, nsrc - 1, 0))

    wn_s[0] = pairs(high)
    wn_s[1] = pairs(wide - high)
    wn_s[2] = pairs(sg_s[...])
    for d in range(PLANE):
        stat = jnp.full((8, 128), NEG, F32)
        for s in range(SLOTS):
            shift = (nz * (s - d)) % 128
            moved = pltpu.roll(lses[s], shift, 1) if shift else lses[s]
            stat = jnp.where(lane8 // nz == s, moved, stat)
        ps_ref[d] = stat

    ar, al = iota((64, 128), 0), iota((64, 128), 1)
    same = jnp.logical_and(ar // 32 == al // 64, ar // 16 % 2 * 4 + ar % 4 == al % 8)
    want = jnp.where(same, ar // 4 % 4, -1).astype(F32)
    left16 = iota((16, 128), 1) < 64

    @pl.loop(0, PLANE, unroll=2)
    def _(d):
        for j in range(nz // 2):
            i = d * nz + 2 * j
            o = jnp.concatenate([o_s[i * CAP + k] for k in range(2 * CAP)], axis=0).astype(BF16)
            hit = want == wn_s[2, pl.ds(i, 1), :]
            pick = [jnp.where(hit, wn_s[k, pl.ds(i, 1), :], 0.0) for k in range(2)]
            res = dot_nn(jnp.concatenate(pick, axis=0).astype(BF16), o)
            res = res[0:64] + res[64:128]
            for a in range(2):
                even, odd = res[32 * a : 32 * a + 16], res[32 * a + 16 : 32 * a + 32]
                po_ref[d, 2 * j + a] = jnp.where(left16, pltpu.roll(even, 64, 1), odd).astype(BF16)


def spread_weights(x, nz):
    low = iota((8, 128), 0) < 4
    xs = pltpu.roll(x, 4, 0)
    yl = jnp.where(low, x, pltpu.roll(xs, 128 - nz, 1))
    yr = jnp.where(low, xs, pltpu.roll(x, 128 - nz, 1))
    return yl, yr


def return_kernel(
    nz, ntp, po_ref, ps_ref, q_hbm, fresh_hbm, w_hbm, resid_hbm, res_out, norm_out,
    q_ref, fresh_ref, wv, resid_ref, rc, rsc, ysnd, ystat, ry, rsy, o1, s1, ro2, rs2, parts,
    in_sem, os_c, or_c, ss_c, sr_c, os_y, or_y, ss_y, sr_y, os_z, or_z, ss_z, sr_z, ts, tr,
):
    me, tp = lax.axis_index("req"), lax.axis_index("tp")
    z, yc = me // PLANE, me % PLANE
    y, core = yc // 2, yc % 2
    sib = yc + 1 - 2 * core
    zpeers = [(z + k) % nz for k in far_first(nz)]
    yorder = [(y + k) % 4 for k in (2, 1, 3, 0)]
    tpeers = [(tp + k) % ntp for k in range(1, ntp)]
    barrier = pltpu.get_barrier_semaphore()
    pl.semaphore_signal(barrier, inc=1, device_id={"req": z * PLANE + sib}, device_id_type=MESH)
    for p in yorder[:3]:
        pl.semaphore_signal(barrier, inc=1, device_id={"req": z * PLANE + 2 * p + core}, device_id_type=MESH)
    for p in zpeers:
        pl.semaphore_signal(barrier, inc=1, device_id={"req": p * PLANE + yc}, device_id_type=MESH)
    for p in tpeers:
        pl.semaphore_signal(barrier, inc=1, device_id={"tp": p}, device_id_type=MESH)
    ins = [
        pltpu.make_async_copy(h, v, in_sem.at[i])
        for i, (h, v) in enumerate(
            [(q_hbm, q_ref), (fresh_hbm, fresh_ref), (w_hbm, wv), (resid_hbm, resid_ref)]
        )
    ]
    start_all(ins)
    pl.semaphore_wait(barrier, nz - 1 + 4 + ntp - 1)

    cores = []
    for i, p in enumerate(yorder):
        to = {"req": z * PLANE + sib}
        theirs = 2 * p + 1 - core
        cores.append(
            [
                remote(ps_ref.at[theirs], rsc.at[i], ss_c.at[i], sr_c.at[i], to),
                remote(po_ref.at[theirs], rc.at[i], os_c.at[i], or_c.at[i], to),
            ]
        )
        start_all(cores[-1])

    row8, lane8 = iota((8, 128), 0), iota((8, 128), 1)
    low, left = row8 < 4, lane8 < 64
    wait_all(ins[:2])
    q16 = head_pair_rows(q_ref[...].astype(F32))
    fresh = fresh_ref[...].astype(F32)
    self_score, self_value = [], []
    for t in range(2):
        kv = jnp.concatenate([fresh[2 * t : 2 * t + 1]] * 4 + [fresh[2 * t + 1 : 2 * t + 2]] * 4, axis=0)
        other = pltpu.roll(kv, 64, 1)
        prod = q16[8 * t : 8 * t + 8] * jnp.where(left, kv, other)
        ls = jnp.sum(jnp.where(left, prod, 0.0), axis=1, keepdims=True)
        rsum = jnp.sum(jnp.where(left, 0.0, prod), axis=1, keepdims=True)
        self_score.append(jnp.where(left, ls, rsum) * 0.125)
        self_value.append(jnp.where(left, other, kv))

    def from_here(x):
        ahead = pltpu.roll(x, (128 - z) % 128, 1)
        behind = pltpu.roll(x, nz - z, 1)
        return jnp.where(lane8 % nz + z < nz, ahead, behind)

    ys = [[], []]
    sides, stats = [], []
    for h in range(2):
        for i, p in enumerate(yorder):
            ours = 2 * p + core
            if h == 0:
                wait_all(cores[i])
                sa, sb = ps_ref[ours], rsc[i]
                top = jnp.maximum(sa, sb)
                ea, eb = jnp.exp(sa - top), jnp.exp(sb - top)
                both = ea + eb
                ystat[i] = from_here(top + jnp.log(both))
                sides.append(spread_weights(from_here(ea / both), nz))
            yl, yr = sides[i]
            for j in range(nz // 2):
                k = 2 * j + h
                halves = []
                zi = (z + k) % nz
                pa, pb = po_ref[ours, zi].astype(F32), rc[i, zi].astype(F32)
                for t in range(2):
                    li = 2 * t * nz + k
                    w = jnp.where(left, yl[:, li : li + 1], yr[:, li : li + 1])
                    b = pb[8 * t : 8 * t + 8]
                    halves.append(b + w * (pa[8 * t : 8 * t + 8] - b))
                ysnd[i, h, j] = jnp.concatenate(halves, axis=0).astype(BF16)
            if i < 3:
                to = {"req": z * PLANE + 2 * p + core}
                if h == 0:
                    ys[h].append(remote(ystat.at[i], rsy.at[i], ss_y.at[i], sr_y.at[i], to))
                    ys[h][-1].start()
                ys[h].append(
                    remote(ysnd.at[i, h], ry.at[i, h], os_y.at[3 * h + i], or_y.at[3 * h + i], to)
                )
                ys[h][-1].start()

    zs = []
    for h in range(2):
        wait_all(ys[h])
        if h == 0:
            stats = [rsy[p] for p in range(3)] + [ystat[3]]
            top = stats[0]
            for p in range(1, 4):
                top = jnp.maximum(top, stats[p])
            ws = [jnp.exp(s - top) for s in stats]
            wsum = ws[0]
            for p in range(1, 4):
                wsum = wsum + ws[p]
            lse = top + jnp.log(wsum)
            sides = [spread_weights(w / wsum, nz) for w in ws]
            by_slot = [pltpu.roll(lse, (128 - nz * s) % 128, 1) if s else lse for s in range(SLOTS)]
            rows = jnp.concatenate(by_slot + [jnp.zeros((96, 128), F32)], axis=0).T
            for k in range(nz):
                s1[k] = rows[k : k + 1]
        for j in range(nz // 2):
            k = 2 * j + h
            pieces = [ry[p, h, j].astype(F32) for p in range(3)] + [ysnd[3, h, j].astype(F32)]
            halves = []
            for t in range(2):
                li = 2 * t * nz + k
                total = jnp.zeros((8, 128), F32)
                for p in range(4):
                    yl, yr = sides[p]
                    w = jnp.where(left, yl[:, li : li + 1], yr[:, li : li + 1])
                    total = total + w * pieces[p][8 * t : 8 * t + 8]
                halves.append(total)
            o1[k] = jnp.concatenate(halves, axis=0).astype(BF16)
        for k in far_first(nz):
            if k % 2 == h:
                to = {"req": (z + k) % nz * PLANE + yc}
                zs.append(remote(s1.at[k], rs2.at[z], ss_z.at[k - 1], sr_z.at[k - 1], to))
                zs.append(remote(o1.at[k], ro2.at[z], os_z.at[k - 1], or_z.at[k - 1], to))
                start_all(zs[-2:])
    ro2[z] = o1[0]
    rs2[z] = s1[0]
    wait_all(zs)

    st = jnp.concatenate([rs2[zi] for zi in range(nz)], axis=0)
    top = jnp.max(st, axis=0, keepdims=True)
    cols = jnp.concatenate(
        [jnp.exp(st - top), jnp.broadcast_to(top, (8, 128)), jnp.zeros((120 - nz, 128), F32)], axis=0
    ).T
    att = []
    for t in range(2):
        x0, x1 = cols[16 * t : 16 * t + 8], cols[16 * t + 8 : 16 * t + 16]
        yl = jnp.where(low, x0, pltpu.roll(x1, 4, 0))
        yr = jnp.where(low, pltpu.roll(x0, 4, 0), x1)
        num = jnp.zeros((8, 128), F32)
        den = jnp.zeros((8, 128), F32)
        for zi in range(nz):
            w = jnp.where(left, yl[:, zi : zi + 1], yr[:, zi : zi + 1])
            num = num + w * ro2[zi, 8 * t : 8 * t + 8].astype(F32)
            den = den + w
        topm = jnp.where(left, yl[:, nz : nz + 1], yr[:, nz : nz + 1])
        best = jnp.maximum(topm, self_score[t])
        a, b = jnp.exp(topm - best), jnp.exp(self_score[t] - best)
        att.append((a * num + b * self_value[t]) / (a * den + b))
    att = jnp.concatenate(att, axis=0)
    r16 = iota((16, 128), 0)
    wide = jnp.concatenate([jnp.where(r16 % 4 == h, att, 0.0) for h in range(4)], axis=1).astype(BF16)
    sel = jnp.where(iota((16, 16), 1) // 4 == iota((16, 16), 0), 1.0, 0.0).astype(BF16)
    lhs = dot_nn(sel, wide).astype(BF16)
    wait_all(ins[2:])
    parts[tp] = dot_nn(lhs, wv[...])[0:SLOTS]
    copies = []
    for i, p in enumerate(tpeers):
        copies.append(remote(parts.at[tp], parts.at[tp], ts.at[i], tr.at[i], {"tp": p}))
    for c in copies:
        c.start()
    for c in copies:
        c.wait()
    stream = parts[0]
    for p in range(1, ntp):
        stream = stream + parts[p]
    stream = resid_ref[...].astype(F32) + stream
    mean = jnp.mean(stream * stream, axis=1, keepdims=True)
    res_out[...] = stream
    norm_out[...] = jnp.broadcast_to(lax.rsqrt(mean + 1e-5), stream.shape)


def vmem(n):
    return [pl.BlockSpec(memory_space=pltpu.VMEM)] * n


def in_hbm(x):
    return pltpu.with_memory_space_constraint(x, pltpu.HBM)


def hbm(n):
    return [pl.BlockSpec(memory_space=pltpu.HBM)] * n


def owner_call(nz, qall, lists, items, slots, pool):
    nsrc = nz * PLANE
    return pl.pallas_call(
        functools.partial(owner_kernel, nz),
        out_shape=(
            jax.ShapeDtypeStruct((PLANE, nz, 16, 128), BF16),
            jax.ShapeDtypeStruct((PLANE, 8, 128), F32),
        ),
        in_specs=vmem(4) + hbm(1),
        out_specs=tuple(vmem(2)),
        scratch_shapes=[
            VM(pool.shape, BF16),
            VM((nsrc * SLOTS, 8, 128), F32),
            VM((nsrc * CAP + 1, 8, 128), F32), VM((nsrc * CAP + 1, 8, 128), F32),
            VM((3, nsrc, 128), F32),
            VM((UNROLL, 8 * CHUNK, 128), F32), VM((UNROLL, 8 * CHUNK, 128), BF16),
            pltpu.SMEM((3 * CHUNK + 8, COLUMNS), I32),
            pltpu.SemaphoreType.DMA((2,)),
        ],
        compiler_params=pltpu.CompilerParams(vmem_limit_bytes=24 << 20),
        name="owner",
    )(qall, lists, items, slots, in_hbm(pool))


def dispatch_call(nz, npages, queries, block_owner, block_page, lengths):
    DMA = pltpu.SemaphoreType.DMA
    return pl.pallas_call(
        functools.partial(dispatch_kernel, nz, npages),
        out_shape=(
            jax.ShapeDtypeStruct((PLANE, 2, nz // 2, 16, 128), BF16),
            jax.ShapeDtypeStruct((3 * CHUNK + 8, COLUMNS), I32),
            jax.ShapeDtypeStruct((16, 128), F32),
            jax.ShapeDtypeStruct((nz * PLANE, 128), F32),
        ),
        in_specs=hbm(4),
        out_specs=tuple(vmem(4)),
        scratch_shapes=[
            VM(queries.shape, BF16), VM((SLOTS, 128), I32), VM((SLOTS, 128), I32), pltpu.SMEM((SLOTS,), I32),
            VM((2, nz // 2, 16, 128), BF16), VM((nz, 2, 128), BF16), VM((nz, 2, 128), BF16),
            VM((PLANE, nz, 128), BF16), VM((PLANE, nz, 128), BF16),
        ]
        + [DMA((4,))] + [DMA((nz - 1,))] * 4 + [DMA((6,))] * 2 + [DMA((8,))] * 2 + [DMA((PLANE - 1,))] * 2,
        compiler_params=pltpu.CompilerParams(
            collective_id=0, has_side_effects=True, vmem_limit_bytes=6 << 20
        ),
        name="dispatch",
    )(*map(in_hbm, (queries, block_owner.reshape(SLOTS, 128), block_page.reshape(SLOTS, 128), lengths)))


def return_call(nz, ntp, po, ps, queries, fresh_key_value, o_weight, resid_in, norm_gain):
    width = o_weight.shape[1]
    DMA = pltpu.SemaphoreType.DMA
    block, half = (nz, 16, 128), (2, nz // 2, 16, 128)
    stream, scale = pl.pallas_call(
        functools.partial(return_kernel, nz, ntp),
        out_shape=(
            jax.ShapeDtypeStruct((SLOTS, width), F32),
            jax.ShapeDtypeStruct((SLOTS, width), F32),
        ),
        in_specs=vmem(2) + hbm(4),
        out_specs=tuple(vmem(2)),
        scratch_shapes=[
            VM(queries.shape, BF16), VM(fresh_key_value.shape, BF16), VM(o_weight.shape, BF16),
            VM(resid_in.shape, BF16),
            VM((4,) + block, BF16), VM((4, 8, 128), F32), VM((4,) + half, BF16), VM((4, 8, 128), F32),
            VM((3,) + half, BF16), VM((3, 8, 128), F32),
            VM(block, BF16), VM((nz, 1, 128), F32), VM(block, BF16), VM((nz, 1, 128), F32),
            VM((ntp, SLOTS, width), F32),
        ]
        + [DMA((4,))] + [DMA((4,))] * 4 + [DMA((6,))] * 2 + [DMA((3,))] * 2 + [DMA((nz - 1,))] * 4 + [DMA((ntp - 1,))] * 2,
        compiler_params=pltpu.CompilerParams(
            collective_id=1, has_side_effects=True, vmem_limit_bytes=12 << 20
        ),
        name="give_back",
    )(po, ps, *map(in_hbm, (queries, fresh_key_value, o_weight, resid_in)))
    return stream.astype(BF16), (stream * scale * norm_gain.astype(F32)).astype(BF16)


def body(nz, ntp, queries, fresh_key_value, pool, block_owner, block_page, lengths, o_weight, resid_in, norm_gain):
    qall, lists, items, slots = dispatch_call(nz, pool.shape[0], queries, block_owner, block_page, lengths)
    po, ps = owner_call(nz, qall, lists, items, slots, pool)
    return return_call(nz, ntp, po, ps, queries, fresh_key_value, o_weight, resid_in, norm_gain)


def solution(mesh):
    nz, ntp = mesh.shape["req"] // PLANE, mesh.shape["tp"]
    placed = (
        P("req", "tp"), P("req", "tp"), P("req", None, "tp"), P("req", None), P("req"), P("req"),
        P("tp", None), P("req", None), P(),
    )
    return jax.shard_map(
        functools.partial(body, nz, ntp),
        mesh=mesh,
        in_specs=placed,
        out_specs=(P("req", None), P("req", None)),
        check_vma=False,
    )
```
